32 devices in a mesh: dp: 8 (over z, x), ctx: 4 (over y, core).
Axes of the slice: x: 2, y: 2, z: 4, core: 2. Of those that a mesh axis runs over, the one named last changes fastest.
Arguments:
- inputs: bfloat16 [8, 512, 5376], P('dp', 'ctx'), may hold values from -6 to 6
- q_proj: bfloat16 [8, 512, 2048], P('dp', 'ctx'), may hold values from -260 to 260
- k_proj: bfloat16 [8, 512, 1024], P('dp', 'ctx'), may hold values from -260 to 260
- v_proj: bfloat16 [8, 512, 1024], P('dp', 'ctx'), may hold values from -6 to 6
- d_attn: bfloat16 [8, 512, 2048], P('dp', 'ctx'), may hold values from -6 to 6
- positions: int32 [8, 512], P('dp', 'ctx'), may hold values from 0 to 511, as said below
- windows: int32 [8], P('dp'), may hold values from 512 to 1024
- q_gain: float32 [128], replicated, may hold values from 0.7 to 5.5
- k_gain: float32 [128], replicated, may hold values from 0.7 to 5.5
- weight: bfloat16 [5376, 4096], P('dp'), may hold values from -0.078125 to 0.078125
Outputs:
- d_inputs: bfloat16 [8, 512, 5376], P('dp', 'ctx')
- d_weight_t: float32 [4096, 5376], P('ctx', 'dp')
- d_q_gain: float32 [128], replicated
- d_k_gain: float32 [128], replicated
The draws below stay inside these ranges and needn't reach their ends.
Inputs may be any that keep to these rules, and one draw needn't show every extreme that they name: `positions`: within each sequence a position counts the tokens since its document began: it grows by one from token to token and falls to 0 where a document begins; the first token of a sequence has position 0. Some sequence holds a single document.
All inputs are finite; a program needn't handle non-finite values.
Results may differ from the reference program's by a relative error of at most 0.029.
Values may be sent and summed in bfloat16 or wider, within the bound.
A program may use at most 128 MiB of HBM per device.

```python
import math
import jax
import jax.numpy as jnp
from jax import lax

D = 5376
QUERY_HEADS = 16
KEY_HEADS = 8
HEAD_SIZE = 128
WIN = 1024
TOK_DEV = 128
QUERY_GROUP = 2
QW = 2048
KW = 1024
PW = 4096
REACH = 8
SEQUENCE_LENGTH = 512
BATCH_COUNT = 8
N_CTX = 4


def draw_heads(key):
    flow_count = jax.random.split(jax.random.fold_in(key, 7), 5)
    column_scale = jnp.exp(jax.random.uniform(flow_count[0], (HEAD_SIZE,), jnp.float32, math.log(0.4), math.log(4.0)))
    query_scale = jnp.exp(jax.random.uniform(flow_count[1], (BATCH_COUNT, SEQUENCE_LENGTH, QUERY_HEADS, 1), jnp.float32, math.log(0.5), math.log(5.0)))
    key_norm_scale = jnp.exp(jax.random.uniform(flow_count[2], (BATCH_COUNT, SEQUENCE_LENGTH, KEY_HEADS, 1), jnp.float32, math.log(0.5), math.log(5.0)))
    query_rows = jax.random.truncated_normal(flow_count[3], -6.0, 6.0, (BATCH_COUNT, SEQUENCE_LENGTH, QUERY_HEADS, HEAD_SIZE), jnp.float32)
    key_unnormed = jax.random.truncated_normal(flow_count[4], -6.0, 6.0, (BATCH_COUNT, SEQUENCE_LENGTH, KEY_HEADS, HEAD_SIZE), jnp.float32)
    return (query_rows * query_scale * column_scale, key_unnormed * key_norm_scale * column_scale)


def draw_q_proj(key, part):
    query_rows, key_output = draw_heads(key)
    return query_rows.reshape(BATCH_COUNT, SEQUENCE_LENGTH, QUERY_HEADS * HEAD_SIZE).astype(jnp.bfloat16)


def draw_k_proj(key, part):
    query_rows, key_output = draw_heads(key)
    return key_output.reshape(BATCH_COUNT, SEQUENCE_LENGTH, KEY_HEADS * HEAD_SIZE).astype(jnp.bfloat16)


def draw_positions(key, part):
    marks = jax.random.randint(jax.random.fold_in(key, 3), (BATCH_COUNT, 2), 1, 3 * SEQUENCE_LENGTH)
    single = jax.random.randint(jax.random.fold_in(key, 5), (), 0, BATCH_COUNT)
    marks = jnp.where((jnp.arange(BATCH_COUNT) == single)[:, None], SEQUENCE_LENGTH, marks)
    index = jnp.arange(SEQUENCE_LENGTH, dtype=jnp.int32)[None, :, None]
    begun = jnp.where(marks[:, None, :] <= index, marks[:, None, :], 0)
    return (index[:, :, 0] - jnp.max(begun, axis=-1)).astype(jnp.int32)


def draw_windows(key, part):
    flow_count = jax.random.split(jax.random.fold_in(key, 4), 3)
    drawn = jax.random.randint(flow_count[0], (BATCH_COUNT,), WIN // 2, WIN + 1)
    widest = jax.random.randint(flow_count[1], (), 0, BATCH_COUNT)
    narrowest = (widest + 1 + jax.random.randint(flow_count[2], (), 0, BATCH_COUNT - 1)) % BATCH_COUNT
    slots = jnp.arange(BATCH_COUNT)
    result = jnp.where(slots == widest, WIN, jnp.where(slots == narrowest, WIN // 2, drawn))
    return result.astype(jnp.int32)


def draw_q_gain(key, part):
    return jax.random.uniform(jax.random.fold_in(key, 11), (HEAD_SIZE,), jnp.float32, 0.7, 1.3)


def draw_k_gain(key, part):
    return jax.random.uniform(jax.random.fold_in(key, 12), (HEAD_SIZE,), jnp.float32, 0.7, 1.3)


def strengthened(values, rng, source, target, blocks, factor):
    owner, partner = [(jnp.arange(values.shape[position]) // (values.shape[position] // blocks)).reshape([-1 if axis == position else 1 for axis in range(values.ndim)]) for position in (source, target)]
    chosen = jax.random.permutation(rng, blocks)[partner]
    strong = (owner == chosen) | (owner == (partner + blocks // 2) % blocks)
    return jnp.where(strong, factor * values, values)


def levels(key, extent, pieces, low, high):
    loudness = 1.0
    for axis_at, parts in pieces:
        draws = jax.random.uniform(jax.random.fold_in(jax.random.fold_in(key, 6), axis_at), (parts,), jnp.float32, low / len(pieces), high / len(pieces))
        loudness = loudness * jnp.repeat(jnp.exp(draws), extent[axis_at] // parts).reshape((-1,) + (1,) * (len(extent) - 1 - axis_at))
    return loudness


def centred(rng, dims, spread, reach, cuts=(), kind=jnp.bfloat16):
    values = jax.random.normal(rng, dims, jnp.float32) * spread
    if len(cuts) > 0:
        values = levels(rng, dims, cuts, -0.22, 0.18) * values
    return jnp.clip(values, min=-reach, max=reach).astype(kind)


def bell_draw_with(key, extent, scale, bound, pieces, heavy, kind=jnp.bfloat16):
    entries = scale * jax.random.normal(key, extent, jnp.float32)
    if pieces:
        entries = entries * levels(key, extent, pieces, -0.22, 0.18)
    return jnp.clip(strengthened(entries, jax.random.fold_in(key, 3), *heavy), -bound, bound).astype(kind)


def setup_inputs(seed: int = 0) -> dict:
    seeds = jax.random.split(jax.random.key(seed), 11)
    return {
        "inputs": centred(seeds[0], (BATCH_COUNT, SEQUENCE_LENGTH, D), 1.0, 6.0, ((0, 8), (1, 4))),
        "q_proj": draw_q_proj(jax.random.fold_in(seeds[10], 71), 0),
        "k_proj": draw_k_proj(jax.random.fold_in(seeds[10], 71), 0),
        "v_proj": centred(seeds[3], (BATCH_COUNT, SEQUENCE_LENGTH, KW), 1.0, 6.0, ((0, 8), (1, 4))),
        "d_attn": bell_draw_with(seeds[4], (BATCH_COUNT, SEQUENCE_LENGTH, QW), 0.5, 6.0, ((0, 8), (1, 4)), (1, 2, 4, 2.0)),
        "positions": draw_positions(jax.random.fold_in(seeds[10], 71), 0),
        "windows": draw_windows(jax.random.fold_in(seeds[10], 71), 0),
        "q_gain": draw_q_gain(jax.random.fold_in(seeds[10], 71), 0),
        "k_gain": draw_k_gain(jax.random.fold_in(seeds[10], 71), 0),
        "weight": centred(seeds[9], (D, PW), D ** -0.5, 0.078125, ((0, 8),)),
    }


score_scale = 168.0 ** (-0.5)
rope_base = 10000.0
norm_eps = 1e-06

def rotated_unit(projected_rows, gain_vector, token_pos, head_count):
    head_width = gain_vector.shape[0]
    rows_heads = projected_rows.reshape(projected_rows.shape[0], head_count, head_width)
    inverse = lax.rsqrt(lax.optimization_barrier(jnp.mean(rows_heads * rows_heads, axis=-1, keepdims=True)) + norm_eps)
    normed = rows_heads * inverse * gain_vector
    half_width = head_width // 2
    frequency = jnp.exp(jnp.arange(half_width, dtype=jnp.float32) * (-2.0 * math.log(rope_base) / head_width))
    angles = token_pos.astype(jnp.float32)[:, None] * frequency[None, :]
    cosine_table = jnp.cos(angles)[:, None, :]
    sine_table = jnp.sin(angles)[:, None, :]
    first_half = normed[..., :half_width]
    second_half = normed[..., half_width:]
    return jnp.concatenate([first_half * cosine_table - second_half * sine_table, second_half * cosine_table + first_half * sine_table], axis=-1)

def rounded_outside(values, keep_mask):
    low = lax.optimization_barrier(values.astype(jnp.bfloat16)).astype(jnp.float32)
    return jnp.where(keep_mask, values, low)

def sequence_grads(q_seq, k_seq, value_sequence, sequence_gradient, position_sequence, window, q_gain, k_gain):

    def query_side(projected_rows, gain_vector):
        return rotated_unit(projected_rows, gain_vector, position_sequence, QUERY_HEADS)

    def key_side(projected_rows, gain_vector):
        return rotated_unit(projected_rows, gain_vector, position_sequence, KEY_HEADS)
    q_full, query_back = jax.vjp(query_side, q_seq.astype(jnp.float32), q_gain)
    k_full, key_back = jax.vjp(key_side, k_seq.astype(jnp.float32), k_gain)
    query_rotated = q_full.astype(jnp.bfloat16)
    key_rotated = k_full.astype(jnp.bfloat16)
    value_heads = value_sequence.reshape(SEQUENCE_LENGTH, KEY_HEADS, HEAD_SIZE)
    head_gradient = sequence_gradient.reshape(SEQUENCE_LENGTH, KEY_HEADS, QUERY_GROUP, HEAD_SIZE)
    query_grouped = query_rotated.reshape(SEQUENCE_LENGTH, KEY_HEADS, QUERY_GROUP, HEAD_SIZE)
    pad_amount = REACH * TOK_DEV
    span_rows = (REACH + 1) * TOK_DEV
    key_padded = jnp.concatenate([jnp.zeros((pad_amount, KEY_HEADS, HEAD_SIZE), jnp.bfloat16), key_rotated], axis=0)
    value_padded = jnp.concatenate([jnp.zeros((pad_amount, KEY_HEADS, HEAD_SIZE), jnp.bfloat16), value_heads], axis=0)
    query_off = jnp.arange(TOK_DEV, dtype=jnp.int32)
    key_off = jnp.arange(span_rows, dtype=jnp.int32)
    own_rows = (key_off >= pad_amount)[:, None, None]

    def block_step(carry, index):
        dk_acc, dv_acc = carry
        start_row = (index * TOK_DEV).astype(jnp.int32)
        q_block = lax.dynamic_slice_in_dim(query_grouped, start_row, TOK_DEV, 0).astype(jnp.float32)
        d_block = lax.dynamic_slice_in_dim(head_gradient, start_row, TOK_DEV, 0).astype(jnp.float32)
        pos_block = lax.dynamic_slice_in_dim(position_sequence, start_row, TOK_DEV, 0)
        k_window = lax.dynamic_slice_in_dim(key_padded, start_row, span_rows, 0).astype(jnp.float32)
        v_window = lax.dynamic_slice_in_dim(value_padded, start_row, span_rows, 0).astype(jnp.float32)
        distance = query_off[:, None] + pad_amount - key_off[None, :]
        allowed = (distance >= 0) & (distance < window) & (distance <= pos_block[:, None])
        scores = jnp.einsum('ahgd,chd->hgac', q_block, k_window) * score_scale
        scores = jnp.where(allowed, scores, -jnp.inf)
        row_max = lax.optimization_barrier(jnp.max(scores, axis=-1, keepdims=True))
        exponent = jnp.exp(scores - row_max)
        probs = exponent / lax.optimization_barrier(jnp.sum(exponent, axis=-1, keepdims=True))
        dprobs = jnp.einsum('ahgd,chd->hgac', d_block, v_window)
        delta = lax.optimization_barrier(jnp.sum(probs * dprobs, axis=-1, keepdims=True))
        dscores = (probs * (dprobs - delta)).astype(jnp.bfloat16).astype(jnp.float32)
        probs_low = probs.astype(jnp.bfloat16).astype(jnp.float32)
        dq_block = jnp.einsum('hgac,chd->ahgd', dscores, k_window) * score_scale
        dk_window = jnp.einsum('hgac,ahgd->chd', dscores, q_block) * score_scale
        dv_window = jnp.einsum('hgac,ahgd->chd', probs_low, d_block)
        dk_window = rounded_outside(dk_window, own_rows)
        dv_window = rounded_outside(dv_window, own_rows)
        dk_acc = lax.dynamic_update_slice_in_dim(dk_acc, lax.dynamic_slice_in_dim(dk_acc, start_row, span_rows, 0) + dk_window, start_row, 0)
        dv_acc = lax.dynamic_update_slice_in_dim(dv_acc, lax.dynamic_slice_in_dim(dv_acc, start_row, span_rows, 0) + dv_window, start_row, 0)
        return ((dk_acc, dv_acc), dq_block.reshape(TOK_DEV, QUERY_HEADS, HEAD_SIZE))
    blank_block = jnp.zeros((pad_amount + SEQUENCE_LENGTH, KEY_HEADS, HEAD_SIZE), jnp.float32)
    (dk_acc, dv_acc), dq_blocks = lax.scan(block_step, (blank_block, blank_block), jnp.arange(N_CTX, dtype=jnp.int32))
    dq_rot = dq_blocks.reshape(SEQUENCE_LENGTH, QUERY_HEADS, HEAD_SIZE)
    dk_rot = dk_acc[pad_amount:]
    dv_proj = dv_acc[pad_amount:].reshape(SEQUENCE_LENGTH, KW)
    dq_proj, dq_gain = query_back(dq_rot)
    dk_proj, dk_gain = key_back(dk_rot)
    d_proj = jnp.concatenate([dq_proj, dk_proj, dv_proj], axis=-1).astype(jnp.bfloat16)
    return (d_proj, dq_gain, dk_gain)

def reference(inputs, q_proj, k_proj, v_proj, d_attn, positions, windows, q_gain, k_gain, weight):

    def one_sequence(members):
        q_seq, k_seq, value_sequence, sequence_gradient, position_sequence, window = members
        return sequence_grads(q_seq, k_seq, value_sequence, sequence_gradient, position_sequence, window, q_gain, k_gain)
    d_proj, dq_gain, dk_gain = lax.map(one_sequence, (q_proj, k_proj, v_proj, d_attn, positions, windows))

    def input_grad(rows_seq):
        return jnp.dot(rows_seq, weight.T, preferred_element_type=jnp.float32).astype(jnp.bfloat16)
    d_inputs = lax.map(input_grad, d_proj)

    def weight_block(total, index):
        start_row = (index * TOK_DEV).astype(jnp.int32)
        grads_rows = lax.dynamic_slice_in_dim(d_proj, start_row, TOK_DEV, 1).reshape(BATCH_COUNT * TOK_DEV, PW)
        input_rows = lax.dynamic_slice_in_dim(inputs, start_row, TOK_DEV, 1).reshape(BATCH_COUNT * TOK_DEV, D)
        term = jnp.dot(grads_rows.T, input_rows, preferred_element_type=jnp.float32)
        return (total + lax.optimization_barrier(term.astype(jnp.bfloat16)).astype(jnp.float32), None)
    d_weight_t, _ = lax.scan(weight_block, jnp.zeros((PW, D), jnp.float32), jnp.arange(N_CTX, dtype=jnp.int32))
    return (d_inputs, d_weight_t, lax.optimization_barrier(jnp.sum(dq_gain, axis=0)), lax.optimization_barrier(jnp.sum(dk_gain, axis=0)))
```

```python
import math

import jax
import jax.numpy as jnp
import numpy as np
from jax import lax
from jax.experimental import pallas as pl
from jax.experimental.pallas import tpu as pltpu
from jax.sharding import PartitionSpec as P

MESH = pl.DeviceIdType.MESH

REACH = 8


score_scale = 168.0 ** (-0.5)
rope_base = 10000.0
norm_eps = 1e-06


def from_behind(value, axis, steps):
    count = lax.axis_size(axis)
    initial, last = (max(0, -steps), min(count, count - steps))
    return lax.ppermute(value, axis, [(source, source + steps) for source in range(initial, last)])


def swapped(value, axis, bit):
    count = lax.axis_size(axis)
    return lax.ppermute(value, axis, [(source, source ^ bit) for source in range(count)])


def flipped(index, bits):
    bit = 1
    while bit <= bits:
        if bits & bit:
            index = index + bit - 2 * bit * (lax.rem(index // bit, 2))
        bit *= 2
    return index


def remote(source, target, send_sem, recv_sem, axis, index):
    return pltpu.make_async_remote_copy(
        src_ref=source,
        dst_ref=target,
        send_sem=send_sem,
        recv_sem=recv_sem,
        device_id={axis: index},
        device_id_type=MESH,
    )


def exchange_kernel(n_dp, n_ctx, reach, parts_ref, pair_ref, cols_ref, far_ref, own_sem, send_a, recv_a, send_b, recv_b):
    row = lax.axis_index("dp")
    col = lax.axis_index("ctx")
    barrier = pltpu.get_barrier_semaphore()
    for step in range(1, n_dp):
        pl.semaphore_signal(barrier, 1, device_id={"dp": lax.rem(row + step, n_dp)}, device_id_type=MESH)
    for step in range(1, n_ctx):
        pl.semaphore_signal(barrier, 1, device_id={"ctx": lax.rem(col + step, n_ctx)}, device_id_type=MESH)
    pl.semaphore_wait(barrier, n_dp + n_ctx - 2)
    for step in range(1, reach + 1):
        copy = remote(pair_ref, far_ref.at[step - 1], send_b.at[step], recv_b.at[step], "ctx", lax.rem(col + step, n_ctx))
        pl.when(col + step < n_ctx)(copy.start)
    own = pltpu.make_async_copy(parts_ref.at[row], cols_ref.at[row], own_sem)
    own.start()
    sends = []
    for step in range(1, n_dp):
        peer = lax.rem(row + step, n_dp)
        copy = remote(parts_ref.at[peer], cols_ref.at[row], send_a.at[step], recv_a.at[step], "dp", peer)
        copy.start()
        sends.append(copy)
    own.wait()
    for step in range(1, n_dp):
        source = lax.rem(row + n_dp - step, n_dp)
        remote(parts_ref.at[source], cols_ref.at[source], send_a.at[step], recv_a.at[step], "dp", source).wait_recv()
        sends[step - 1].wait_send()
    for step in range(1, reach + 1):
        copy = remote(pair_ref, far_ref.at[step - 1], send_b.at[step], recv_b.at[step], "ctx", lax.rem(col + step, n_ctx))
        pl.when(col + step < n_ctx)(copy.wait_send)
        pl.when(col >= step)(copy.wait_recv)


def exchanged(parts, pair, reach):
    n_dp, n_ctx = lax.axis_size("dp"), lax.axis_size("ctx")
    anywhere = pl.BlockSpec(memory_space=pl.ANY)
    dma = pltpu.SemaphoreType.DMA
    return pl.pallas_call(
        lambda *refs: exchange_kernel(n_dp, n_ctx, reach, *refs),
        out_shape=(
            jax.ShapeDtypeStruct(parts.shape, parts.dtype),
            jax.ShapeDtypeStruct((reach,) + pair.shape, pair.dtype),
        ),
        in_specs=[anywhere, anywhere],
        out_specs=(anywhere, anywhere),
        scratch_shapes=[dma, dma((n_dp,)), dma((n_dp,)), dma((reach + 1,)), dma((reach + 1,))],
        compiler_params=pltpu.CompilerParams(collective_id=1, has_side_effects=True),
        name="exchange",
    )(parts, pair)


def project_kernel(
    n_dp, n_ctx, d_ref, w_ref, cols_ref, gain_ref, back_ref, sum_ref, gain_out,
    blocks, acc, outbox, terms, got, gain_rows, gain_sent, gain_got,
    own_sem, send_g, recv_g, send_o, recv_o, send_w, recv_w, send_r, recv_r, send_c, recv_c,
):
    row = lax.axis_index("dp")
    col = lax.axis_index("ctx")
    line = n_dp // 2
    place = row // 2
    lane = lax.rem(row, 2)
    twin = 1 - 2 * lane
    width = w_ref.shape[1]
    bits = [1 << k for k in range(n_ctx.bit_length() - 1)]
    barrier = pltpu.get_barrier_semaphore()
    for step in range(1, n_dp):
        pl.semaphore_signal(barrier, 1, device_id={"dp": lax.rem(row + step, n_dp)}, device_id_type=MESH)
    for bit in bits:
        pl.semaphore_signal(barrier, 1, device_id={"ctx": flipped(col, bit)}, device_id_type=MESH)
    pl.semaphore_wait(barrier, n_dp - 1 + len(bits))

    def relay(block, way, target):
        return remote(blocks.at[block], blocks.at[block], send_g.at[way, block], recv_g.at[block], "dp", target)

    def arrived(block):
        relay(block, 0, lax.rem(row + 1, n_dp)).wait_recv()

    def back(block, target):
        return remote(outbox.at[block], back_ref.at[row], send_o.at[block], recv_o.at[row], "dp", target)

    def product(block):
        acc[...] = jnp.zeros_like(acc)
        depth = 2048

        @pl.loop(0, width // depth)
        def _(k):
            span = pl.ds(pl.multiple_of(k * depth, depth), depth)
            acc[...] += lax.dot_general(
                blocks[block, :, span], w_ref[:, span], (((1,), (1,)), ((), ())),
                preferred_element_type=jnp.float32,
            )

        outbox[block] = acc[...].astype(outbox.dtype)

    def answer(block):
        product(block)
        back(block, block).start()

    blocks[row] = d_ref[...]
    pl.when(place < line - 1)(lambda: relay(row, 0, row + 2).start())
    pl.when(place > 0)(lambda: relay(row, 1, row - 2).start())
    relay(row, 2, row + twin).start()

    def gain_to(peer):
        return remote(gain_ref, gain_rows.at[row], send_r.at[peer], recv_r.at[row], "dp", peer)

    gain_rows[row] = gain_ref[...]
    for step in range(1, n_dp):
        gain_to(lax.rem(row + step, n_dp)).start()
    product(row)
    own = pltpu.make_async_copy(outbox.at[row], back_ref.at[row], own_sem)
    own.start()

    @pl.loop(1, line + 1)
    def _(step):
        @pl.when(place >= step)
        def _():
            block = row - 2 * step
            arrived(block)
            pl.when(place < line - 1)(lambda: relay(block, 0, row + 2).start())
            relay(block, 2, row + twin).start()

        @pl.when(place + step < line)
        def _():
            block = row + 2 * step
            arrived(block)
            pl.when(place > 0)(lambda: relay(block, 1, row - 2).start())
            relay(block, 2, row + twin).start()

        pl.when(place >= step)(lambda: answer(row - 2 * step))
        pl.when(place + step < line)(lambda: answer(row + 2 * step))

        @pl.when(place >= step - 1)
        def _():
            block = row + twin - 2 * (step - 1)
            arrived(block)
            answer(block)

        @pl.when((step > 1) & (place + step - 1 < line))
        def _():
            block = row + twin + 2 * (step - 1)
            arrived(block)
            answer(block)

    tokens = n_dp * blocks.shape[1]
    rows = width // n_ctx
    tile = min(512, rows)

    def fill(slot):
        start = flipped(col, slot) * rows

        @pl.loop(0, rows // tile)
        def _(k):
            span = pl.ds(pl.multiple_of(start + k * tile, tile), tile)
            left = blocks[:, :, span].reshape(tokens, tile)
            right = cols_ref[...].reshape(tokens, cols_ref.shape[2])
            term = lax.dot_general(
                left, right, (((0,), (0,)), ((), ())), preferred_element_type=jnp.float32
            )
            terms[slot, pl.ds(pl.multiple_of(k * tile, tile), tile), :] = term.astype(terms.dtype)

    def share(slot):
        bit = slot & -slot
        return remote(terms.at[slot], got.at[slot], send_w.at[slot], recv_w.at[slot], "ctx", flipped(col, bit))

    def merge(slot, bit):
        share(slot + bit).wait_recv()
        if slot:
            total = terms[slot].astype(jnp.float32) + got[slot + bit].astype(jnp.float32)
            terms[slot] = total.astype(terms.dtype)
            if slot & (2 * bit):
                share(slot).start()
        else:
            held = sum_ref[...] if bit > 1 else terms[0].astype(jnp.float32)
            sum_ref[...] = held + got[bit].astype(jnp.float32)

    for slot in reversed(range(0, n_ctx, 2)):
        fill(slot + 1)
        share(slot + 1).start()
        fill(slot)
        merge(slot, 1)

    for step in range(1, n_dp):
        peer = lax.rem(row + step, n_dp)
        remote(gain_ref, gain_rows.at[peer], send_r.at[peer], recv_r.at[peer], "dp", peer).wait_recv()
    gain_total = gain_rows[0]
    for peer in range(1, n_dp):
        gain_total = gain_total + gain_rows[peer]
    for level, bit in enumerate(bits):
        gain_sent[level] = gain_total
        copy = remote(
            gain_sent.at[level], gain_got.at[level], send_c.at[level], recv_c.at[level],
            "ctx", flipped(col, bit),
        )
        copy.start()
        copy.wait()
        gain_total = gain_total + gain_got[level]
    gain_out[...] = gain_total

    for bit in bits[1:]:
        for slot in reversed(range(0, n_ctx, 2 * bit)):
            merge(slot, bit)
    for step in range(1, n_dp):
        gain_to(lax.rem(row + step, n_dp)).wait_send()
    for slot in range(1, n_ctx):
        share(slot).wait_send()
    own.wait()

    @pl.loop(1, n_dp)
    def _(step):
        source = lax.rem(row + step, n_dp)
        remote(outbox.at[source], back_ref.at[source], send_o.at[source], recv_o.at[source], "dp", source).wait_recv()
        back(source, source).wait_send()

    relay(row, 2, row + twin).wait_send()
    pl.when(place < line - 1)(lambda: relay(row, 0, row + 2).wait_send())
    pl.when(place > 0)(lambda: relay(row, 1, row - 2).wait_send())

    @pl.loop(1, line)
    def _(step):
        @pl.when(place >= step)
        def _():
            block = row - 2 * step
            pl.when(place < line - 1)(lambda: relay(block, 0, row + 2).wait_send())
            relay(block, 2, row + twin).wait_send()

        @pl.when(place + step < line)
        def _():
            block = row + 2 * step
            pl.when(place > 0)(lambda: relay(block, 1, row - 2).wait_send())
            relay(block, 2, row + twin).wait_send()


def projected(d_own, weight, cols, gains):
    n_dp, n_ctx = lax.axis_size("dp"), lax.axis_size("ctx")
    toks, width = d_own.shape
    part = weight.shape[0]
    dma = pltpu.SemaphoreType.DMA
    levels = n_ctx.bit_length() - 1
    vmem = pl.BlockSpec(memory_space=pltpu.VMEM)
    return pl.pallas_call(
        lambda *refs: project_kernel(n_dp, n_ctx, *refs),
        out_shape=(
            jax.ShapeDtypeStruct((n_dp, toks, part), jnp.bfloat16),
            jax.ShapeDtypeStruct((width // n_ctx, part), jnp.float32),
            jax.ShapeDtypeStruct(gains.shape, jnp.float32),
        ),
        in_specs=[vmem, vmem, vmem, vmem],
        out_specs=(pl.BlockSpec(memory_space=pl.ANY), vmem, vmem),
        scratch_shapes=[
            pltpu.VMEM((n_dp, toks, width), jnp.bfloat16),
            pltpu.VMEM((toks, part), jnp.float32),
            pltpu.VMEM((n_dp, toks, part), jnp.bfloat16),
            pltpu.VMEM((n_ctx, width // n_ctx, part), jnp.bfloat16),
            pltpu.VMEM((n_ctx, width // n_ctx, part), jnp.bfloat16),
            pltpu.VMEM((n_dp,) + gains.shape, jnp.float32),
            pltpu.VMEM((levels,) + gains.shape, jnp.float32),
            pltpu.VMEM((levels,) + gains.shape, jnp.float32),
            dma,
            dma((3, n_dp)),
            dma((n_dp,)),
            dma((n_dp,)),
            dma((n_dp,)),
            dma((n_ctx,)),
            dma((n_ctx,)),
            dma((n_dp,)),
            dma((n_dp,)),
            dma((levels,)),
            dma((levels,)),
        ],
        compiler_params=pltpu.CompilerParams(
            collective_id=2, has_side_effects=True, vmem_limit_bytes=56 * 1024 * 1024
        ),
        name="project",
    )(d_own, weight, cols, gains)


def rotated_unit(projected_rows, gain_vector, token_pos, head_count):
    head_width = gain_vector.shape[0]
    rows_heads = projected_rows.reshape(projected_rows.shape[0], head_count, head_width)
    inverse = lax.rsqrt(jnp.mean(rows_heads * rows_heads, axis=-1, keepdims=True) + norm_eps)
    normed = rows_heads * inverse * gain_vector
    half_width = head_width // 2
    frequency = jnp.exp(
        jnp.arange(half_width, dtype=jnp.float32) * (-2.0 * math.log(rope_base) / head_width)
    )
    angles = token_pos.astype(jnp.float32)[:, None] * frequency[None, :]
    cosine_table = jnp.cos(angles)[:, None, :]
    sine_table = jnp.sin(angles)[:, None, :]
    first_half = normed[..., :half_width]
    second_half = normed[..., half_width:]
    return jnp.concatenate(
        [
            first_half * cosine_table - second_half * sine_table,
            second_half * cosine_table + first_half * sine_table,
        ],
        axis=-1,
    )


def shards(inputs, q_proj, k_proj, v_proj, d_attn, positions, windows, q_gain, k_gain, weight):
    tok_rows = inputs.shape[1]
    head_width = q_gain.shape[0]
    query_heads = q_proj.shape[2] // head_width
    key_heads = k_proj.shape[2] // head_width
    group_size = query_heads // key_heads
    token_pos = positions[0]
    window = windows[0]
    dp_count = lax.axis_size("dp")
    model_width = inputs.shape[2]
    input_parts = inputs[0].reshape(tok_rows, dp_count, model_width // dp_count).transpose(1, 0, 2)
    def query_side(projected_rows, gain_vector):
        return rotated_unit(projected_rows, gain_vector, token_pos, query_heads)

    def key_side(projected_rows, gain_vector):
        return rotated_unit(projected_rows, gain_vector, token_pos, key_heads)

    q_full, query_back = jax.vjp(query_side, q_proj[0].astype(jnp.float32), q_gain)
    k_full, key_back = jax.vjp(key_side, k_proj[0].astype(jnp.float32), k_gain)
    query_rotated = q_full.astype(jnp.bfloat16).reshape(tok_rows, key_heads, group_size, head_width)
    key_rotated = k_full.astype(jnp.bfloat16)
    v_own = v_proj[0].reshape(tok_rows, key_heads, head_width)
    reach_count = min(REACH, lax.axis_size("ctx") - 1)
    own_pair = jnp.stack([key_rotated, v_own])
    input_cols, far_pairs = exchanged(input_parts, own_pair, reach_count)
    known = jnp.arange(1, reach_count + 1) <= lax.axis_index("ctx")
    far_pairs = jnp.where(known[:, None, None, None, None], far_pairs, 0)
    all_keys = jnp.concatenate([key_rotated[None], far_pairs[:, 0]])
    all_values = jnp.concatenate([v_own[None], far_pairs[:, 1]])
    block_ids = jnp.arange(reach_count + 1, dtype=jnp.int32)
    offsets = jnp.arange(tok_rows, dtype=jnp.int32)
    distance = block_ids[None, :, None] * tok_rows + offsets[:, None, None] - offsets[None, None, :]
    allowed = (distance >= 0) & (distance < window) & (distance <= token_pos[:, None, None])
    scores = (
        jnp.einsum("ahgd,bchd->hgabc", query_rotated, all_keys, preferred_element_type=jnp.float32)
        * score_scale
    )
    scores = jnp.where(allowed, scores, -jnp.inf)
    row_max = jnp.max(scores, axis=(3, 4), keepdims=True)
    exponent = jnp.exp(scores - row_max)
    probs = exponent / jnp.sum(exponent, axis=(3, 4), keepdims=True)
    head_gradient = d_attn[0].reshape(tok_rows, key_heads, group_size, head_width)
    dprobs = jnp.einsum(
        "ahgd,bchd->hgabc", head_gradient, all_values, preferred_element_type=jnp.float32
    )
    delta = jnp.sum(probs * dprobs, axis=(3, 4), keepdims=True)
    dscores = (probs * (dprobs - delta)).astype(jnp.bfloat16)
    probs_low = probs.astype(jnp.bfloat16)
    dq_rot = (
        jnp.einsum("hgabc,bchd->ahgd", dscores, all_keys, preferred_element_type=jnp.float32)
        * score_scale
    )
    dk_blocks = (
        jnp.einsum("hgabc,ahgd->bchd", dscores, query_rotated, preferred_element_type=jnp.float32)
        * score_scale
    )
    dv_blocks = jnp.einsum(
        "hgabc,ahgd->bchd", probs_low, head_gradient, preferred_element_type=jnp.float32
    )
    dq_proj, dq_gain = query_back(dq_rot.reshape(tok_rows, query_heads, head_width))
    pair_total = jnp.stack([dk_blocks[0], dv_blocks[0]])
    for distance_steps in range(1, reach_count + 1):
        far_pair = jnp.stack([dk_blocks[distance_steps], dv_blocks[distance_steps]])
        back_pair = from_behind(far_pair.astype(jnp.bfloat16), "ctx", -distance_steps)
        pair_total = pair_total + back_pair.astype(jnp.float32)
    dk_proj, dk_gain = key_back(pair_total[0])
    dv_proj = pair_total[1].reshape(tok_rows, key_heads * head_width)
    d_own = jnp.concatenate([dq_proj, dk_proj, dv_proj], axis=-1).astype(jnp.bfloat16)
    gains = jnp.pad(jnp.stack([dq_gain, dk_gain]), ((0, 6), (0, 0)))
    d_parts, d_weight_t, gain_sums = projected(d_own, weight, input_cols, gains)
    dq_gain_all, dk_gain_all = gain_sums[0], gain_sums[1]
    d_inputs = d_parts.transpose(1, 0, 2).reshape(1, tok_rows, model_width)
    return (d_inputs, d_weight_t, dq_gain_all, dk_gain_all)


def walk_code(line, place):
    digits = []
    for step in range(line + 1):
        if step == 0:
            digits.append(2 * place)
            continue
        for other in (place - step, place + step):
            if 0 <= other < line:
                digits.append(2 * other)
        for other in (place - step + 1, place + step - 1):
            if 0 <= other < line and 2 * other + 1 not in digits:
                digits.append(2 * other + 1)
    code = 0
    for digit in reversed(digits):
        code = code * 2 * line + digit
    return code


def unit_rows(values):
    inverse = lax.rsqrt(jnp.sum(values * values, axis=-1, keepdims=True) * (1.0 / values.shape[-1]) + norm_eps)
    return values * inverse, inverse


def turned(values, cosine, sine):
    return values * cosine + pltpu.roll(values, values.shape[-1] // 2, 1) * sine


def turned_back(values, cosine, sine):
    return values * cosine + pltpu.roll(values * sine, values.shape[-1] // 2, 1)


def norm_back(unit, inverse, gain, grad):
    scaled = grad * gain
    inner = jnp.sum(unit * scaled, axis=-1, keepdims=True) * (1.0 / unit.shape[-1])
    return inverse * (scaled - unit * inner)


def folded(values):
    return jnp.sum(values.reshape(values.shape[0] // 8, 8, values.shape[1]), axis=0)


def layer_kernel(
    n_dp, n_ctx, part,
    in_ref, q_ref, k_ref, v_ref, da_ref, pos_ref, win_ref, qgain_ref, kgain_ref, freq_ref, w_ref,
    din_ref, dw_ref, gain_out,
    qs, ks, vs, ds, pos_own, pos_all, cos_t, sin_t, low_t, qrot, dstack, krot, dk_acc, dv_acc,
    blocks, wext, cols, acc, prod, mine, keep, core_out, core_in, y_out, y_in, ret_out, ret_in,
    gain_acc, gain_own, gain_rows, gain_col, gain_cols, dw_out, dw_in,
    loc_a, loc_w, loc_x, send_p, recv_p, send_a, recv_a, send_x, recv_x, send_xy, recv_xy,
    send_xc, recv_xc, send_xf, recv_xf, send_g, recv_g, send_c, recv_c, send_y, recv_y, send_r, recv_r,
    send_n, recv_n, send_m, recv_m, send_d, recv_d,
):
    row = lax.axis_index("dp")
    col = lax.axis_index("ctx")
    line = n_dp // 2
    place = row // 2
    lane = lax.rem(row, 2)
    twin = row + 1 - 2 * lane
    head = qgain_ref.shape[1]
    toks = in_ref.shape[0]
    wide = cols.shape[2]
    peers = range(1, n_ctx)
    key_base = q_ref.shape[1]
    value_base = key_base + k_ref.shape[1]
    groups = qs.shape[0]
    pair = qs.shape[2]
    unit = blocks.shape[3]

    barrier = pltpu.get_barrier_semaphore()
    for step in range(1, n_dp):
        pl.semaphore_signal(barrier, 1, device_id={"dp": lax.rem(row + step, n_dp)}, device_id_type=MESH)
    for step in peers:
        pl.semaphore_signal(barrier, 1, device_id={"ctx": flipped(col, step)}, device_id_type=MESH)

    first_tile = row * part // head
    shift = row * part - first_tile * head
    wext[...] = jnp.zeros_like(wext)
    shifted = pl.ds(pl.multiple_of(shift, 32), part)

    def weight_copies(g):
        sources = (
            ((2 * groups * col + 2 * g) * head, 0, 2 * head),
            (key_base + (groups * col + g) * head, 2 * head, head),
            (value_base + (groups * col + g) * head, 3 * head, head),
        )
        return [
            pltpu.make_async_copy(
                w_ref.at[:, pl.ds(pl.multiple_of(start, head), size)],
                wext.at[g, shifted, pl.ds(at, size)],
                loc_w.at[g, n],
            )
            for n, (start, at, size) in enumerate(sources)
        ]

    pos_own[...] = jnp.broadcast_to(pos_ref[...].astype(jnp.float32), pos_own.shape)
    pos_all[col] = pos_own[...]
    own_rows = pl.ds(pl.multiple_of(col * toks, toks), toks)

    def piece(target, g, source_col):
        at = pl.ds(pl.multiple_of(source_col * toks, toks), toks)
        wide_at = pl.ds(pl.multiple_of((groups * target + g) * pair, pair), pair)
        thin_at = pl.ds(pl.multiple_of((groups * target + g) * head, head), head)
        return (
            (q_ref.at[:, wide_at], qs.at[g, at, :]),
            (k_ref.at[:, thin_at], ks.at[g, at, :]),
            (v_ref.at[:, thin_at], vs.at[g, at, :]),
            (da_ref.at[:, wide_at], ds.at[g, at, :]),
        )

    def head_copies(step, g, receiving=False):
        peer = flipped(col, step)
        return [
            remote(source, target, send_a.at[step, g, n], recv_a.at[step, g, n], "ctx", peer)
            for n, (source, target) in enumerate(piece(peer, g, peer if receiving else col))
        ]

    def own_copies(g):
        return [
            pltpu.make_async_copy(source, target, loc_a.at[g, n])
            for n, (source, target) in enumerate(piece(col, g, col))
        ]

    def pos_copy(step, source_col):
        return remote(pos_own, pos_all.at[source_col], send_p.at[step], recv_p.at[step], "ctx", flipped(col, step))

    for copy in own_copies(0):
        copy.start()
    pl.semaphore_wait(barrier, n_dp + n_ctx - 2)
    for step in peers:
        pos_copy(step, col).start()
    for g in range(groups):
        for step in reversed(peers):
            for copy in head_copies(step, g):
                copy.start()
    for g in range(1, groups):
        for copy in own_copies(g):
            copy.start()

    def slab(index):
        start = index * part // head
        return pl.ds(pl.multiple_of(start * head, head), wide)

    def col_send(peer):
        return remote(in_ref.at[:, slab(peer)], cols.at[row, own_rows, :], send_x.at[peer], recv_x.at[row], "dp", peer)

    def col_recv(source):
        return remote(in_ref.at[:, slab(row)], cols.at[source, own_rows, :], send_x.at[source], recv_x.at[source], "dp", source)

    for step in range(1, n_dp):
        col_send(lax.rem(row + step, n_dp)).start()
    own_cols = pltpu.make_async_copy(in_ref.at[:, slab(row)], cols.at[row, own_rows, :], loc_x)
    own_cols.start()
    for g in range(groups):
        for copy in weight_copies(g):
            copy.start()

    for step in peers:
        pos_copy(step, flipped(col, step)).wait_recv()

    @pl.loop(0, n_ctx)
    def _(block):
        rows = pl.ds(pl.multiple_of(block * toks, toks), toks)
        place_rows = jnp.broadcast_to(pos_all[block][0:1, :], (toks, toks)).T
        angle = place_rows * freq_ref[...]
        side = lax.broadcasted_iota(jnp.int32, (toks, head), 1)
        cos_t[rows, :] = jnp.cos(angle)
        sine = jnp.sin(angle)
        sin_t[rows, :] = jnp.where(side < head // 2, -sine, sine)
        index = lax.broadcasted_iota(jnp.int32, (toks, head), 0) + block * toks
        low_t[rows, :] = index - jnp.minimum(win_ref[0] - 1, place_rows.astype(jnp.int32))

    gain_acc[...] = jnp.zeros_like(gain_acc)

    def relay(block, g, way, target):
        return remote(blocks.at[block, g], blocks.at[block, g], send_g.at[way, block, g], recv_g.at[block, g], "dp", target)

    @pl.loop(0, groups)
    def _(g):
        for step in reversed(peers):
            for copy in head_copies(step, g, True):
                copy.wait_recv()
        for copy in own_copies(g):
            copy.wait()

        @pl.loop(0, n_ctx)
        def _(block):
            rows = pl.ds(pl.multiple_of(block * toks, toks), toks)
            cosine, sine = cos_t[rows, :], sin_t[rows, :]
            key_unit, _ = unit_rows(ks[g, rows, :].astype(jnp.float32))
            krot[rows, :] = turned(key_unit * kgain_ref[...], cosine, sine).astype(krot.dtype)
            for h in range(2):
                span = slice(h * head, (h + 1) * head)
                at = slice(h * toks, (h + 1) * toks)
                query_unit, _ = unit_rows(qs[g, rows, span].astype(jnp.float32))
                qrot[block, at, :] = turned(query_unit * qgain_ref[...], cosine, sine).astype(qrot.dtype)
                dstack[block, at, :] = ds[g, rows, span]

        dk_acc[...] = jnp.zeros_like(dk_acc)
        dv_acc[...] = jnp.zeros_like(dv_acc)
        for block in range(n_ctx):
            count = (block + 1) * toks
            rows = slice(block * toks, (block + 1) * toks)
            query, grad = qrot[block], dstack[block]
            keys, values = krot[:count, :], vs[g, :count, :]
            contract_last = (((1,), (1,)), ((), ()))
            contract_first = (((0,), (0,)), ((), ()))
            scores = lax.dot_general(query, keys, contract_last, preferred_element_type=jnp.float32) * score_scale
            key_at = lax.broadcasted_iota(jnp.int32, scores.shape, 1)
            query_at = lax.rem(lax.broadcasted_iota(jnp.int32, scores.shape, 0), toks) + block * toks
            low = jnp.concatenate([low_t[rows, :]] * 2, axis=0)
            low = jnp.concatenate([low] * (block + 1), axis=1)
            scores = jnp.where((key_at >= low) & (key_at <= query_at), scores, -jnp.inf)
            exponent = jnp.exp(scores - jnp.max(scores, axis=-1, keepdims=True))
            probs = exponent * (1.0 / jnp.sum(exponent, axis=-1, keepdims=True))
            dprobs = lax.dot_general(grad, values, contract_last, preferred_element_type=jnp.float32)
            delta = jnp.sum(probs * dprobs, axis=-1, keepdims=True)
            dscores = (probs * (dprobs - delta)).astype(jnp.bfloat16)
            dquery = (
                lax.dot_general(dscores, keys, (((1,), (0,)), ((), ())), preferred_element_type=jnp.float32)
                * score_scale
            )
            dk_acc[:count, :] += lax.dot_general(dscores, query, contract_first, preferred_element_type=jnp.float32)
            dv_acc[:count, :] += lax.dot_general(
                probs.astype(jnp.bfloat16), grad, contract_first, preferred_element_type=jnp.float32
            )
            cosine, sine = cos_t[rows, :], sin_t[rows, :]
            for h in range(2):
                span = slice(h * head, (h + 1) * head)
                query_unit, inverse = unit_rows(qs[g, rows, span].astype(jnp.float32))
                back = turned_back(dquery[h * toks:(h + 1) * toks, :], cosine, sine)
                gain_acc[0] += folded(back * query_unit)
                blocks[row, g, rows, span] = norm_back(query_unit, inverse, qgain_ref[...], back).astype(blocks.dtype)

        @pl.loop(0, n_ctx)
        def _(block):
            rows = pl.ds(pl.multiple_of(block * toks, toks), toks)
            key_unit, inverse = unit_rows(ks[g, rows, :].astype(jnp.float32))
            back = turned_back(dk_acc[rows, :] * score_scale, cos_t[rows, :], sin_t[rows, :])
            gain_acc[1] += folded(back * key_unit)
            blocks[row, g, rows, 2 * head:3 * head] = norm_back(
                key_unit, inverse, kgain_ref[...], back
            ).astype(blocks.dtype)
            blocks[row, g, rows, 3 * head:4 * head] = dv_acc[rows, :].astype(blocks.dtype)

        relay(row, g, 2, twin).start()
        pl.when(place < line - 1)(lambda: relay(row, g, 0, row + 2).start())
        pl.when(place > 0)(lambda: relay(row, g, 1, row - 2).start())

    gain_own[...] = jnp.zeros_like(gain_own)
    gain_own[0:1, :] = jnp.sum(gain_acc[0], axis=0, keepdims=True)
    gain_own[1:2, :] = jnp.sum(gain_acc[1], axis=0, keepdims=True)
    gain_rows[row] = gain_own[...]

    def gain_to(peer, source):
        return remote(gain_own, gain_rows.at[source], send_n.at[peer], recv_n.at[source], "dp", peer)

    def gain_across(step, source_col):
        return remote(gain_col, gain_cols.at[source_col], send_m.at[step], recv_m.at[step], "ctx", flipped(col, step))

    for step in range(1, n_dp):
        gain_to(lax.rem(row + step, n_dp), row).start()

    code = walk_code(line, 0)
    for other in range(1, line):
        code = jnp.where(place == other, walk_code(line, other), code)

    def member(digit):
        flag = lax.rem(digit, 2)
        return digit - flag + lane + flag * (1 - 2 * lane)

    def rows_of(step):
        return pl.ds(pl.multiple_of(flipped(col, step) * toks, toks), toks)

    def cols_out(block, step, sends, recvs, receiving=False, rows=0):
        at = rows_of((rows ^ step) if receiving else rows)
        return remote(
            cols.at[block, at, :], cols.at[block, at, :], sends.at[block], recvs.at[block], "ctx", flipped(col, step)
        )

    def spread(k, rest):
        block = member(lax.rem(rest, n_dp))
        pl.when(block != row)(lambda: col_recv(block).wait_recv())
        pl.when(block == row)(own_cols.wait)
        cols_out(block, 2, send_xy, recv_xy).start()
        cols_out(block, 1, send_xc, recv_xc).start()
        return rest // n_dp

    lax.fori_loop(0, n_dp, spread, code)
    for g in range(groups):
        for copy in weight_copies(g):
            copy.wait()
    acc[...] = jnp.zeros_like(acc)

    def core_copy(block):
        return remote(core_out.at[block], core_in.at[block], send_c.at[block], recv_c.at[block], "ctx", flipped(col, 1))

    def y_copy(block):
        return remote(y_out.at[block], y_in.at[block], send_y.at[block], recv_y.at[block], "ctx", flipped(col, 2))

    def back_send(block):
        return remote(ret_out.at[block], ret_in.at[row], send_r.at[block], recv_r.at[row], "dp", block)

    def back_recv(source):
        return remote(ret_out.at[source], ret_in.at[source], send_r.at[source], recv_r.at[source], "dp", source)

    tile = 256

    def take(k, block, digit):
        zone = digit // 2
        flag = lax.rem(digit, 2)
        for g in range(groups):
            pl.when(block != row)(lambda: relay(block, g, 2, twin).wait_recv())

            @pl.when((flag == 0) & (zone < place))
            def _():
                pl.when(place < line - 1)(lambda: relay(block, g, 0, row + 2).start())
                relay(block, g, 2, twin).start()

            @pl.when((flag == 0) & (zone > place))
            def _():
                pl.when(place > 0)(lambda: relay(block, g, 1, row - 2).start())
                relay(block, g, 2, twin).start()

        @pl.loop(0, wide // tile)
        def _(n):
            span = pl.ds(pl.multiple_of(n * tile, tile), tile)
            total = None
            for g in range(groups):
                term = lax.dot_general(
                    blocks[block, g], wext[g, span, :], (((1,), (1,)), ((), ())), preferred_element_type=jnp.float32
                )
                total = term if total is None else total + term
            prod[:, span] = total

        slot = lax.rem(k, 2)
        core_out[block, 0] = prod[rows_of(1), :].astype(core_out.dtype)
        core_out[block, 1] = prod[rows_of(3), :].astype(core_out.dtype)
        core_copy(block).start()
        mine[slot, 0] = prod[rows_of(0), :]
        mine[slot, 1] = prod[rows_of(2), :]

    def cross_core(k, block):
        slot = lax.rem(k + 1, 2)
        core_copy(block).wait_recv()
        y_out[block] = (mine[slot, 1] + core_in[block, 1].astype(jnp.float32)).astype(y_out.dtype)
        y_copy(block).start()
        keep[slot] = mine[slot, 0] + core_in[block, 0].astype(jnp.float32)

    def cross_y(k, block):
        slot = lax.rem(k, 2)
        y_copy(block).wait_recv()
        total = (keep[slot] + y_in[block].astype(jnp.float32)).astype(ret_out.dtype)

        @pl.when(block != row)
        def _():
            ret_out[block] = total
            back_send(block).start()

        @pl.when(block == row)
        def _():
            ret_in[row] = total

    def weigh(block):
        cols_out(block, 1, send_xc, recv_xc, True).wait_recv()
        cols_out(block, 1, send_xf, recv_xf, True, 2).wait_recv()
        for g in range(groups):
            @pl.loop(0, unit // tile)
            def _(n):
                span = pl.ds(pl.multiple_of(n * tile, tile), tile)
                at = pl.ds(pl.multiple_of(g * unit + n * tile, tile), tile)
                acc[at, :] += lax.dot_general(
                    blocks[block, g, :, span], cols[block], (((0,), (0,)), ((), ())),
                    preferred_element_type=jnp.float32,
                )

    def walk(k, carry):
        rest, last, older = carry
        digit = lax.rem(rest, n_dp)
        block = member(digit)
        pl.when(k < n_dp)(lambda: take(k, block, digit))
        pl.when((k >= 1) & (k <= n_dp))(lambda: cross_core(k, last))
        pl.when(k >= 2)(lambda: cross_y(k, older))
        pl.when((k >= 1) & (k <= n_dp))(lambda: weigh(last))

        @pl.when(k < n_dp)
        def _():
            cols_out(block, 2, send_xy, recv_xy, True).wait_recv()
            cols_out(block, 1, send_xf, recv_xf, False, 2).start()

        @pl.when(k == 2)
        def _():
            for step in range(1, n_dp):
                source = lax.rem(row + step, n_dp)
                gain_to(source, source).wait_recv()
            total = gain_rows[0]
            for other in range(1, n_dp):
                total = total + gain_rows[other]
            gain_col[...] = total
            gain_cols[col] = total
            for step in peers:
                gain_across(step, col).start()

        return rest // n_dp, block, last

    lax.fori_loop(0, n_dp + 2, walk, (code, row, row))

    def shares(g, source, receiving):
        q_target, k_target, v_target = source // 2, n_ctx // 2, n_ctx // 2 + 1
        plans = (
            (0, 2 * head, q_target, lax.rem(source, 2) * groups * 2 * head + g * 2 * head),
            (2 * head, head, k_target, (groups * source + g) * head),
            (3 * head, head, v_target, (groups * source + g) * head),
        )
        out = []
        for n, (start, size, target, at) in enumerate(plans):
            out.append((target, remote(
                dw_out.at[pl.ds(g * unit + start, size), :],
                dw_in.at[pl.ds(pl.multiple_of(at, head), size), :],
                send_d.at[g, n], recv_d.at[source, g], "ctx", source if receiving else target,
            ), start, size, at))
        return out

    for g in range(groups):
        half = slice(g * unit, (g + 1) * unit)
        dw_out[half, :] = acc[half, :].astype(dw_out.dtype)
        for target, copy, _, _, _ in shares(g, col, False):
            pl.when(target != col)(copy.start)

    for step in peers:
        gain_across(step, flipped(col, step)).wait_recv()
    gain_total = gain_cols[0]
    for other in range(1, n_ctx):
        gain_total = gain_total + gain_cols[other]
    gain_out[...] = gain_total

    for step in range(1, n_dp):
        back_recv(lax.rem(row + step, n_dp)).wait_recv()
    starts = [index * part // head for index in range(n_dp)]
    pieces = wide // head
    for index in range(n_dp):
        first = 1 if index > 0 and starts[index] < starts[index - 1] + pieces else 0
        last = pieces - 1 if index + 1 < n_dp and starts[index + 1] < starts[index] + pieces else pieces
        base = starts[index] * head
        din_ref[:, base + first * head:base + last * head] = ret_in[index, :, first * head:last * head]
        if last < pieces:
            both = ret_in[index, :, last * head:].astype(jnp.float32) + ret_in[index + 1, :, :head].astype(jnp.float32)
            din_ref[:, base + last * head:base + pieces * head] = both.astype(din_ref.dtype)

    def finish(read, at, size):
        for rest in sorted({index * part % head for index in range(n_dp)}):
            @pl.when(shift == rest)
            def _():
                dw_ref[pl.ds(pl.multiple_of(at, head), size), :] = read()[:, rest:rest + part]

    for step in range(n_ctx):
        source = flipped(col, step)
        for g in range(groups):
            for target, copy, start, size, at in shares(g, source, True):
                @pl.when(target == col)
                def _():
                    if step == 0:
                        finish(lambda: acc[g * unit + start:g * unit + start + size, :], at, size)
                    else:
                        copy.wait_recv()
                        finish(
                            lambda: dw_in[pl.ds(pl.multiple_of(at, head), size), :].astype(jnp.float32), at, size
                        )

    for step in peers:
        pos_copy(step, col).wait_send()
        gain_across(step, col).wait_send()
        for g in range(groups):
            for copy in head_copies(step, g):
                copy.wait_send()
    for g in range(groups):
        for target, copy, _, _, _ in shares(g, col, False):
            pl.when(target != col)(copy.wait_send)

    @pl.loop(1, n_dp)
    def _(step):
        peer = lax.rem(row + step, n_dp)
        col_send(peer).wait_send()
        gain_to(peer, row).wait_send()
        back_send(peer).wait_send()

    @pl.loop(0, n_dp)
    def _(block):
        cols_out(block, 2, send_xy, recv_xy).wait_send()
        cols_out(block, 1, send_xc, recv_xc).wait_send()
        cols_out(block, 1, send_xf, recv_xf, False, 2).wait_send()
        core_copy(block).wait_send()
        y_copy(block).wait_send()
        zone = block // 2

        @pl.when(lax.rem(block, 2) == lane)
        def _():
            for g in range(groups):
                relay(block, g, 2, twin).wait_send()
                pl.when((zone <= place) & (place < line - 1))(lambda: relay(block, g, 0, row + 2).wait_send())
                pl.when((zone >= place) & (place > 0))(lambda: relay(block, g, 1, row - 2).wait_send())


def layer(inputs, q_proj, k_proj, v_proj, d_attn, positions, windows, q_gain, k_gain, weight):
    n_dp, n_ctx = lax.axis_size("dp"), lax.axis_size("ctx")
    toks, model = inputs.shape
    part = weight.shape[0]
    head = q_gain.shape[0]
    groups = k_proj.shape[1] // head // n_ctx
    pair = q_proj.shape[1] // n_ctx // groups
    unit = pair + 2 * head
    length = n_ctx * toks
    wide = max(-(-(index * part % head + part) // head) for index in range(n_dp)) * head
    frequency = np.exp(np.arange(head // 2) * (-2.0 * math.log(rope_base) / head))
    frequency = jnp.asarray(np.tile(frequency, 2)[None, :], jnp.float32)
    dma = pltpu.SemaphoreType.DMA
    vmem = pl.BlockSpec(memory_space=pltpu.VMEM)
    smem = pl.BlockSpec(memory_space=pltpu.SMEM)
    anywhere = pl.BlockSpec(memory_space=pl.ANY)
    low, full = jnp.bfloat16, jnp.float32
    return pl.pallas_call(
        lambda *refs: layer_kernel(n_dp, n_ctx, part, *refs),
        out_shape=(
            jax.ShapeDtypeStruct((toks, model), low),
            jax.ShapeDtypeStruct((groups * unit, part), full),
            jax.ShapeDtypeStruct((8, head), full),
        ),
        in_specs=[anywhere] * 5 + [vmem, smem, vmem, vmem, vmem, anywhere],
        out_specs=(vmem, vmem, vmem),
        scratch_shapes=[
            pltpu.VMEM((groups, length, pair), low),
            pltpu.VMEM((groups, length, head), low),
            pltpu.VMEM((groups, length, head), low),
            pltpu.VMEM((groups, length, pair), low),
            pltpu.VMEM((8, head), full),
            pltpu.VMEM((n_ctx, 8, head), full),
            pltpu.VMEM((length, head), full),
            pltpu.VMEM((length, head), full),
            pltpu.VMEM((length, head), jnp.int32),
            pltpu.VMEM((n_ctx, 2 * toks, head), low),
            pltpu.VMEM((n_ctx, 2 * toks, head), low),
            pltpu.VMEM((length, head), low),
            pltpu.VMEM((length, head), full),
            pltpu.VMEM((length, head), full),
            pltpu.VMEM((n_dp, groups, length, unit), low),
            pltpu.VMEM((groups, wide, unit), low),
            pltpu.VMEM((n_dp, length, wide), low),
            pltpu.VMEM((groups * unit, wide), full),
            pltpu.VMEM((length, wide), full),
            pltpu.VMEM((2, 2, toks, wide), full),
            pltpu.VMEM((2, toks, wide), full),
            pltpu.VMEM((n_dp, 2, toks, wide), low),
            pltpu.VMEM((n_dp, 2, toks, wide), low),
            pltpu.VMEM((n_dp, toks, wide), low),
            pltpu.VMEM((n_dp, toks, wide), low),
            pltpu.VMEM((n_dp, toks, wide), low),
            pltpu.VMEM((n_dp, toks, wide), low),
            pltpu.VMEM((2, 8, head), full),
            pltpu.VMEM((8, head), full),
            pltpu.VMEM((n_dp, 8, head), full),
            pltpu.VMEM((8, head), full),
            pltpu.VMEM((n_ctx, 8, head), full),
            pltpu.VMEM((groups * unit, wide), low),
            pltpu.VMEM((groups * unit, wide), low),
            dma((groups, 4)),
            dma((groups, 3)),
            dma,
            dma((n_ctx,)),
            dma((n_ctx,)),
            dma((n_ctx, groups, 4)),
            dma((n_ctx, groups, 4)),
            dma((n_dp,)),
            dma((n_dp,)),
            dma((n_dp,)),
            dma((n_dp,)),
            dma((n_dp,)),
            dma((n_dp,)),
            dma((n_dp,)),
            dma((n_dp,)),
            dma((3, n_dp, groups)),
            dma((n_dp, groups)),
            dma((n_dp,)),
            dma((n_dp,)),
            dma((n_dp,)),
            dma((n_dp,)),
            dma((n_dp,)),
            dma((n_dp,)),
            dma((n_dp,)),
            dma((n_dp,)),
            dma((n_ctx,)),
            dma((n_ctx,)),
            dma((groups, 3)),
            dma((n_ctx, groups)),
        ],
        compiler_params=pltpu.CompilerParams(
            collective_id=3, has_side_effects=True, vmem_limit_bytes=58 * 1024 * 1024
        ),
        name="layer",
    )(
        inputs, q_proj, k_proj, v_proj, d_attn, positions, windows,
        q_gain[None, :], k_gain[None, :], frequency, weight,
    )


def head_shards(inputs, q_proj, k_proj, v_proj, d_attn, positions, windows, q_gain, k_gain, weight):
    d_inputs, d_weight_t, gains = layer(
        inputs[0], q_proj[0], k_proj[0], v_proj[0], d_attn[0], positions, windows, q_gain, k_gain, weight
    )
    return (d_inputs[None], d_weight_t, gains[0], gains[1])


def by_heads(mesh):
    return mesh.shape["dp"] == 8 and mesh.shape["ctx"] == 4


def solution(mesh):
    placed = (
        P("dp", "ctx", None),
        P("dp", "ctx", None),
        P("dp", "ctx", None),
        P("dp", "ctx", None),
        P("dp", "ctx", None),
        P("dp", "ctx"),
        P("dp"),
        P(),
        P(),
        P("dp", None),
    )
    return jax.shard_map(
        head_shards if by_heads(mesh) else shards,
        mesh=mesh,
        in_specs=placed,
        out_specs=(P("dp", "ctx", None), P("ctx", "dp"), P(), P()),
        check_vma=False,
    )
```

```python
import math

import jax
import jax.numpy as jnp
import numpy as np
from jax import lax
from jax.experimental import pallas as pl
from jax.experimental.pallas import tpu as pltpu
from jax.sharding import PartitionSpec as P

MESH = pl.DeviceIdType.MESH

REACH = 8


score_scale = 168.0 ** (-0.5)
rope_base = 10000.0
norm_eps = 1e-06


def from_behind(value, axis, steps):
    count = lax.axis_size(axis)
    initial, last = (max(0, -steps), min(count, count - steps))
    return lax.ppermute(value, axis, [(source, source + steps) for source in range(initial, last)])


def swapped(value, axis, bit):
    count = lax.axis_size(axis)
    return lax.ppermute(value, axis, [(source, source ^ bit) for source in range(count)])


def flipped(index, bits):
    bit = 1
    while bit <= bits:
        if bits & bit:
            index = index + bit - 2 * bit * (lax.rem(index // bit, 2))
        bit *= 2
    return index


def remote(source, target, send_sem, recv_sem, axis, index):
    return pltpu.make_async_remote_copy(
        src_ref=source,
        dst_ref=target,
        send_sem=send_sem,
        recv_sem=recv_sem,
        device_id={axis: index},
        device_id_type=MESH,
    )


def exchange_kernel(n_dp, n_ctx, reach, parts_ref, pair_ref, cols_ref, far_ref, own_sem, send_a, recv_a, send_b, recv_b):
    row = lax.axis_index("dp")
    col = lax.axis_index("ctx")
    barrier = pltpu.get_barrier_semaphore()
    for step in range(1, n_dp):
        pl.semaphore_signal(barrier, 1, device_id={"dp": lax.rem(row + step, n_dp)}, device_id_type=MESH)
    for step in range(1, n_ctx):
        pl.semaphore_signal(barrier, 1, device_id={"ctx": lax.rem(col + step, n_ctx)}, device_id_type=MESH)
    pl.semaphore_wait(barrier, n_dp + n_ctx - 2)
    for step in range(1, reach + 1):
        copy = remote(pair_ref, far_ref.at[step - 1], send_b.at[step], recv_b.at[step], "ctx", lax.rem(col + step, n_ctx))
        pl.when(col + step < n_ctx)(copy.start)
    own = pltpu.make_async_copy(parts_ref.at[row], cols_ref.at[row], own_sem)
    own.start()
    sends = []
    for step in range(1, n_dp):
        peer = lax.rem(row + step, n_dp)
        copy = remote(parts_ref.at[peer], cols_ref.at[row], send_a.at[step], recv_a.at[step], "dp", peer)
        copy.start()
        sends.append(copy)
    own.wait()
    for step in range(1, n_dp):
        source = lax.rem(row + n_dp - step, n_dp)
        remote(parts_ref.at[source], cols_ref.at[source], send_a.at[step], recv_a.at[step], "dp", source).wait_recv()
        sends[step - 1].wait_send()
    for step in range(1, reach + 1):
        copy = remote(pair_ref, far_ref.at[step - 1], send_b.at[step], recv_b.at[step], "ctx", lax.rem(col + step, n_ctx))
        pl.when(col + step < n_ctx)(copy.wait_send)
        pl.when(col >= step)(copy.wait_recv)


def exchanged(parts, pair, reach):
    n_dp, n_ctx = lax.axis_size("dp"), lax.axis_size("ctx")
    anywhere = pl.BlockSpec(memory_space=pl.ANY)
    dma = pltpu.SemaphoreType.DMA
    return pl.pallas_call(
        lambda *refs: exchange_kernel(n_dp, n_ctx, reach, *refs),
        out_shape=(
            jax.ShapeDtypeStruct(parts.shape, parts.dtype),
            jax.ShapeDtypeStruct((reach,) + pair.shape, pair.dtype),
        ),
        in_specs=[anywhere, anywhere],
        out_specs=(anywhere, anywhere),
        scratch_shapes=[dma, dma((n_dp,)), dma((n_dp,)), dma((reach + 1,)), dma((reach + 1,))],
        compiler_params=pltpu.CompilerParams(collective_id=1, has_side_effects=True),
        name="exchange",
    )(parts, pair)


def project_kernel(
    n_dp, n_ctx, d_ref, w_ref, cols_ref, gain_ref, back_ref, sum_ref, gain_out,
    blocks, acc, outbox, terms, got, gain_rows, gain_sent, gain_got,
    own_sem, send_g, recv_g, send_o, recv_o, send_w, recv_w, send_r, recv_r, send_c, recv_c,
):
    row = lax.axis_index("dp")
    col = lax.axis_index("ctx")
    line = n_dp // 2
    place = row // 2
    lane = lax.rem(row, 2)
    twin = 1 - 2 * lane
    width = w_ref.shape[1]
    bits = [1 << k for k in range(n_ctx.bit_length() - 1)]
    barrier = pltpu.get_barrier_semaphore()
    for step in range(1, n_dp):
        pl.semaphore_signal(barrier, 1, device_id={"dp": lax.rem(row + step, n_dp)}, device_id_type=MESH)
    for bit in bits:
        pl.semaphore_signal(barrier, 1, device_id={"ctx": flipped(col, bit)}, device_id_type=MESH)
    pl.semaphore_wait(barrier, n_dp - 1 + len(bits))

    def relay(block, way, target):
        return remote(blocks.at[block], blocks.at[block], send_g.at[way, block], recv_g.at[block], "dp", target)

    def arrived(block):
        relay(block, 0, lax.rem(row + 1, n_dp)).wait_recv()

    def back(block, target):
        return remote(outbox.at[block], back_ref.at[row], send_o.at[block], recv_o.at[row], "dp", target)

    def product(block):
        acc[...] = jnp.zeros_like(acc)
        depth = 2048

        @pl.loop(0, width // depth)
        def _(k):
            span = pl.ds(pl.multiple_of(k * depth, depth), depth)
            acc[...] += lax.dot_general(
                blocks[block, :, span], w_ref[:, span], (((1,), (1,)), ((), ())),
                preferred_element_type=jnp.float32,
            )

        outbox[block] = acc[...].astype(outbox.dtype)

    def answer(block):
        product(block)
        back(block, block).start()

    blocks[row] = d_ref[...]
    pl.when(place < line - 1)(lambda: relay(row, 0, row + 2).start())
    pl.when(place > 0)(lambda: relay(row, 1, row - 2).start())
    relay(row, 2, row + twin).start()

    def gain_to(peer):
        return remote(gain_ref, gain_rows.at[row], send_r.at[peer], recv_r.at[row], "dp", peer)

    gain_rows[row] = gain_ref[...]
    for step in range(1, n_dp):
        gain_to(lax.rem(row + step, n_dp)).start()
    product(row)
    own = pltpu.make_async_copy(outbox.at[row], back_ref.at[row], own_sem)
    own.start()

    @pl.loop(1, line + 1)
    def _(step):
        @pl.when(place >= step)
        def _():
            block = row - 2 * step
            arrived(block)
            pl.when(place < line - 1)(lambda: relay(block, 0, row + 2).start())
            relay(block, 2, row + twin).start()

        @pl.when(place + step < line)
        def _():
            block = row + 2 * step
            arrived(block)
            pl.when(place > 0)(lambda: relay(block, 1, row - 2).start())
            relay(block, 2, row + twin).start()

        pl.when(place >= step)(lambda: answer(row - 2 * step))
        pl.when(place + step < line)(lambda: answer(row + 2 * step))

        @pl.when(place >= step - 1)
        def _():
            block = row + twin - 2 * (step - 1)
            arrived(block)
            answer(block)

        @pl.when((step > 1) & (place + step - 1 < line))
        def _():
            block = row + twin + 2 * (step - 1)
            arrived(block)
            answer(block)

    tokens = n_dp * blocks.shape[1]
    rows = width // n_ctx
    tile = min(512, rows)

    def fill(slot):
        start = flipped(col, slot) * rows

        @pl.loop(0, rows // tile)
        def _(k):
            span = pl.ds(pl.multiple_of(start + k * tile, tile), tile)
            left = blocks[:, :, span].reshape(tokens, tile)
            right = cols_ref[...].reshape(tokens, cols_ref.shape[2])
            term = lax.dot_general(
                left, right, (((0,), (0,)), ((), ())), preferred_element_type=jnp.float32
            )
            terms[slot, pl.ds(pl.multiple_of(k * tile, tile), tile), :] = term.astype(terms.dtype)

    def share(slot):
        bit = slot & -slot
        return remote(terms.at[slot], got.at[slot], send_w.at[slot], recv_w.at[slot], "ctx", flipped(col, bit))

    def merge(slot, bit):
        share(slot + bit).wait_recv()
        if slot:
            total = terms[slot].astype(jnp.float32) + got[slot + bit].astype(jnp.float32)
            terms[slot] = total.astype(terms.dtype)
            if slot & (2 * bit):
                share(slot).start()
        else:
            held = sum_ref[...] if bit > 1 else terms[0].astype(jnp.float32)
            sum_ref[...] = held + got[bit].astype(jnp.float32)

    for slot in reversed(range(0, n_ctx, 2)):
        fill(slot + 1)
        share(slot + 1).start()
        fill(slot)
        merge(slot, 1)

    for step in range(1, n_dp):
        peer = lax.rem(row + step, n_dp)
        remote(gain_ref, gain_rows.at[peer], send_r.at[peer], recv_r.at[peer], "dp", peer).wait_recv()
    gain_total = gain_rows[0]
    for peer in range(1, n_dp):
        gain_total = gain_total + gain_rows[peer]
    for level, bit in enumerate(bits):
        gain_sent[level] = gain_total
        copy = remote(
            gain_sent.at[level], gain_got.at[level], send_c.at[level], recv_c.at[level],
            "ctx", flipped(col, bit),
        )
        copy.start()
        copy.wait()
        gain_total = gain_total + gain_got[level]
    gain_out[...] = gain_total

    for bit in bits[1:]:
        for slot in reversed(range(0, n_ctx, 2 * bit)):
            merge(slot, bit)
    for step in range(1, n_dp):
        gain_to(lax.rem(row + step, n_dp)).wait_send()
    for slot in range(1, n_ctx):
        share(slot).wait_send()
    own.wait()

    @pl.loop(1, n_dp)
    def _(step):
        source = lax.rem(row + step, n_dp)
        remote(outbox.at[source], back_ref.at[source], send_o.at[source], recv_o.at[source], "dp", source).wait_recv()
        back(source, source).wait_send()

    relay(row, 2, row + twin).wait_send()
    pl.when(place < line - 1)(lambda: relay(row, 0, row + 2).wait_send())
    pl.when(place > 0)(lambda: relay(row, 1, row - 2).wait_send())

    @pl.loop(1, line)
    def _(step):
        @pl.when(place >= step)
        def _():
            block = row - 2 * step
            pl.when(place < line - 1)(lambda: relay(block, 0, row + 2).wait_send())
            relay(block, 2, row + twin).wait_send()

        @pl.when(place + step < line)
        def _():
            block = row + 2 * step
            pl.when(place > 0)(lambda: relay(block, 1, row - 2).wait_send())
            relay(block, 2, row + twin).wait_send()


def projected(d_own, weight, cols, gains):
    n_dp, n_ctx = lax.axis_size("dp"), lax.axis_size("ctx")
    toks, width = d_own.shape
    part = weight.shape[0]
    dma = pltpu.SemaphoreType.DMA
    levels = n_ctx.bit_length() - 1
    vmem = pl.BlockSpec(memory_space=pltpu.VMEM)
    return pl.pallas_call(
        lambda *refs: project_kernel(n_dp, n_ctx, *refs),
        out_shape=(
            jax.ShapeDtypeStruct((n_dp, toks, part), jnp.bfloat16),
            jax.ShapeDtypeStruct((width // n_ctx, part), jnp.float32),
            jax.ShapeDtypeStruct(gains.shape, jnp.float32),
        ),
        in_specs=[vmem, vmem, vmem, vmem],
        out_specs=(pl.BlockSpec(memory_space=pl.ANY), vmem, vmem),
        scratch_shapes=[
            pltpu.VMEM((n_dp, toks, width), jnp.bfloat16),
            pltpu.VMEM((toks, part), jnp.float32),
            pltpu.VMEM((n_dp, toks, part), jnp.bfloat16),
            pltpu.VMEM((n_ctx, width // n_ctx, part), jnp.bfloat16),
            pltpu.VMEM((n_ctx, width // n_ctx, part), jnp.bfloat16),
            pltpu.VMEM((n_dp,) + gains.shape, jnp.float32),
            pltpu.VMEM((levels,) + gains.shape, jnp.float32),
            pltpu.VMEM((levels,) + gains.shape, jnp.float32),
            dma,
            dma((3, n_dp)),
            dma((n_dp,)),
            dma((n_dp,)),
            dma((n_dp,)),
            dma((n_ctx,)),
            dma((n_ctx,)),
            dma((n_dp,)),
            dma((n_dp,)),
            dma((levels,)),
            dma((levels,)),
        ],
        compiler_params=pltpu.CompilerParams(
            collective_id=2, has_side_effects=True, vmem_limit_bytes=56 * 1024 * 1024
        ),
        name="project",
    )(d_own, weight, cols, gains)


def rotated_unit(projected_rows, gain_vector, token_pos, head_count):
    head_width = gain_vector.shape[0]
    rows_heads = projected_rows.reshape(projected_rows.shape[0], head_count, head_width)
    inverse = lax.rsqrt(jnp.mean(rows_heads * rows_heads, axis=-1, keepdims=True) + norm_eps)
    normed = rows_heads * inverse * gain_vector
    half_width = head_width // 2
    frequency = jnp.exp(
        jnp.arange(half_width, dtype=jnp.float32) * (-2.0 * math.log(rope_base) / head_width)
    )
    angles = token_pos.astype(jnp.float32)[:, None] * frequency[None, :]
    cosine_table = jnp.cos(angles)[:, None, :]
    sine_table = jnp.sin(angles)[:, None, :]
    first_half = normed[..., :half_width]
    second_half = normed[..., half_width:]
    return jnp.concatenate(
        [
            first_half * cosine_table - second_half * sine_table,
            second_half * cosine_table + first_half * sine_table,
        ],
        axis=-1,
    )


def shards(inputs, q_proj, k_proj, v_proj, d_attn, positions, windows, q_gain, k_gain, weight):
    tok_rows = inputs.shape[1]
    head_width = q_gain.shape[0]
    query_heads = q_proj.shape[2] // head_width
    key_heads = k_proj.shape[2] // head_width
    group_size = query_heads // key_heads
    token_pos = positions[0]
    window = windows[0]
    dp_count = lax.axis_size("dp")
    model_width = inputs.shape[2]
    input_parts = inputs[0].reshape(tok_rows, dp_count, model_width // dp_count).transpose(1, 0, 2)
    def query_side(projected_rows, gain_vector):
        return rotated_unit(projected_rows, gain_vector, token_pos, query_heads)

    def key_side(projected_rows, gain_vector):
        return rotated_unit(projected_rows, gain_vector, token_pos, key_heads)

    q_full, query_back = jax.vjp(query_side, q_proj[0].astype(jnp.float32), q_gain)
    k_full, key_back = jax.vjp(key_side, k_proj[0].astype(jnp.float32), k_gain)
    query_rotated = q_full.astype(jnp.bfloat16).reshape(tok_rows, key_heads, group_size, head_width)
    key_rotated = k_full.astype(jnp.bfloat16)
    v_own = v_proj[0].reshape(tok_rows, key_heads, head_width)
    reach_count = min(REACH, lax.axis_size("ctx") - 1)
    own_pair = jnp.stack([key_rotated, v_own])
    input_cols, far_pairs = exchanged(input_parts, own_pair, reach_count)
    known = jnp.arange(1, reach_count + 1) <= lax.axis_index("ctx")
    far_pairs = jnp.where(known[:, None, None, None, None], far_pairs, 0)
    all_keys = jnp.concatenate([key_rotated[None], far_pairs[:, 0]])
    all_values = jnp.concatenate([v_own[None], far_pairs[:, 1]])
    block_ids = jnp.arange(reach_count + 1, dtype=jnp.int32)
    offsets = jnp.arange(tok_rows, dtype=jnp.int32)
    distance = block_ids[None, :, None] * tok_rows + offsets[:, None, None] - offsets[None, None, :]
    allowed = (distance >= 0) & (distance < window) & (distance <= token_pos[:, None, None])
    scores = (
        jnp.einsum("ahgd,bchd->hgabc", query_rotated, all_keys, preferred_element_type=jnp.float32)
        * score_scale
    )
    scores = jnp.where(allowed, scores, -jnp.inf)
    row_max = jnp.max(scores, axis=(3, 4), keepdims=True)
    exponent = jnp.exp(scores - row_max)
    probs = exponent / jnp.sum(exponent, axis=(3, 4), keepdims=True)
    head_gradient = d_attn[0].reshape(tok_rows, key_heads, group_size, head_width)
    dprobs = jnp.einsum(
        "ahgd,bchd->hgabc", head_gradient, all_values, preferred_element_type=jnp.float32
    )
    delta = jnp.sum(probs * dprobs, axis=(3, 4), keepdims=True)
    dscores = (probs * (dprobs - delta)).astype(jnp.bfloat16)
    probs_low = probs.astype(jnp.bfloat16)
    dq_rot = (
        jnp.einsum("hgabc,bchd->ahgd", dscores, all_keys, preferred_element_type=jnp.float32)
        * score_scale
    )
    dk_blocks = (
        jnp.einsum("hgabc,ahgd->bchd", dscores, query_rotated, preferred_element_type=jnp.float32)
        * score_scale
    )
    dv_blocks = jnp.einsum(
        "hgabc,ahgd->bchd", probs_low, head_gradient, preferred_element_type=jnp.float32
    )
    dq_proj, dq_gain = query_back(dq_rot.reshape(tok_rows, query_heads, head_width))
    pair_total = jnp.stack([dk_blocks[0], dv_blocks[0]])
    for distance_steps in range(1, reach_count + 1):
        far_pair = jnp.stack([dk_blocks[distance_steps], dv_blocks[distance_steps]])
        back_pair = from_behind(far_pair.astype(jnp.bfloat16), "ctx", -distance_steps)
        pair_total = pair_total + back_pair.astype(jnp.float32)
    dk_proj, dk_gain = key_back(pair_total[0])
    dv_proj = pair_total[1].reshape(tok_rows, key_heads * head_width)
    d_own = jnp.concatenate([dq_proj, dk_proj, dv_proj], axis=-1).astype(jnp.bfloat16)
    gains = jnp.pad(jnp.stack([dq_gain, dk_gain]), ((0, 6), (0, 0)))
    d_parts, d_weight_t, gain_sums = projected(d_own, weight, input_cols, gains)
    dq_gain_all, dk_gain_all = gain_sums[0], gain_sums[1]
    d_inputs = d_parts.transpose(1, 0, 2).reshape(1, tok_rows, model_width)
    return (d_inputs, d_weight_t, dq_gain_all, dk_gain_all)


def walk_code(line, place):
    far = 2 * (place + 1 - 2 * (place % 2)) + 1
    digits = []
    for step in range(line + 1):
        if step == 0:
            digits.append(2 * place)
            continue
        for other in (place - step, place + step):
            if 0 <= other < line:
                digits.append(2 * other)
        for other in (place - step + 1, place + step - 1):
            if 0 <= other < line and 2 * other + 1 not in digits + [far]:
                digits.append(2 * other + 1)
    digits.append(far)
    code = 0
    for digit in reversed(digits):
        code = code * 2 * line + digit
    return code


def unit_rows(values):
    inverse = lax.rsqrt(jnp.sum(values * values, axis=-1, keepdims=True) * (1.0 / values.shape[-1]) + norm_eps)
    return values * inverse, inverse


def turned(values, cosine, sine):
    return values * cosine + pltpu.roll(values, values.shape[-1] // 2, 1) * sine


def turned_back(values, cosine, sine):
    return values * cosine + pltpu.roll(values * sine, values.shape[-1] // 2, 1)


def norm_back(unit, inverse, gain, grad):
    scaled = grad * gain
    inner = jnp.sum(unit * scaled, axis=-1, keepdims=True) * (1.0 / unit.shape[-1])
    return inverse * (scaled - unit * inner)


def folded(values):
    return jnp.sum(values.reshape(values.shape[0] // 8, 8, values.shape[1]), axis=0)


def layer_kernel(
    n_dp, n_ctx, part,
    in_ref, q_ref, k_ref, v_ref, da_ref, pos_ref, win_ref, qgain_ref, kgain_ref, freq_ref, w_ref,
    ret_in, dw_in, gain_out,
    qs, ks, vs, ds, pos_own, pos_all, cos_t, sin_t, low_t, qrot, dstack, krot, dk_acc, dv_acc,
    blocks, wext, cols, acc, prod, keep, core_out, core_in, y_out, y_in, ret_out,
    gain_acc, gain_own, gain_rows, gain_col, gain_cols, dw_out,
    loc_a, loc_w, loc_x, send_p, recv_p, send_a, recv_a, send_x, recv_x, send_xy, recv_xy,
    send_xc, recv_xc, send_xf, recv_xf, send_g, recv_g, send_c, recv_c, send_y, recv_y, send_r, recv_r,
    send_n, recv_n, send_m, recv_m, send_d, recv_d, own_d, recv_z, own_r,
):
    row = lax.axis_index("dp")
    col = lax.axis_index("ctx")
    line = n_dp // 2
    place = row // 2
    lane = lax.rem(row, 2)
    twin = row + 1 - 2 * lane
    near = place + 1 - 2 * lax.rem(place, 2)
    head = qgain_ref.shape[1]
    toks = in_ref.shape[0]
    wide = cols.shape[2]
    peers = range(1, n_ctx)
    key_base = q_ref.shape[1]
    value_base = key_base + k_ref.shape[1]
    groups = qs.shape[0]
    pair = qs.shape[2]
    unit = blocks.shape[3]

    barrier = pltpu.get_barrier_semaphore()
    for step in range(1, n_dp):
        pl.semaphore_signal(barrier, 1, device_id={"dp": lax.rem(row + step, n_dp)}, device_id_type=MESH)
    for step in peers:
        pl.semaphore_signal(barrier, 1, device_id={"ctx": flipped(col, step)}, device_id_type=MESH)

    first_tile = row * part // head
    shift = row * part - first_tile * head
    wext[...] = jnp.zeros_like(wext)
    shifted = pl.ds(pl.multiple_of(shift, 32), part)

    def weight_copies(g):
        sources = (
            ((2 * groups * col + 2 * g) * head, 0, 2 * head),
            (key_base + (groups * col + g) * head, 2 * head, head),
            (value_base + (groups * col + g) * head, 3 * head, head),
        )
        return [
            pltpu.make_async_copy(
                w_ref.at[:, pl.ds(pl.multiple_of(start, head), size)],
                wext.at[g, shifted, pl.ds(at, size)],
                loc_w.at[g, n],
            )
            for n, (start, at, size) in enumerate(sources)
        ]

    pos_own[...] = jnp.broadcast_to(pos_ref[...].astype(jnp.float32), pos_own.shape)
    pos_all[col] = pos_own[...]
    own_rows = pl.ds(pl.multiple_of(col * toks, toks), toks)

    def piece(target, g, source_col):
        at = pl.ds(pl.multiple_of(source_col * toks, toks), toks)
        wide_at = pl.ds(pl.multiple_of((groups * target + g) * pair, pair), pair)
        thin_at = pl.ds(pl.multiple_of((groups * target + g) * head, head), head)
        return (
            (q_ref.at[:, wide_at], qs.at[g, at, :]),
            (k_ref.at[:, thin_at], ks.at[g, at, :]),
            (v_ref.at[:, thin_at], vs.at[g, at, :]),
            (da_ref.at[:, wide_at], ds.at[g, at, :]),
        )

    def head_copies(step, g, receiving=False):
        peer = flipped(col, step)
        return [
            remote(source, target, send_a.at[step, g, n], recv_a.at[step, g, n], "ctx", peer)
            for n, (source, target) in enumerate(piece(peer, g, peer if receiving else col))
        ]

    def own_copies(g):
        return [
            pltpu.make_async_copy(source, target, loc_a.at[g, n])
            for n, (source, target) in enumerate(piece(col, g, col))
        ]

    def pos_copy(step, source_col):
        return remote(pos_own, pos_all.at[source_col], send_p.at[step], recv_p.at[step], "ctx", flipped(col, step))

    for copy in own_copies(0):
        copy.start()
    pl.semaphore_wait(barrier, n_dp + n_ctx - 2)
    for step in peers:
        pos_copy(step, col).start()
    for g in range(groups):
        for step in reversed(peers):
            for copy in head_copies(step, g):
                copy.start()
    for g in range(1, groups):
        for copy in own_copies(g):
            copy.start()

    def slab(index):
        start = index * part // head
        return pl.ds(pl.multiple_of(start * head, head), wide)

    def col_send(peer):
        return remote(in_ref.at[:, slab(peer)], cols.at[row, own_rows, :], send_x.at[peer], recv_x.at[row], "dp", peer)

    def col_recv(source):
        return remote(in_ref.at[:, slab(row)], cols.at[source, own_rows, :], send_x.at[source], recv_x.at[source], "dp", source)

    code = walk_code(line, 0)
    for other in range(1, line):
        code = jnp.where(place == other, walk_code(line, other), code)

    def member(digit):
        flag = lax.rem(digit, 2)
        return digit - flag + lane + flag * (1 - 2 * lane)

    def rows_of(step):
        return pl.ds(pl.multiple_of(flipped(col, step) * toks, toks), toks)

    def cols_out(block, step, sends, recvs, receiving=False, rows=0):
        at = rows_of((rows ^ step) if receiving else rows)
        return remote(
            cols.at[block, at, :], cols.at[block, at, :], sends.at[block], recvs.at[block], "ctx", flipped(col, step)
        )

    def spread(block):
        pl.when(block != row)(lambda: col_recv(block).wait_recv())
        pl.when(block == row)(own_cols.wait)
        cols_out(block, 2, send_xy, recv_xy).start()
        cols_out(block, 1, send_xc, recv_xc).start()

    own_cols = pltpu.make_async_copy(in_ref.at[:, slab(row)], cols.at[row, own_rows, :], loc_x)
    own_cols.start()

    def send_cols(step, rest):
        col_send(member(lax.rem(rest, n_dp))).start()
        return rest // n_dp

    lax.fori_loop(1, n_dp, send_cols, code // n_dp)
    for g in range(groups):
        for copy in weight_copies(g):
            copy.start()
    gain_acc[...] = jnp.zeros_like(gain_acc)
    acc[...] = jnp.zeros_like(acc)
    spread(row)

    for step in peers:
        pos_copy(step, flipped(col, step)).wait_recv()

    @pl.loop(0, n_ctx)
    def _(block):
        rows = pl.ds(pl.multiple_of(block * toks, toks), toks)
        place_rows = jnp.broadcast_to(pos_all[block][0:1, :], (toks, toks)).T
        angle = place_rows * freq_ref[...]
        side = lax.broadcasted_iota(jnp.int32, (toks, head), 1)
        cos_t[rows, :] = jnp.cos(angle)
        sine = jnp.sin(angle)
        sin_t[rows, :] = jnp.where(side < head // 2, -sine, sine)
        index = lax.broadcasted_iota(jnp.int32, (toks, head), 0) + block * toks
        low_t[rows, :] = index - jnp.minimum(win_ref[0] - 1, place_rows.astype(jnp.int32))

    def relay(block, g, way, target):
        return remote(blocks.at[block, g], blocks.at[block, g], send_g.at[way, block, g], recv_g.at[block, g], "dp", target)

    @pl.loop(0, groups)
    def _(g):
        for step in reversed(peers):
            for copy in head_copies(step, g, True):
                copy.wait_recv()
        for copy in own_copies(g):
            copy.wait()

        @pl.loop(0, n_ctx)
        def _(block):
            rows = pl.ds(pl.multiple_of(block * toks, toks), toks)
            cosine, sine = cos_t[rows, :], sin_t[rows, :]
            key_unit, _ = unit_rows(ks[g, rows, :].astype(jnp.float32))
            krot[rows, :] = turned(key_unit * kgain_ref[...], cosine, sine).astype(krot.dtype)
            for h in range(2):
                span = slice(h * head, (h + 1) * head)
                at = slice(h * toks, (h + 1) * toks)
                query_unit, _ = unit_rows(qs[g, rows, span].astype(jnp.float32))
                qrot[block, at, :] = turned(query_unit * qgain_ref[...], cosine, sine).astype(qrot.dtype)
                dstack[block, at, :] = ds[g, rows, span]

        dk_acc[...] = jnp.zeros_like(dk_acc)
        dv_acc[...] = jnp.zeros_like(dv_acc)
        for block in range(n_ctx):
            count = (block + 1) * toks
            rows = slice(block * toks, (block + 1) * toks)
            query, grad = qrot[block], dstack[block]
            keys, values = krot[:count, :], vs[g, :count, :]
            contract_last = (((1,), (1,)), ((), ()))
            contract_first = (((0,), (0,)), ((), ()))
            scores = lax.dot_general(query, keys, contract_last, preferred_element_type=jnp.float32) * score_scale
            key_at = lax.broadcasted_iota(jnp.int32, scores.shape, 1)
            query_at = lax.rem(lax.broadcasted_iota(jnp.int32, scores.shape, 0), toks) + block * toks
            low = jnp.concatenate([low_t[rows, :]] * 2, axis=0)
            low = jnp.concatenate([low] * (block + 1), axis=1)
            scores = jnp.where((key_at >= low) & (key_at <= query_at), scores, -jnp.inf)
            exponent = jnp.exp(scores - jnp.max(scores, axis=-1, keepdims=True))
            probs = exponent * (1.0 / jnp.sum(exponent, axis=-1, keepdims=True))
            dprobs = lax.dot_general(grad, values, contract_last, preferred_element_type=jnp.float32)
            delta = jnp.sum(probs * dprobs, axis=-1, keepdims=True)
            dscores = (probs * (dprobs - delta)).astype(jnp.bfloat16)
            dquery = (
                lax.dot_general(dscores, keys, (((1,), (0,)), ((), ())), preferred_element_type=jnp.float32)
                * score_scale
            )
            dk_acc[:count, :] += lax.dot_general(dscores, query, contract_first, preferred_element_type=jnp.float32)
            dv_acc[:count, :] += lax.dot_general(
                probs.astype(jnp.bfloat16), grad, contract_first, preferred_element_type=jnp.float32
            )
            cosine, sine = cos_t[rows, :], sin_t[rows, :]
            for h in range(2):
                span = slice(h * head, (h + 1) * head)
                query_unit, inverse = unit_rows(qs[g, rows, span].astype(jnp.float32))
                back = turned_back(dquery[h * toks:(h + 1) * toks, :], cosine, sine)
                gain_acc[0] += folded(back * query_unit)
                blocks[row, g, rows, span] = norm_back(query_unit, inverse, qgain_ref[...], back).astype(blocks.dtype)

        @pl.loop(0, n_ctx)
        def _(block):
            rows = pl.ds(pl.multiple_of(block * toks, toks), toks)
            key_unit, inverse = unit_rows(ks[g, rows, :].astype(jnp.float32))
            back = turned_back(dk_acc[rows, :] * score_scale, cos_t[rows, :], sin_t[rows, :])
            gain_acc[1] += folded(back * key_unit)
            blocks[row, g, rows, 2 * head:3 * head] = norm_back(
                key_unit, inverse, kgain_ref[...], back
            ).astype(blocks.dtype)
            blocks[row, g, rows, 3 * head:4 * head] = dv_acc[rows, :].astype(blocks.dtype)

        relay(row, g, 2, twin).start()
        pl.when(place < line - 1)(lambda: relay(row, g, 0, row + 2).start())
        pl.when(place > 0)(lambda: relay(row, g, 1, row - 2).start())

    gain_own[...] = jnp.zeros_like(gain_own)
    gain_own[0:1, :] = jnp.sum(gain_acc[0], axis=0, keepdims=True)
    gain_own[1:2, :] = jnp.sum(gain_acc[1], axis=0, keepdims=True)
    gain_rows[row] = gain_own[...]

    def gain_to(peer, source):
        return remote(gain_own, gain_rows.at[source], send_n.at[peer], recv_n.at[source], "dp", peer)

    def gain_across(step, source_col):
        return remote(gain_col, gain_cols.at[source_col], send_m.at[step], recv_m.at[step], "ctx", flipped(col, step))

    for step in range(1, n_dp):
        gain_to(lax.rem(row + step, n_dp), row).start()

    for g in range(groups):
        for copy in weight_copies(g):
            copy.wait()

    def core_copy(block):
        return remote(core_out.at[block], core_in.at[block], send_c.at[block], recv_c.at[block], "ctx", flipped(col, 1))

    def y_copy(block):
        return remote(y_out.at[block], y_in.at[block], send_y.at[block], recv_y.at[block], "ctx", flipped(col, 2))

    def back_send(block):
        return remote(ret_out.at[block], ret_in.at[row], send_r.at[block], recv_r.at[row], "dp", block)

    def own_back():
        return pltpu.make_async_copy(ret_out.at[row], ret_in.at[row], own_r)

    def back_recv(source):
        return remote(ret_out.at[source], ret_in.at[source], send_r.at[source], recv_r.at[source], "dp", source)

    tile = 256

    cut = blocks.shape[2] // 8 * 4
    last_group = groups - 1

    def most(block, target):
        ref = blocks.at[block, last_group, pl.ds(0, cut), :]
        return remote(ref, ref, send_g.at[2, block, last_group], recv_g.at[block, last_group], "dp", target)

    def remainder(block, target):
        ref = blocks.at[block, last_group, pl.ds(cut, blocks.shape[2] - cut), :]
        return remote(ref, ref, send_g.at[3, block, last_group], recv_z, "dp", target)

    def take(k, block, digit):
        zone = digit // 2
        flag = lax.rem(digit, 2)
        for g in range(groups):
            if g < groups - 1:
                pl.when(block != row)(lambda: relay(block, g, 2, twin).wait_recv())
            else:
                pl.when((block != row) & ((flag == 0) | (zone != near)))(lambda: relay(block, g, 2, twin).wait_recv())

                @pl.when((flag == 1) & (zone == near))
                def _():
                    most(block, twin).wait_recv()
                    remainder(block, twin).wait_recv()

            @pl.when((flag == 0) & (zone < place) & (place < line - 1))
            def _():
                relay(block, g, 0, row + 2).start()

            @pl.when((flag == 0) & (zone > place) & (place > 0))
            def _():
                relay(block, g, 1, row - 2).start()

            if g < groups - 1:
                pl.when((flag == 0) & (zone != place))(lambda: relay(block, g, 2, twin).start())
            else:
                pl.when((flag == 0) & (zone != place) & (zone != near))(lambda: relay(block, g, 2, twin).start())
                pl.when((flag == 0) & (zone == near))(lambda: most(block, twin).start())

        @pl.when(k == line + 1)
        def _():
            remainder(twin, 2 * near + lane).start()

        @pl.loop(0, wide // tile)
        def _(n):
            span = pl.ds(pl.multiple_of(n * tile, tile), tile)
            total = None
            for g in range(groups):
                term = lax.dot_general(
                    blocks[block, g], wext[g, span, :], (((1,), (1,)), ((), ())), preferred_element_type=jnp.float32
                )
                total = term if total is None else total + term
            prod[:, span] = total

        core_out[block, 0] = prod[rows_of(1), :].astype(core_out.dtype)
        core_out[block, 1] = prod[rows_of(3), :].astype(core_out.dtype)
        core_copy(block).start()

    def cross_core(block):
        core_copy(block).wait_recv()
        y_out[block] = (prod[rows_of(2), :] + core_in[block, 1].astype(jnp.float32)).astype(y_out.dtype)
        y_copy(block).start()
        keep[block] = prod[rows_of(0), :] + core_in[block, 0].astype(jnp.float32)

    def cross_y(block):
        y_copy(block).wait_recv()
        ret_out[block] = (keep[block] + y_in[block].astype(jnp.float32)).astype(ret_out.dtype)
        pl.when(block != row)(lambda: back_send(block).start())
        pl.when(block == row)(lambda: own_back().start())

    def weigh(block):
        cols_out(block, 1, send_xc, recv_xc, True).wait_recv()
        cols_out(block, 1, send_xf, recv_xf, True, 2).wait_recv()

        @pl.loop(0, groups * (wide // tile))
        def _(n):
            g = n // (wide // tile)
            span = pl.ds(pl.multiple_of(lax.rem(n, wide // tile) * tile, tile), tile)
            at = pl.ds(pl.multiple_of(g * unit, unit), unit)
            acc[span, at] += lax.dot_general(
                cols[block, :, span], blocks[block, g], (((0,), (0,)), ((), ())),
                preferred_element_type=jnp.float32,
            )

    def pass_on(block):
        cols_out(block, 2, send_xy, recv_xy, True).wait_recv()
        cols_out(block, 1, send_xf, recv_xf, False, 2).start()

    def advance(needed, rest, action):
        pl.when(needed)(lambda: action(member(lax.rem(rest, n_dp))))
        return jnp.where(needed, rest // n_dp, rest)

    def walk(k, carry):
        rest, spreads, passes, weighs, crosses, _ = carry
        digit = lax.rem(rest, n_dp)
        block = member(digit)
        take(k, block, digit)
        for needed in (k <= 1, k <= 1, k <= 1, k == 1):
            spreads = advance(needed, spreads, spread)
        for _ in range(2):
            passes = advance((k >= 1) & (k <= 4), passes, pass_on)
        for needed in (k >= 3, (k >= 3) & (k <= 5)):
            weighs = advance(needed, weighs, weigh)
        cross_core(block)
        for needed in (k >= 3, (k == 3) | (k == 5)):
            crosses = advance(needed, crosses, cross_y)

        @pl.when(k == 2)
        def _():
            for step in range(1, n_dp):
                source = lax.rem(row + step, n_dp)
                gain_to(source, source).wait_recv()
            total = gain_rows[0]
            for other in range(1, n_dp):
                total = total + gain_rows[other]
            gain_col[...] = total
            gain_cols[col] = total
            for step in peers:
                gain_across(step, col).start()

        return rest // n_dp, spreads, passes, weighs, crosses, block

    last = lax.fori_loop(0, n_dp, walk, (code, code // n_dp, code, code, code, row))[-1]

    def plans(source):
        k_target, v_target = n_ctx // 2, n_ctx // 2 + 1
        return (
            (0, 2 * head, source // 2, lax.rem(source, 2) * groups * 2 * head),
            (2 * head, head, k_target, groups * source * head),
            (3 * head, head, v_target, groups * source * head),
        )

    def share(g, source, plan, peer, receiving=False):
        start, size, target, at = plan
        here = dw_out.at[shifted, pl.ds(pl.multiple_of(g * unit + start, head), size)]
        there = dw_in.at[:, pl.ds(pl.multiple_of(at + g * size, head), size)]
        if peer is None:
            return pltpu.make_async_copy(here, there, own_d.at[g])
        return remote(here, there, send_d.at[g, start // head], recv_d.at[source, g], "ctx", peer)

    @pl.loop(0, groups)
    def _(g):
        at = pl.ds(pl.multiple_of(g * unit, unit), unit)
        dw_out[:, at] = acc[:, at].astype(dw_out.dtype)
        for plan in plans(col):
            pl.when(plan[2] != col)(lambda: share(g, col, plan, plan[2]).start())
            pl.when(plan[2] == col)(lambda: share(g, col, plan, None).start())

    cross_y(last)

    for step in peers:
        gain_across(step, flipped(col, step)).wait_recv()
    gain_total = gain_cols[0]
    for other in range(1, n_ctx):
        gain_total = gain_total + gain_cols[other]
    gain_out[...] = gain_total

    for step in range(1, n_dp):
        back_recv(lax.rem(row + step, n_dp)).wait_recv()
    own_back().wait()

    for step in range(n_ctx):
        source = flipped(col, step)
        for plan in plans(source):
            for g in range(groups):
                if step:
                    pl.when(plan[2] == col)(lambda: share(g, source, plan, source).wait_recv())
                else:
                    pl.when(plan[2] == col)(lambda: share(g, source, plan, None).wait())

    for step in peers:
        pos_copy(step, col).wait_send()
        gain_across(step, col).wait_send()
        for g in range(groups):
            for copy in head_copies(step, g):
                copy.wait_send()
    for plan in plans(col):
        for g in range(groups):
            pl.when(plan[2] != col)(lambda: share(g, col, plan, plan[2]).wait_send())

    @pl.loop(1, n_dp)
    def _(step):
        peer = lax.rem(row + step, n_dp)
        col_send(peer).wait_send()
        gain_to(peer, row).wait_send()
        back_send(peer).wait_send()

    @pl.loop(0, n_dp)
    def _(block):
        cols_out(block, 2, send_xy, recv_xy).wait_send()
        cols_out(block, 1, send_xc, recv_xc).wait_send()
        cols_out(block, 1, send_xf, recv_xf, False, 2).wait_send()
        core_copy(block).wait_send()
        y_copy(block).wait_send()
        zone = block // 2

        @pl.when(lax.rem(block, 2) == lane)
        def _():
            for g in range(groups):
                if g < groups - 1:
                    relay(block, g, 2, twin).wait_send()
                else:
                    pl.when(zone != near)(lambda: relay(block, g, 2, twin).wait_send())
                    pl.when(zone == near)(lambda: most(block, twin).wait_send())
                pl.when((zone <= place) & (place < line - 1))(lambda: relay(block, g, 0, row + 2).wait_send())
                pl.when((zone >= place) & (place > 0))(lambda: relay(block, g, 1, row - 2).wait_send())

    remainder(twin, 2 * near + lane).wait_send()


def layer(inputs, q_proj, k_proj, v_proj, d_attn, positions, windows, q_gain, k_gain, weight):
    n_dp, n_ctx = lax.axis_size("dp"), lax.axis_size("ctx")
    toks, model = inputs.shape
    part = weight.shape[0]
    head = q_gain.shape[0]
    groups = k_proj.shape[1] // head // n_ctx
    pair = q_proj.shape[1] // n_ctx // groups
    unit = pair + 2 * head
    length = n_ctx * toks
    wide = max(-(-(index * part % head + part) // head) for index in range(n_dp)) * head
    frequency = np.exp(np.arange(head // 2) * (-2.0 * math.log(rope_base) / head))
    frequency = jnp.asarray(np.tile(frequency, 2)[None, :], jnp.float32)
    dma = pltpu.SemaphoreType.DMA
    vmem = pl.BlockSpec(memory_space=pltpu.VMEM)
    smem = pl.BlockSpec(memory_space=pltpu.SMEM)
    anywhere = pl.BlockSpec(memory_space=pl.ANY)
    low, full = jnp.bfloat16, jnp.float32
    return pl.pallas_call(
        lambda *refs: layer_kernel(n_dp, n_ctx, part, *refs),
        out_shape=(
            jax.ShapeDtypeStruct((n_dp, toks, wide), low),
            jax.ShapeDtypeStruct((part, groups * unit), low),
            jax.ShapeDtypeStruct((8, head), full),
        ),
        in_specs=[anywhere] * 5 + [vmem, smem, vmem, vmem, vmem, anywhere],
        out_specs=(anywhere, anywhere, vmem),
        scratch_shapes=[
            pltpu.VMEM((groups, length, pair), low),
            pltpu.VMEM((groups, length, head), low),
            pltpu.VMEM((groups, length, head), low),
            pltpu.VMEM((groups, length, pair), low),
            pltpu.VMEM((8, head), full),
            pltpu.VMEM((n_ctx, 8, head), full),
            pltpu.VMEM((length, head), full),
            pltpu.VMEM((length, head), full),
            pltpu.VMEM((length, head), jnp.int32),
            pltpu.VMEM((n_ctx, 2 * toks, head), low),
            pltpu.VMEM((n_ctx, 2 * toks, head), low),
            pltpu.VMEM((length, head), low),
            pltpu.VMEM((length, head), full),
            pltpu.VMEM((length, head), full),
            pltpu.VMEM((n_dp, groups, length, unit), low),
            pltpu.VMEM((groups, wide, unit), low),
            pltpu.VMEM((n_dp, length, wide), low),
            pltpu.VMEM((wide, groups * unit), full),
            pltpu.VMEM((length, wide), full),
            pltpu.VMEM((n_dp, toks, wide), full),
            pltpu.VMEM((n_dp, 2, toks, wide), low),
            pltpu.VMEM((n_dp, 2, toks, wide), low),
            pltpu.VMEM((n_dp, toks, wide), low),
            pltpu.VMEM((n_dp, toks, wide), low),
            pltpu.VMEM((n_dp, toks, wide), low),
            pltpu.VMEM((2, 8, head), full),
            pltpu.VMEM((8, head), full),
            pltpu.VMEM((n_dp, 8, head), full),
            pltpu.VMEM((8, head), full),
            pltpu.VMEM((n_ctx, 8, head), full),
            pltpu.VMEM((wide, groups * unit), low),
            dma((groups, 4)),
            dma((groups, 3)),
            dma,
            dma((n_ctx,)),
            dma((n_ctx,)),
            dma((n_ctx, groups, 4)),
            dma((n_ctx, groups, 4)),
            dma((n_dp,)),
            dma((n_dp,)),
            dma((n_dp,)),
            dma((n_dp,)),
            dma((n_dp,)),
            dma((n_dp,)),
            dma((n_dp,)),
            dma((n_dp,)),
            dma((4, n_dp, groups)),
            dma((n_dp, groups)),
            dma((n_dp,)),
            dma((n_dp,)),
            dma((n_dp,)),
            dma((n_dp,)),
            dma((n_dp,)),
            dma((n_dp,)),
            dma((n_dp,)),
            dma((n_dp,)),
            dma((n_ctx,)),
            dma((n_ctx,)),
            dma((groups, unit // head)),
            dma((n_ctx, groups)),
            dma((groups,)),
            dma,
            dma,
        ],
        compiler_params=pltpu.CompilerParams(
            collective_id=3, has_side_effects=True, vmem_limit_bytes=58 * 1024 * 1024
        ),
        name="layer",
    )(
        inputs, q_proj, k_proj, v_proj, d_attn, positions, windows,
        q_gain[None, :], k_gain[None, :], frequency, weight,
    )


def finish_kernel(part, ret_ref, dw_ref, gain_ref, din_ref, out_ref, q_out, k_out):
    count, _, wide = ret_ref.shape
    head = gain_ref.shape[1]
    starts = [index * part // head for index in range(count)]
    pieces = wide // head
    for index in range(count):
        first = 1 if index > 0 and starts[index] < starts[index - 1] + pieces else 0
        last = pieces - 1 if index + 1 < count and starts[index + 1] < starts[index] + pieces else pieces
        base = starts[index] * head
        din_ref[:, base + first * head:base + last * head] = ret_ref[index, :, first * head:last * head]
        if last < pieces:
            both = ret_ref[index, :, last * head:].astype(jnp.float32) + ret_ref[index + 1, :, :head].astype(jnp.float32)
            din_ref[:, base + last * head:base + pieces * head] = both.astype(din_ref.dtype)
    out_ref[...] = dw_ref[...].astype(out_ref.dtype)
    q_out[...] = gain_ref[0:1, :]
    k_out[...] = gain_ref[1:2, :]


def finished(returned, weight_rows, gains, model):
    n_dp, toks, wide = returned.shape
    part, rows = weight_rows.shape
    head = gains.shape[1]
    steps = 4
    return pl.pallas_call(
        lambda *refs: finish_kernel(part, *refs),
        grid=(steps,),
        out_shape=(
            jax.ShapeDtypeStruct((toks, model), jnp.bfloat16),
            jax.ShapeDtypeStruct((part, rows), jnp.float32),
            jax.ShapeDtypeStruct((1, head), jnp.float32),
            jax.ShapeDtypeStruct((1, head), jnp.float32),
        ),
        in_specs=[
            pl.BlockSpec((n_dp, toks // steps, wide), lambda i: (0, i, 0)),
            pl.BlockSpec((part, rows // steps), lambda i: (0, i)),
            pl.BlockSpec((8, head), lambda i: (0, 0)),
        ],
        out_specs=(
            pl.BlockSpec((toks // steps, model), lambda i: (i, 0)),
            pl.BlockSpec((part, rows // steps), lambda i: (0, i)),
            pl.BlockSpec((1, head), lambda i: (0, 0)),
            pl.BlockSpec((1, head), lambda i: (0, 0)),
        ),
        compiler_params=pltpu.CompilerParams(vmem_limit_bytes=58 * 1024 * 1024),
        name="finish",
    )(returned, weight_rows, gains)


def head_shards(inputs, q_proj, k_proj, v_proj, d_attn, positions, windows, q_gain, k_gain, weight):
    returned, weight_rows, gains = layer(
        inputs[0], q_proj[0], k_proj[0], v_proj[0], d_attn[0], positions, windows, q_gain, k_gain, weight
    )
    d_inputs, d_weight, dq_gain, dk_gain = finished(returned, weight_rows, gains, inputs.shape[2])
    return (d_inputs[None], d_weight.T, dq_gain[0], dk_gain[0])


def by_heads(mesh):
    return mesh.shape["dp"] == 8 and mesh.shape["ctx"] == 4


def solution(mesh):
    placed = (
        P("dp", "ctx", None),
        P("dp", "ctx", None),
        P("dp", "ctx", None),
        P("dp", "ctx", None),
        P("dp", "ctx", None),
        P("dp", "ctx"),
        P("dp"),
        P(),
        P(),
        P("dp", None),
    )
    return jax.shard_map(
        head_shards if by_heads(mesh) else shards,
        mesh=mesh,
        in_specs=placed,
        out_specs=(P("dp", "ctx", None), P("ctx", "dp"), P(), P()),
        check_vma=False,
    )
```

```python
import math

import jax
import jax.numpy as jnp
import numpy as np
from jax import lax
from jax.experimental import pallas as pl
from jax.experimental.pallas import tpu as pltpu
from jax.sharding import PartitionSpec as P

MESH = pl.DeviceIdType.MESH

REACH = 8


score_scale = 168.0 ** (-0.5)
rope_base = 10000.0
norm_eps = 1e-06


def from_behind(value, axis, steps):
    count = lax.axis_size(axis)
    initial, last = (max(0, -steps), min(count, count - steps))
    return lax.ppermute(value, axis, [(source, source + steps) for source in range(initial, last)])


def swapped(value, axis, bit):
    count = lax.axis_size(axis)
    return lax.ppermute(value, axis, [(source, source ^ bit) for source in range(count)])


def flipped(index, bits):
    bit = 1
    while bit <= bits:
        if bits & bit:
            index = index + bit - 2 * bit * (lax.rem(index // bit, 2))
        bit *= 2
    return index


def remote(source, target, send_sem, recv_sem, axis, index):
    return pltpu.make_async_remote_copy(
        src_ref=source,
        dst_ref=target,
        send_sem=send_sem,
        recv_sem=recv_sem,
        device_id={axis: index},
        device_id_type=MESH,
    )


def exchange_kernel(n_dp, n_ctx, reach, parts_ref, pair_ref, cols_ref, far_ref, own_sem, send_a, recv_a, send_b, recv_b):
    row = lax.axis_index("dp")
    col = lax.axis_index("ctx")
    barrier = pltpu.get_barrier_semaphore()
    for step in range(1, n_dp):
        pl.semaphore_signal(barrier, 1, device_id={"dp": lax.rem(row + step, n_dp)}, device_id_type=MESH)
    for step in range(1, n_ctx):
        pl.semaphore_signal(barrier, 1, device_id={"ctx": lax.rem(col + step, n_ctx)}, device_id_type=MESH)
    pl.semaphore_wait(barrier, n_dp + n_ctx - 2)
    for step in range(1, reach + 1):
        copy = remote(pair_ref, far_ref.at[step - 1], send_b.at[step], recv_b.at[step], "ctx", lax.rem(col + step, n_ctx))
        pl.when(col + step < n_ctx)(copy.start)
    own = pltpu.make_async_copy(parts_ref.at[row], cols_ref.at[row], own_sem)
    own.start()
    sends = []
    for step in range(1, n_dp):
        peer = lax.rem(row + step, n_dp)
        copy = remote(parts_ref.at[peer], cols_ref.at[row], send_a.at[step], recv_a.at[step], "dp", peer)
        copy.start()
        sends.append(copy)
    own.wait()
    for step in range(1, n_dp):
        source = lax.rem(row + n_dp - step, n_dp)
        remote(parts_ref.at[source], cols_ref.at[source], send_a.at[step], recv_a.at[step], "dp", source).wait_recv()
        sends[step - 1].wait_send()
    for step in range(1, reach + 1):
        copy = remote(pair_ref, far_ref.at[step - 1], send_b.at[step], recv_b.at[step], "ctx", lax.rem(col + step, n_ctx))
        pl.when(col + step < n_ctx)(copy.wait_send)
        pl.when(col >= step)(copy.wait_recv)


def exchanged(parts, pair, reach):
    n_dp, n_ctx = lax.axis_size("dp"), lax.axis_size("ctx")
    anywhere = pl.BlockSpec(memory_space=pl.ANY)
    dma = pltpu.SemaphoreType.DMA
    return pl.pallas_call(
        lambda *refs: exchange_kernel(n_dp, n_ctx, reach, *refs),
        out_shape=(
            jax.ShapeDtypeStruct(parts.shape, parts.dtype),
            jax.ShapeDtypeStruct((reach,) + pair.shape, pair.dtype),
        ),
        in_specs=[anywhere, anywhere],
        out_specs=(anywhere, anywhere),
        scratch_shapes=[dma, dma((n_dp,)), dma((n_dp,)), dma((reach + 1,)), dma((reach + 1,))],
        compiler_params=pltpu.CompilerParams(collective_id=1, has_side_effects=True),
        name="exchange",
    )(parts, pair)


def project_kernel(
    n_dp, n_ctx, d_ref, w_ref, cols_ref, gain_ref, back_ref, sum_ref, gain_out,
    blocks, acc, outbox, terms, got, gain_rows, gain_sent, gain_got,
    own_sem, send_g, recv_g, send_o, recv_o, send_w, recv_w, send_r, recv_r, send_c, recv_c,
):
    row = lax.axis_index("dp")
    col = lax.axis_index("ctx")
    line = n_dp // 2
    place = row // 2
    lane = lax.rem(row, 2)
    twin = 1 - 2 * lane
    width = w_ref.shape[1]
    bits = [1 << k for k in range(n_ctx.bit_length() - 1)]
    barrier = pltpu.get_barrier_semaphore()
    for step in range(1, n_dp):
        pl.semaphore_signal(barrier, 1, device_id={"dp": lax.rem(row + step, n_dp)}, device_id_type=MESH)
    for bit in bits:
        pl.semaphore_signal(barrier, 1, device_id={"ctx": flipped(col, bit)}, device_id_type=MESH)
    pl.semaphore_wait(barrier, n_dp - 1 + len(bits))

    def relay(block, way, target):
        return remote(blocks.at[block], blocks.at[block], send_g.at[way, block], recv_g.at[block], "dp", target)

    def arrived(block):
        relay(block, 0, lax.rem(row + 1, n_dp)).wait_recv()

    def back(block, target):
        return remote(outbox.at[block], back_ref.at[row], send_o.at[block], recv_o.at[row], "dp", target)

    def product(block):
        acc[...] = jnp.zeros_like(acc)
        depth = 2048

        @pl.loop(0, width // depth)
        def _(k):
            span = pl.ds(pl.multiple_of(k * depth, depth), depth)
            acc[...] += lax.dot_general(
                blocks[block, :, span], w_ref[:, span], (((1,), (1,)), ((), ())),
                preferred_element_type=jnp.float32,
            )

        outbox[block] = acc[...].astype(outbox.dtype)

    def answer(block):
        product(block)
        back(block, block).start()

    blocks[row] = d_ref[...]
    pl.when(place < line - 1)(lambda: relay(row, 0, row + 2).start())
    pl.when(place > 0)(lambda: relay(row, 1, row - 2).start())
    relay(row, 2, row + twin).start()

    def gain_to(peer):
        return remote(gain_ref, gain_rows.at[row], send_r.at[peer], recv_r.at[row], "dp", peer)

    gain_rows[row] = gain_ref[...]
    for step in range(1, n_dp):
        gain_to(lax.rem(row + step, n_dp)).start()
    product(row)
    own = pltpu.make_async_copy(outbox.at[row], back_ref.at[row], own_sem)
    own.start()

    @pl.loop(1, line + 1)
    def _(step):
        @pl.when(place >= step)
        def _():
            block = row - 2 * step
            arrived(block)
            pl.when(place < line - 1)(lambda: relay(block, 0, row + 2).start())
            relay(block, 2, row + twin).start()

        @pl.when(place + step < line)
        def _():
            block = row + 2 * step
            arrived(block)
            pl.when(place > 0)(lambda: relay(block, 1, row - 2).start())
            relay(block, 2, row + twin).start()

        pl.when(place >= step)(lambda: answer(row - 2 * step))
        pl.when(place + step < line)(lambda: answer(row + 2 * step))

        @pl.when(place >= step - 1)
        def _():
            block = row + twin - 2 * (step - 1)
            arrived(block)
            answer(block)

        @pl.when((step > 1) & (place + step - 1 < line))
        def _():
            block = row + twin + 2 * (step - 1)
            arrived(block)
            answer(block)

    tokens = n_dp * blocks.shape[1]
    rows = width // n_ctx
    tile = min(512, rows)

    def fill(slot):
        start = flipped(col, slot) * rows

        @pl.loop(0, rows // tile)
        def _(k):
            span = pl.ds(pl.multiple_of(start + k * tile, tile), tile)
            left = blocks[:, :, span].reshape(tokens, tile)
            right = cols_ref[...].reshape(tokens, cols_ref.shape[2])
            term = lax.dot_general(
                left, right, (((0,), (0,)), ((), ())), preferred_element_type=jnp.float32
            )
            terms[slot, pl.ds(pl.multiple_of(k * tile, tile), tile), :] = term.astype(terms.dtype)

    def share(slot):
        bit = slot & -slot
        return remote(terms.at[slot], got.at[slot], send_w.at[slot], recv_w.at[slot], "ctx", flipped(col, bit))

    def merge(slot, bit):
        share(slot + bit).wait_recv()
        if slot:
            total = terms[slot].astype(jnp.float32) + got[slot + bit].astype(jnp.float32)
            terms[slot] = total.astype(terms.dtype)
            if slot & (2 * bit):
                share(slot).start()
        else:
            held = sum_ref[...] if bit > 1 else terms[0].astype(jnp.float32)
            sum_ref[...] = held + got[bit].astype(jnp.float32)

    for slot in reversed(range(0, n_ctx, 2)):
        fill(slot + 1)
        share(slot + 1).start()
        fill(slot)
        merge(slot, 1)

    for step in range(1, n_dp):
        peer = lax.rem(row + step, n_dp)
        remote(gain_ref, gain_rows.at[peer], send_r.at[peer], recv_r.at[peer], "dp", peer).wait_recv()
    gain_total = gain_rows[0]
    for peer in range(1, n_dp):
        gain_total = gain_total + gain_rows[peer]
    for level, bit in enumerate(bits):
        gain_sent[level] = gain_total
        copy = remote(
            gain_sent.at[level], gain_got.at[level], send_c.at[level], recv_c.at[level],
            "ctx", flipped(col, bit),
        )
        copy.start()
        copy.wait()
        gain_total = gain_total + gain_got[level]
    gain_out[...] = gain_total

    for bit in bits[1:]:
        for slot in reversed(range(0, n_ctx, 2 * bit)):
            merge(slot, bit)
    for step in range(1, n_dp):
        gain_to(lax.rem(row + step, n_dp)).wait_send()
    for slot in range(1, n_ctx):
        share(slot).wait_send()
    own.wait()

    @pl.loop(1, n_dp)
    def _(step):
        source = lax.rem(row + step, n_dp)
        remote(outbox.at[source], back_ref.at[source], send_o.at[source], recv_o.at[source], "dp", source).wait_recv()
        back(source, source).wait_send()

    relay(row, 2, row + twin).wait_send()
    pl.when(place < line - 1)(lambda: relay(row, 0, row + 2).wait_send())
    pl.when(place > 0)(lambda: relay(row, 1, row - 2).wait_send())

    @pl.loop(1, line)
    def _(step):
        @pl.when(place >= step)
        def _():
            block = row - 2 * step
            pl.when(place < line - 1)(lambda: relay(block, 0, row + 2).wait_send())
            relay(block, 2, row + twin).wait_send()

        @pl.when(place + step < line)
        def _():
            block = row + 2 * step
            pl.when(place > 0)(lambda: relay(block, 1, row - 2).wait_send())
            relay(block, 2, row + twin).wait_send()


def projected(d_own, weight, cols, gains):
    n_dp, n_ctx = lax.axis_size("dp"), lax.axis_size("ctx")
    toks, width = d_own.shape
    part = weight.shape[0]
    dma = pltpu.SemaphoreType.DMA
    levels = n_ctx.bit_length() - 1
    vmem = pl.BlockSpec(memory_space=pltpu.VMEM)
    return pl.pallas_call(
        lambda *refs: project_kernel(n_dp, n_ctx, *refs),
        out_shape=(
            jax.ShapeDtypeStruct((n_dp, toks, part), jnp.bfloat16),
            jax.ShapeDtypeStruct((width // n_ctx, part), jnp.float32),
            jax.ShapeDtypeStruct(gains.shape, jnp.float32),
        ),
        in_specs=[vmem, vmem, vmem, vmem],
        out_specs=(pl.BlockSpec(memory_space=pl.ANY), vmem, vmem),
        scratch_shapes=[
            pltpu.VMEM((n_dp, toks, width), jnp.bfloat16),
            pltpu.VMEM((toks, part), jnp.float32),
            pltpu.VMEM((n_dp, toks, part), jnp.bfloat16),
            pltpu.VMEM((n_ctx, width // n_ctx, part), jnp.bfloat16),
            pltpu.VMEM((n_ctx, width // n_ctx, part), jnp.bfloat16),
            pltpu.VMEM((n_dp,) + gains.shape, jnp.float32),
            pltpu.VMEM((levels,) + gains.shape, jnp.float32),
            pltpu.VMEM((levels,) + gains.shape, jnp.float32),
            dma,
            dma((3, n_dp)),
            dma((n_dp,)),
            dma((n_dp,)),
            dma((n_dp,)),
            dma((n_ctx,)),
            dma((n_ctx,)),
            dma((n_dp,)),
            dma((n_dp,)),
            dma((levels,)),
            dma((levels,)),
        ],
        compiler_params=pltpu.CompilerParams(
            collective_id=2, has_side_effects=True, vmem_limit_bytes=56 * 1024 * 1024
        ),
        name="project",
    )(d_own, weight, cols, gains)


def rotated_unit(projected_rows, gain_vector, token_pos, head_count):
    head_width = gain_vector.shape[0]
    rows_heads = projected_rows.reshape(projected_rows.shape[0], head_count, head_width)
    inverse = lax.rsqrt(jnp.mean(rows_heads * rows_heads, axis=-1, keepdims=True) + norm_eps)
    normed = rows_heads * inverse * gain_vector
    half_width = head_width // 2
    frequency = jnp.exp(
        jnp.arange(half_width, dtype=jnp.float32) * (-2.0 * math.log(rope_base) / head_width)
    )
    angles = token_pos.astype(jnp.float32)[:, None] * frequency[None, :]
    cosine_table = jnp.cos(angles)[:, None, :]
    sine_table = jnp.sin(angles)[:, None, :]
    first_half = normed[..., :half_width]
    second_half = normed[..., half_width:]
    return jnp.concatenate(
        [
            first_half * cosine_table - second_half * sine_table,
            second_half * cosine_table + first_half * sine_table,
        ],
        axis=-1,
    )


def shards(inputs, q_proj, k_proj, v_proj, d_attn, positions, windows, q_gain, k_gain, weight):
    tok_rows = inputs.shape[1]
    head_width = q_gain.shape[0]
    query_heads = q_proj.shape[2] // head_width
    key_heads = k_proj.shape[2] // head_width
    group_size = query_heads // key_heads
    token_pos = positions[0]
    window = windows[0]
    dp_count = lax.axis_size("dp")
    model_width = inputs.shape[2]
    input_parts = inputs[0].reshape(tok_rows, dp_count, model_width // dp_count).transpose(1, 0, 2)
    def query_side(projected_rows, gain_vector):
        return rotated_unit(projected_rows, gain_vector, token_pos, query_heads)

    def key_side(projected_rows, gain_vector):
        return rotated_unit(projected_rows, gain_vector, token_pos, key_heads)

    q_full, query_back = jax.vjp(query_side, q_proj[0].astype(jnp.float32), q_gain)
    k_full, key_back = jax.vjp(key_side, k_proj[0].astype(jnp.float32), k_gain)
    query_rotated = q_full.astype(jnp.bfloat16).reshape(tok_rows, key_heads, group_size, head_width)
    key_rotated = k_full.astype(jnp.bfloat16)
    v_own = v_proj[0].reshape(tok_rows, key_heads, head_width)
    reach_count = min(REACH, lax.axis_size("ctx") - 1)
    own_pair = jnp.stack([key_rotated, v_own])
    input_cols, far_pairs = exchanged(input_parts, own_pair, reach_count)
    known = jnp.arange(1, reach_count + 1) <= lax.axis_index("ctx")
    far_pairs = jnp.where(known[:, None, None, None, None], far_pairs, 0)
    all_keys = jnp.concatenate([key_rotated[None], far_pairs[:, 0]])
    all_values = jnp.concatenate([v_own[None], far_pairs[:, 1]])
    block_ids = jnp.arange(reach_count + 1, dtype=jnp.int32)
    offsets = jnp.arange(tok_rows, dtype=jnp.int32)
    distance = block_ids[None, :, None] * tok_rows + offsets[:, None, None] - offsets[None, None, :]
    allowed = (distance >= 0) & (distance < window) & (distance <= token_pos[:, None, None])
    scores = (
        jnp.einsum("ahgd,bchd->hgabc", query_rotated, all_keys, preferred_element_type=jnp.float32)
        * score_scale
    )
    scores = jnp.where(allowed, scores, -jnp.inf)
    row_max = jnp.max(scores, axis=(3, 4), keepdims=True)
    exponent = jnp.exp(scores - row_max)
    probs = exponent / jnp.sum(exponent, axis=(3, 4), keepdims=True)
    head_gradient = d_attn[0].reshape(tok_rows, key_heads, group_size, head_width)
    dprobs = jnp.einsum(
        "ahgd,bchd->hgabc", head_gradient, all_values, preferred_element_type=jnp.float32
    )
    delta = jnp.sum(probs * dprobs, axis=(3, 4), keepdims=True)
    dscores = (probs * (dprobs - delta)).astype(jnp.bfloat16)
    probs_low = probs.astype(jnp.bfloat16)
    dq_rot = (
        jnp.einsum("hgabc,bchd->ahgd", dscores, all_keys, preferred_element_type=jnp.float32)
        * score_scale
    )
    dk_blocks = (
        jnp.einsum("hgabc,ahgd->bchd", dscores, query_rotated, preferred_element_type=jnp.float32)
        * score_scale
    )
    dv_blocks = jnp.einsum(
        "hgabc,ahgd->bchd", probs_low, head_gradient, preferred_element_type=jnp.float32
    )
    dq_proj, dq_gain = query_back(dq_rot.reshape(tok_rows, query_heads, head_width))
    pair_total = jnp.stack([dk_blocks[0], dv_blocks[0]])
    for distance_steps in range(1, reach_count + 1):
        far_pair = jnp.stack([dk_blocks[distance_steps], dv_blocks[distance_steps]])
        back_pair = from_behind(far_pair.astype(jnp.bfloat16), "ctx", -distance_steps)
        pair_total = pair_total + back_pair.astype(jnp.float32)
    dk_proj, dk_gain = key_back(pair_total[0])
    dv_proj = pair_total[1].reshape(tok_rows, key_heads * head_width)
    d_own = jnp.concatenate([dq_proj, dk_proj, dv_proj], axis=-1).astype(jnp.bfloat16)
    gains = jnp.pad(jnp.stack([dq_gain, dk_gain]), ((0, 6), (0, 0)))
    d_parts, d_weight_t, gain_sums = projected(d_own, weight, input_cols, gains)
    dq_gain_all, dk_gain_all = gain_sums[0], gain_sums[1]
    d_inputs = d_parts.transpose(1, 0, 2).reshape(1, tok_rows, model_width)
    return (d_inputs, d_weight_t, dq_gain_all, dk_gain_all)


def walk_code(line, place):
    far = 2 * (place + 1 - 2 * (place % 2)) + 1
    digits = []
    for step in range(line + 1):
        if step == 0:
            digits.append(2 * place)
            continue
        for other in (place - step, place + step):
            if 0 <= other < line:
                digits.append(2 * other)
        for other in (place - step + 1, place + step - 1):
            if 0 <= other < line and 2 * other + 1 not in digits + [far]:
                digits.append(2 * other + 1)
    digits.append(far)
    code = 0
    for digit in reversed(digits):
        code = code * 2 * line + digit
    return code


def unit_rows(values):
    inverse = lax.rsqrt(jnp.sum(values * values, axis=-1, keepdims=True) * (1.0 / values.shape[-1]) + norm_eps)
    return values * inverse, inverse


def turned(values, cosine, sine):
    return values * cosine + pltpu.roll(values, values.shape[-1] // 2, 1) * sine


def turned_back(values, cosine, sine):
    return values * cosine + pltpu.roll(values * sine, values.shape[-1] // 2, 1)


def norm_back(unit, inverse, gain, grad):
    scaled = grad * gain
    inner = jnp.sum(unit * scaled, axis=-1, keepdims=True) * (1.0 / unit.shape[-1])
    return inverse * (scaled - unit * inner)


def folded(values):
    return jnp.sum(values.reshape(values.shape[0] // 8, 8, values.shape[1]), axis=0)


def layer_kernel(
    n_dp, n_ctx, part,
    in_ref, q_ref, k_ref, v_ref, da_ref, pos_ref, win_ref, qgain_ref, kgain_ref, freq_ref, w_ref,
    ret_in, dw_in, gain_out,
    qs, ks, vs, ds, pos_own, pos_all, cos_t, sin_t, low_t, qrot, dstack, krot, dk_acc, dv_acc,
    blocks, wext, cols, acc, prod, mine, keep, core_out, core_in, y_out, y_in, ret_out,
    gain_acc, gain_own, gain_rows, gain_col, gain_cols, dw_out,
    loc_a, loc_w, loc_x, send_p, recv_p, send_a, recv_a, send_x, recv_x, send_xy, recv_xy,
    send_xc, recv_xc, send_xf, recv_xf, send_g, recv_g, send_c, recv_c, send_y, recv_y, send_r, recv_r,
    send_n, recv_n, send_m, recv_m, send_d, recv_d, own_d, recv_z, own_r,
):
    row = lax.axis_index("dp")
    col = lax.axis_index("ctx")
    line = n_dp // 2
    place = row // 2
    lane = lax.rem(row, 2)
    twin = row + 1 - 2 * lane
    near = place + 1 - 2 * lax.rem(place, 2)
    head = qgain_ref.shape[1]
    toks = in_ref.shape[0]
    wide = cols.shape[2]
    peers = range(1, n_ctx)
    key_base = q_ref.shape[1]
    value_base = key_base + k_ref.shape[1]
    groups = qs.shape[0]
    pair = qs.shape[2]
    unit = blocks.shape[3]

    barrier = pltpu.get_barrier_semaphore()
    for step in range(1, n_dp):
        pl.semaphore_signal(barrier, 1, device_id={"dp": lax.rem(row + step, n_dp)}, device_id_type=MESH)
    for step in peers:
        pl.semaphore_signal(barrier, 1, device_id={"ctx": flipped(col, step)}, device_id_type=MESH)

    first_tile = row * part // head
    shift = row * part - first_tile * head
    wext[...] = jnp.zeros_like(wext)
    shifted = pl.ds(pl.multiple_of(shift, 32), part)

    def weight_copies(g):
        sources = (
            ((2 * groups * col + 2 * g) * head, 0, 2 * head),
            (key_base + (groups * col + g) * head, 2 * head, head),
            (value_base + (groups * col + g) * head, 3 * head, head),
        )
        return [
            pltpu.make_async_copy(
                w_ref.at[:, pl.ds(pl.multiple_of(start, head), size)],
                wext.at[g, shifted, pl.ds(at, size)],
                loc_w.at[g, n],
            )
            for n, (start, at, size) in enumerate(sources)
        ]

    pos_own[...] = jnp.broadcast_to(pos_ref[...].astype(jnp.float32), pos_own.shape)
    pos_all[col] = pos_own[...]
    own_rows = pl.ds(pl.multiple_of(col * toks, toks), toks)

    def piece(target, g, source_col):
        at = pl.ds(pl.multiple_of(source_col * toks, toks), toks)
        wide_at = pl.ds(pl.multiple_of((groups * target + g) * pair, pair), pair)
        thin_at = pl.ds(pl.multiple_of((groups * target + g) * head, head), head)
        return (
            (q_ref.at[:, wide_at], qs.at[g, at, :]),
            (k_ref.at[:, thin_at], ks.at[g, at, :]),
            (v_ref.at[:, thin_at], vs.at[g, at, :]),
            (da_ref.at[:, wide_at], ds.at[g, at, :]),
        )

    def head_copies(step, g, receiving=False):
        peer = flipped(col, step)
        return [
            remote(source, target, send_a.at[step, g, n], recv_a.at[step, g, n], "ctx", peer)
            for n, (source, target) in enumerate(piece(peer, g, peer if receiving else col))
        ]

    def own_copies(g):
        return [
            pltpu.make_async_copy(source, target, loc_a.at[g, n])
            for n, (source, target) in enumerate(piece(col, g, col))
        ]

    def pos_copy(step, source_col):
        return remote(pos_own, pos_all.at[source_col], send_p.at[step], recv_p.at[step], "ctx", flipped(col, step))

    for copy in own_copies(0):
        copy.start()
    pl.semaphore_wait(barrier, n_dp + n_ctx - 2)
    for step in peers:
        pos_copy(step, col).start()
    for g in range(groups):
        for step in reversed(peers):
            for copy in head_copies(step, g):
                copy.start()
    for g in range(1, groups):
        for copy in own_copies(g):
            copy.start()

    def slab(index):
        start = index * part // head
        return pl.ds(pl.multiple_of(start * head, head), wide)

    def col_send(peer):
        return remote(in_ref.at[:, slab(peer)], cols.at[row, own_rows, :], send_x.at[peer], recv_x.at[row], "dp", peer)

    def col_recv(source):
        return remote(in_ref.at[:, slab(row)], cols.at[source, own_rows, :], send_x.at[source], recv_x.at[source], "dp", source)

    code = walk_code(line, 0)
    for other in range(1, line):
        code = jnp.where(place == other, walk_code(line, other), code)

    def member(digit):
        flag = lax.rem(digit, 2)
        return digit - flag + lane + flag * (1 - 2 * lane)

    def rows_of(step):
        return pl.ds(pl.multiple_of(flipped(col, step) * toks, toks), toks)

    def cols_out(block, step, sends, recvs, receiving=False, rows=0):
        at = rows_of((rows ^ step) if receiving else rows)
        return remote(
            cols.at[block, at, :], cols.at[block, at, :], sends.at[block], recvs.at[block], "ctx", flipped(col, step)
        )

    def spread(block):
        pl.when(block != row)(lambda: col_recv(block).wait_recv())
        pl.when(block == row)(own_cols.wait)
        cols_out(block, 2, send_xy, recv_xy).start()
        cols_out(block, 1, send_xc, recv_xc).start()

    own_cols = pltpu.make_async_copy(in_ref.at[:, slab(row)], cols.at[row, own_rows, :], loc_x)
    own_cols.start()

    def send_cols(step, rest):
        col_send(member(lax.rem(rest, n_dp))).start()
        return rest // n_dp

    lax.fori_loop(1, n_dp, send_cols, code // n_dp)
    for g in range(groups):
        for copy in weight_copies(g):
            copy.start()
    gain_acc[...] = jnp.zeros_like(gain_acc)
    acc[...] = jnp.zeros_like(acc)
    spread(row)

    for step in peers:
        pos_copy(step, flipped(col, step)).wait_recv()

    @pl.loop(0, n_ctx)
    def _(block):
        rows = pl.ds(pl.multiple_of(block * toks, toks), toks)
        place_rows = jnp.broadcast_to(pos_all[block][0:1, :], (toks, toks)).T
        angle = place_rows * freq_ref[...]
        side = lax.broadcasted_iota(jnp.int32, (toks, head), 1)
        cos_t[rows, :] = jnp.cos(angle)
        sine = jnp.sin(angle)
        sin_t[rows, :] = jnp.where(side < head // 2, -sine, sine)
        index = lax.broadcasted_iota(jnp.int32, (toks, head), 0) + block * toks
        low_t[rows, :] = index - jnp.minimum(win_ref[0] - 1, place_rows.astype(jnp.int32))

    def relay(block, g, way, target):
        return remote(blocks.at[block, g], blocks.at[block, g], send_g.at[way, block, g], recv_g.at[block, g], "dp", target)

    @pl.loop(0, groups)
    def _(g):
        for step in reversed(peers):
            for copy in head_copies(step, g, True):
                copy.wait_recv()
        for copy in own_copies(g):
            copy.wait()

        @pl.loop(0, n_ctx)
        def _(block):
            rows = pl.ds(pl.multiple_of(block * toks, toks), toks)
            cosine, sine = cos_t[rows, :], sin_t[rows, :]
            key_unit, _ = unit_rows(ks[g, rows, :].astype(jnp.float32))
            krot[rows, :] = turned(key_unit * kgain_ref[...], cosine, sine).astype(krot.dtype)
            for h in range(2):
                span = slice(h * head, (h + 1) * head)
                at = slice(h * toks, (h + 1) * toks)
                query_unit, _ = unit_rows(qs[g, rows, span].astype(jnp.float32))
                qrot[block, at, :] = turned(query_unit * qgain_ref[...], cosine, sine).astype(qrot.dtype)
                dstack[block, at, :] = ds[g, rows, span]

        dk_acc[...] = jnp.zeros_like(dk_acc)
        dv_acc[...] = jnp.zeros_like(dv_acc)
        for block in range(n_ctx):
            count = (block + 1) * toks
            rows = slice(block * toks, (block + 1) * toks)
            query, grad = qrot[block], dstack[block]
            keys, values = krot[:count, :], vs[g, :count, :]
            contract_last = (((1,), (1,)), ((), ()))
            contract_first = (((0,), (0,)), ((), ()))
            scores = lax.dot_general(query, keys, contract_last, preferred_element_type=jnp.float32) * score_scale
            key_at = lax.broadcasted_iota(jnp.int32, scores.shape, 1)
            query_at = lax.rem(lax.broadcasted_iota(jnp.int32, scores.shape, 0), toks) + block * toks
            low = jnp.concatenate([low_t[rows, :]] * 2, axis=0)
            low = jnp.concatenate([low] * (block + 1), axis=1)
            scores = jnp.where((key_at >= low) & (key_at <= query_at), scores, -jnp.inf)
            exponent = jnp.exp(scores - jnp.max(scores, axis=-1, keepdims=True))
            probs = exponent * (1.0 / jnp.sum(exponent, axis=-1, keepdims=True))
            dprobs = lax.dot_general(grad, values, contract_last, preferred_element_type=jnp.float32)
            delta = jnp.sum(probs * dprobs, axis=-1, keepdims=True)
            dscores = (probs * (dprobs - delta)).astype(jnp.bfloat16)
            dquery = (
                lax.dot_general(dscores, keys, (((1,), (0,)), ((), ())), preferred_element_type=jnp.float32)
                * score_scale
            )
            dk_acc[:count, :] += lax.dot_general(dscores, query, contract_first, preferred_element_type=jnp.float32)
            dv_acc[:count, :] += lax.dot_general(
                probs.astype(jnp.bfloat16), grad, contract_first, preferred_element_type=jnp.float32
            )
            cosine, sine = cos_t[rows, :], sin_t[rows, :]
            for h in range(2):
                span = slice(h * head, (h + 1) * head)
                query_unit, inverse = unit_rows(qs[g, rows, span].astype(jnp.float32))
                back = turned_back(dquery[h * toks:(h + 1) * toks, :], cosine, sine)
                gain_acc[0] += folded(back * query_unit)
                blocks[row, g, rows, span] = norm_back(query_unit, inverse, qgain_ref[...], back).astype(blocks.dtype)

        @pl.loop(0, n_ctx)
        def _(block):
            rows = pl.ds(pl.multiple_of(block * toks, toks), toks)
            key_unit, inverse = unit_rows(ks[g, rows, :].astype(jnp.float32))
            back = turned_back(dk_acc[rows, :] * score_scale, cos_t[rows, :], sin_t[rows, :])
            gain_acc[1] += folded(back * key_unit)
            blocks[row, g, rows, 2 * head:3 * head] = norm_back(
                key_unit, inverse, kgain_ref[...], back
            ).astype(blocks.dtype)
            blocks[row, g, rows, 3 * head:4 * head] = dv_acc[rows, :].astype(blocks.dtype)

        relay(row, g, 2, twin).start()
        pl.when(place < line - 1)(lambda: relay(row, g, 0, row + 2).start())
        pl.when(place > 0)(lambda: relay(row, g, 1, row - 2).start())

    gain_own[...] = jnp.zeros_like(gain_own)
    gain_own[0:1, :] = jnp.sum(gain_acc[0], axis=0, keepdims=True)
    gain_own[1:2, :] = jnp.sum(gain_acc[1], axis=0, keepdims=True)
    gain_rows[row] = gain_own[...]

    def gain_to(peer, source):
        return remote(gain_own, gain_rows.at[source], send_n.at[peer], recv_n.at[source], "dp", peer)

    def gain_across(step, source_col):
        return remote(gain_col, gain_cols.at[source_col], send_m.at[step], recv_m.at[step], "ctx", flipped(col, step))

    for step in range(1, n_dp):
        gain_to(lax.rem(row + step, n_dp), row).start()

    for g in range(groups):
        for copy in weight_copies(g):
            copy.wait()

    def core_copy(block):
        return remote(core_out.at[block], core_in.at[block], send_c.at[block], recv_c.at[block], "ctx", flipped(col, 1))

    def y_copy(block):
        return remote(y_out.at[block], y_in.at[block], send_y.at[block], recv_y.at[block], "ctx", flipped(col, 2))

    def back_send(block):
        return remote(ret_out.at[block], ret_in.at[row], send_r.at[block], recv_r.at[row], "dp", block)

    def own_back():
        return pltpu.make_async_copy(ret_out.at[row], ret_in.at[row], own_r)

    def back_recv(source):
        return remote(ret_out.at[source], ret_in.at[source], send_r.at[source], recv_r.at[source], "dp", source)

    tile = 256

    cut = blocks.shape[2] // 8 * 4
    last_group = groups - 1

    def most(block, target):
        ref = blocks.at[block, last_group, pl.ds(0, cut), :]
        return remote(ref, ref, send_g.at[2, block, last_group], recv_g.at[block, last_group], "dp", target)

    def remainder(block, target):
        ref = blocks.at[block, last_group, pl.ds(cut, blocks.shape[2] - cut), :]
        return remote(ref, ref, send_g.at[3, block, last_group], recv_z, "dp", target)

    def take(k, block, digit):
        zone = digit // 2
        flag = lax.rem(digit, 2)
        for g in range(groups):
            if g < groups - 1:
                pl.when(block != row)(lambda: relay(block, g, 2, twin).wait_recv())
            else:
                pl.when((block != row) & ((flag == 0) | (zone != near)))(lambda: relay(block, g, 2, twin).wait_recv())

                @pl.when((flag == 1) & (zone == near))
                def _():
                    most(block, twin).wait_recv()
                    remainder(block, twin).wait_recv()

            @pl.when((flag == 0) & (zone < place) & (place < line - 1))
            def _():
                relay(block, g, 0, row + 2).start()

            @pl.when((flag == 0) & (zone > place) & (place > 0))
            def _():
                relay(block, g, 1, row - 2).start()

            if g < groups - 1:
                pl.when((flag == 0) & (zone != place))(lambda: relay(block, g, 2, twin).start())
            else:
                pl.when((flag == 0) & (zone != place) & (zone != near))(lambda: relay(block, g, 2, twin).start())
                pl.when((flag == 0) & (zone == near))(lambda: most(block, twin).start())

        @pl.when(k == line + 1)
        def _():
            remainder(twin, 2 * near + lane).start()

        @pl.loop(0, wide // tile)
        def _(n):
            span = pl.ds(pl.multiple_of(n * tile, tile), tile)
            total = None
            for g in range(groups):
                term = lax.dot_general(
                    blocks[block, g], wext[g, span, :], (((1,), (1,)), ((), ())), preferred_element_type=jnp.float32
                )
                total = term if total is None else total + term
            prod[:, span] = total

        core_out[block, 0] = prod[rows_of(1), :].astype(core_out.dtype)
        core_out[block, 1] = prod[rows_of(3), :].astype(core_out.dtype)
        core_copy(block).start()
        keep[block] = prod[rows_of(0), :]
        mine[block] = prod[rows_of(2), :]

    def cross_core(block):
        core_copy(block).wait_recv()
        y_out[block] = (mine[block] + core_in[block, 1].astype(jnp.float32)).astype(y_out.dtype)
        y_copy(block).start()
        keep[block] += core_in[block, 0].astype(jnp.float32)

    def cross_y(block):
        y_copy(block).wait_recv()
        ret_out[block] = (keep[block] + y_in[block].astype(jnp.float32)).astype(ret_out.dtype)
        pl.when(block != row)(lambda: back_send(block).start())
        pl.when(block == row)(lambda: own_back().start())

    def weigh(block):
        cols_out(block, 1, send_xc, recv_xc, True).wait_recv()
        cols_out(block, 1, send_xf, recv_xf, True, 2).wait_recv()

        @pl.loop(0, groups * (wide // tile))
        def _(n):
            g = n // (wide // tile)
            span = pl.ds(pl.multiple_of(lax.rem(n, wide // tile) * tile, tile), tile)
            at = pl.ds(pl.multiple_of(g * unit, unit), unit)
            acc[span, at] += lax.dot_general(
                cols[block, :, span], blocks[block, g], (((0,), (0,)), ((), ())),
                preferred_element_type=jnp.float32,
            )

    def pass_on(block):
        cols_out(block, 2, send_xy, recv_xy, True).wait_recv()
        cols_out(block, 1, send_xf, recv_xf, False, 2).start()

    def repeat(counts, k, rest, action):
        count = 0
        for at, value in enumerate(counts):
            count = count + jnp.where(k == at, value, 0)

        def once(_, left):
            action(member(lax.rem(left, n_dp)))
            return left // n_dp

        return lax.fori_loop(0, count, once, rest)

    def walk(k, carry):
        rest, spreads, passes, weighs, cores, crosses = carry
        digit = lax.rem(rest, n_dp)
        take(k, member(digit), digit)
        spreads = repeat([0, 4, 3], k, spreads, spread)
        crosses = repeat([0, 0, 0, 0, 3, 1, 1, 1], k, crosses, cross_y)
        passes = repeat([0, 0, 0, 2, 4, 2], k, passes, pass_on)
        weighs = repeat([0, 0, 0, 0, 2, 2, 2, 2], k, weighs, weigh)
        cores = repeat([0, 1, 1, 1, 2, 1, 1, 1], k, cores, cross_core)

        @pl.when(k == 2)
        def _():
            for step in range(1, n_dp):
                source = lax.rem(row + step, n_dp)
                gain_to(source, source).wait_recv()
            total = gain_rows[0]
            for other in range(1, n_dp):
                total = total + gain_rows[other]
            gain_col[...] = total
            gain_cols[col] = total
            for step in peers:
                gain_across(step, col).start()

        return rest // n_dp, spreads, passes, weighs, cores, crosses

    crosses = lax.fori_loop(0, n_dp, walk, (code, code // n_dp, code, code, code, code))[-1]

    def plans(source):
        k_target, v_target = n_ctx // 2, n_ctx // 2 + 1
        return (
            (0, 2 * head, source // 2, lax.rem(source, 2) * groups * 2 * head),
            (2 * head, head, k_target, groups * source * head),
            (3 * head, head, v_target, groups * source * head),
        )

    def share(g, source, plan, peer, receiving=False):
        start, size, target, at = plan
        here = dw_out.at[shifted, pl.ds(pl.multiple_of(g * unit + start, head), size)]
        there = dw_in.at[:, pl.ds(pl.multiple_of(at + g * size, head), size)]
        if peer is None:
            return pltpu.make_async_copy(here, there, own_d.at[g])
        return remote(here, there, send_d.at[g, start // head], recv_d.at[source, g], "ctx", peer)

    @pl.loop(0, groups)
    def _(g):
        at = pl.ds(pl.multiple_of(g * unit, unit), unit)
        dw_out[:, at] = acc[:, at].astype(dw_out.dtype)
        for plan in plans(col):
            pl.when(plan[2] != col)(lambda: share(g, col, plan, plan[2]).start())
            pl.when(plan[2] == col)(lambda: share(g, col, plan, None).start())

    @pl.loop(0, 2, init_carry=crosses)
    def _(_, left):
        cross_y(member(lax.rem(left, n_dp)))
        return left // n_dp

    for step in peers:
        gain_across(step, flipped(col, step)).wait_recv()
    gain_total = gain_cols[0]
    for other in range(1, n_ctx):
        gain_total = gain_total + gain_cols[other]
    gain_out[...] = gain_total

    for step in range(1, n_dp):
        back_recv(lax.rem(row + step, n_dp)).wait_recv()
    own_back().wait()

    for step in range(n_ctx):
        source = flipped(col, step)
        for plan in plans(source):
            for g in range(groups):
                if step:
                    pl.when(plan[2] == col)(lambda: share(g, source, plan, source).wait_recv())
                else:
                    pl.when(plan[2] == col)(lambda: share(g, source, plan, None).wait())

    for step in peers:
        pos_copy(step, col).wait_send()
        gain_across(step, col).wait_send()
        for g in range(groups):
            for copy in head_copies(step, g):
                copy.wait_send()
    for plan in plans(col):
        for g in range(groups):
            pl.when(plan[2] != col)(lambda: share(g, col, plan, plan[2]).wait_send())

    @pl.loop(1, n_dp)
    def _(step):
        peer = lax.rem(row + step, n_dp)
        col_send(peer).wait_send()
        gain_to(peer, row).wait_send()
        back_send(peer).wait_send()

    @pl.loop(0, n_dp)
    def _(block):
        cols_out(block, 2, send_xy, recv_xy).wait_send()
        cols_out(block, 1, send_xc, recv_xc).wait_send()
        cols_out(block, 1, send_xf, recv_xf, False, 2).wait_send()
        core_copy(block).wait_send()
        y_copy(block).wait_send()
        zone = block // 2

        @pl.when(lax.rem(block, 2) == lane)
        def _():
            for g in range(groups):
                if g < groups - 1:
                    relay(block, g, 2, twin).wait_send()
                else:
                    pl.when(zone != near)(lambda: relay(block, g, 2, twin).wait_send())
                    pl.when(zone == near)(lambda: most(block, twin).wait_send())
                pl.when((zone <= place) & (place < line - 1))(lambda: relay(block, g, 0, row + 2).wait_send())
                pl.when((zone >= place) & (place > 0))(lambda: relay(block, g, 1, row - 2).wait_send())

    remainder(twin, 2 * near + lane).wait_send()


def layer(inputs, q_proj, k_proj, v_proj, d_attn, positions, windows, q_gain, k_gain, weight):
    n_dp, n_ctx = lax.axis_size("dp"), lax.axis_size("ctx")
    toks, model = inputs.shape
    part = weight.shape[0]
    head = q_gain.shape[0]
    groups = k_proj.shape[1] // head // n_ctx
    pair = q_proj.shape[1] // n_ctx // groups
    unit = pair + 2 * head
    length = n_ctx * toks
    wide = max(-(-(index * part % head + part) // head) for index in range(n_dp)) * head
    frequency = np.exp(np.arange(head // 2) * (-2.0 * math.log(rope_base) / head))
    frequency = jnp.asarray(np.tile(frequency, 2)[None, :], jnp.float32)
    dma = pltpu.SemaphoreType.DMA
    vmem = pl.BlockSpec(memory_space=pltpu.VMEM)
    smem = pl.BlockSpec(memory_space=pltpu.SMEM)
    anywhere = pl.BlockSpec(memory_space=pl.ANY)
    low, full = jnp.bfloat16, jnp.float32
    return pl.pallas_call(
        lambda *refs: layer_kernel(n_dp, n_ctx, part, *refs),
        out_shape=(
            jax.ShapeDtypeStruct((n_dp, toks, wide), low),
            jax.ShapeDtypeStruct((part, groups * unit), low),
            jax.ShapeDtypeStruct((8, head), full),
        ),
        in_specs=[anywhere] * 5 + [vmem, smem, vmem, vmem, vmem, anywhere],
        out_specs=(anywhere, anywhere, vmem),
        scratch_shapes=[
            pltpu.VMEM((groups, length, pair), low),
            pltpu.VMEM((groups, length, head), low),
            pltpu.VMEM((groups, length, head), low),
            pltpu.VMEM((groups, length, pair), low),
            pltpu.VMEM((8, head), full),
            pltpu.VMEM((n_ctx, 8, head), full),
            pltpu.VMEM((length, head), full),
            pltpu.VMEM((length, head), full),
            pltpu.VMEM((length, head), jnp.int32),
            pltpu.VMEM((n_ctx, 2 * toks, head), low),
            pltpu.VMEM((n_ctx, 2 * toks, head), low),
            pltpu.VMEM((length, head), low),
            pltpu.VMEM((length, head), full),
            pltpu.VMEM((length, head), full),
            pltpu.VMEM((n_dp, groups, length, unit), low),
            pltpu.VMEM((groups, wide, unit), low),
            pltpu.VMEM((n_dp, length, wide), low),
            pltpu.VMEM((wide, groups * unit), full),
            pltpu.VMEM((length, wide), full),
            pltpu.VMEM((n_dp, toks, wide), full),
            pltpu.VMEM((n_dp, toks, wide), full),
            pltpu.VMEM((n_dp, 2, toks, wide), low),
            pltpu.VMEM((n_dp, 2, toks, wide), low),
            pltpu.VMEM((n_dp, toks, wide), low),
            pltpu.VMEM((n_dp, toks, wide), low),
            pltpu.VMEM((n_dp, toks, wide), low),
            pltpu.VMEM((2, 8, head), full),
            pltpu.VMEM((8, head), full),
            pltpu.VMEM((n_dp, 8, head), full),
            pltpu.VMEM((8, head), full),
            pltpu.VMEM((n_ctx, 8, head), full),
            pltpu.VMEM((wide, groups * unit), low),
            dma((groups, 4)),
            dma((groups, 3)),
            dma,
            dma((n_ctx,)),
            dma((n_ctx,)),
            dma((n_ctx, groups, 4)),
            dma((n_ctx, groups, 4)),
            dma((n_dp,)),
            dma((n_dp,)),
            dma((n_dp,)),
            dma((n_dp,)),
            dma((n_dp,)),
            dma((n_dp,)),
            dma((n_dp,)),
            dma((n_dp,)),
            dma((4, n_dp, groups)),
            dma((n_dp, groups)),
            dma((n_dp,)),
            dma((n_dp,)),
            dma((n_dp,)),
            dma((n_dp,)),
            dma((n_dp,)),
            dma((n_dp,)),
            dma((n_dp,)),
            dma((n_dp,)),
            dma((n_ctx,)),
            dma((n_ctx,)),
            dma((groups, unit // head)),
            dma((n_ctx, groups)),
            dma((groups,)),
            dma,
            dma,
        ],
        compiler_params=pltpu.CompilerParams(
            collective_id=3, has_side_effects=True, vmem_limit_bytes=58 * 1024 * 1024
        ),
        name="layer",
    )(
        inputs, q_proj, k_proj, v_proj, d_attn, positions, windows,
        q_gain[None, :], k_gain[None, :], frequency, weight,
    )


def finish_kernel(part, ret_ref, dw_ref, gain_ref, din_ref, out_ref, q_out, k_out):
    count, _, wide = ret_ref.shape
    head = gain_ref.shape[1]
    starts = [index * part // head for index in range(count)]
    pieces = wide // head
    for index in range(count):
        first = 1 if index > 0 and starts[index] < starts[index - 1] + pieces else 0
        last = pieces - 1 if index + 1 < count and starts[index + 1] < starts[index] + pieces else pieces
        base = starts[index] * head
        din_ref[:, base + first * head:base + last * head] = ret_ref[index, :, first * head:last * head]
        if last < pieces:
            both = ret_ref[index, :, last * head:].astype(jnp.float32) + ret_ref[index + 1, :, :head].astype(jnp.float32)
            din_ref[:, base + last * head:base + pieces * head] = both.astype(din_ref.dtype)
    out_ref[...] = dw_ref[...].astype(out_ref.dtype)
    q_out[...] = gain_ref[0:1, :]
    k_out[...] = gain_ref[1:2, :]


def finished(returned, weight_rows, gains, model):
    n_dp, toks, wide = returned.shape
    part, rows = weight_rows.shape
    head = gains.shape[1]
    steps = 2
    return pl.pallas_call(
        lambda *refs: finish_kernel(part, *refs),
        grid=(steps,),
        out_shape=(
            jax.ShapeDtypeStruct((toks, model), jnp.bfloat16),
            jax.ShapeDtypeStruct((part, rows), jnp.float32),
            jax.ShapeDtypeStruct((1, head), jnp.float32),
            jax.ShapeDtypeStruct((1, head), jnp.float32),
        ),
        in_specs=[
            pl.BlockSpec((n_dp, toks // steps, wide), lambda i: (0, i, 0)),
            pl.BlockSpec((part // steps, rows), lambda i: (i, 0)),
            pl.BlockSpec((8, head), lambda i: (0, 0)),
        ],
        out_specs=(
            pl.BlockSpec((toks // steps, model), lambda i: (i, 0)),
            pl.BlockSpec((part // steps, rows), lambda i: (i, 0)),
            pl.BlockSpec((1, head), lambda i: (0, 0)),
            pl.BlockSpec((1, head), lambda i: (0, 0)),
        ),
        compiler_params=pltpu.CompilerParams(vmem_limit_bytes=58 * 1024 * 1024),
        name="finish",
    )(returned, weight_rows, gains)


def head_shards(inputs, q_proj, k_proj, v_proj, d_attn, positions, windows, q_gain, k_gain, weight):
    returned, weight_rows, gains = layer(
        inputs[0], q_proj[0], k_proj[0], v_proj[0], d_attn[0], positions, windows, q_gain, k_gain, weight
    )
    d_inputs, d_weight, dq_gain, dk_gain = finished(returned, weight_rows, gains, inputs.shape[2])
    return (d_inputs[None], d_weight.T, dq_gain[0], dk_gain[0])


def by_heads(mesh):
    return mesh.shape["dp"] == 8 and mesh.shape["ctx"] == 4


def solution(mesh):
    placed = (
        P("dp", "ctx", None),
        P("dp", "ctx", None),
        P("dp", "ctx", None),
        P("dp", "ctx", None),
        P("dp", "ctx", None),
        P("dp", "ctx"),
        P("dp"),
        P(),
        P(),
        P("dp", None),
    )
    return jax.shard_map(
        head_shards if by_heads(mesh) else shards,
        mesh=mesh,
        in_specs=placed,
        out_specs=(P("dp", "ctx", None), P("ctx", "dp"), P(), P()),
        check_vma=False,
    )
```

```python
import math

import jax
import jax.numpy as jnp
import numpy as np
from jax import lax
from jax.experimental import pallas as pl
from jax.experimental.pallas import tpu as pltpu
from jax.sharding import PartitionSpec as P

MESH = pl.DeviceIdType.MESH

REACH = 8


score_scale = 168.0 ** (-0.5)
rope_base = 10000.0
norm_eps = 1e-06


def from_behind(value, axis, steps):
    count = lax.axis_size(axis)
    initial, last = (max(0, -steps), min(count, count - steps))
    return lax.ppermute(value, axis, [(source, source + steps) for source in range(initial, last)])


def swapped(value, axis, bit):
    count = lax.axis_size(axis)
    return lax.ppermute(value, axis, [(source, source ^ bit) for source in range(count)])


def flipped(index, bits):
    bit = 1
    while bit <= bits:
        if bits & bit:
            index = index + bit - 2 * bit * (lax.rem(index // bit, 2))
        bit *= 2
    return index


def remote(source, target, send_sem, recv_sem, axis, index):
    return pltpu.make_async_remote_copy(
        src_ref=source,
        dst_ref=target,
        send_sem=send_sem,
        recv_sem=recv_sem,
        device_id={axis: index},
        device_id_type=MESH,
    )


def exchange_kernel(n_dp, n_ctx, reach, parts_ref, pair_ref, cols_ref, far_ref, own_sem, send_a, recv_a, send_b, recv_b):
    row = lax.axis_index("dp")
    col = lax.axis_index("ctx")
    barrier = pltpu.get_barrier_semaphore()
    for step in range(1, n_dp):
        pl.semaphore_signal(barrier, 1, device_id={"dp": lax.rem(row + step, n_dp)}, device_id_type=MESH)
    for step in range(1, n_ctx):
        pl.semaphore_signal(barrier, 1, device_id={"ctx": lax.rem(col + step, n_ctx)}, device_id_type=MESH)
    pl.semaphore_wait(barrier, n_dp + n_ctx - 2)
    for step in range(1, reach + 1):
        copy = remote(pair_ref, far_ref.at[step - 1], send_b.at[step], recv_b.at[step], "ctx", lax.rem(col + step, n_ctx))
        pl.when(col + step < n_ctx)(copy.start)
    own = pltpu.make_async_copy(parts_ref.at[row], cols_ref.at[row], own_sem)
    own.start()
    sends = []
    for step in range(1, n_dp):
        peer = lax.rem(row + step, n_dp)
        copy = remote(parts_ref.at[peer], cols_ref.at[row], send_a.at[step], recv_a.at[step], "dp", peer)
        copy.start()
        sends.append(copy)
    own.wait()
    for step in range(1, n_dp):
        source = lax.rem(row + n_dp - step, n_dp)
        remote(parts_ref.at[source], cols_ref.at[source], send_a.at[step], recv_a.at[step], "dp", source).wait_recv()
        sends[step - 1].wait_send()
    for step in range(1, reach + 1):
        copy = remote(pair_ref, far_ref.at[step - 1], send_b.at[step], recv_b.at[step], "ctx", lax.rem(col + step, n_ctx))
        pl.when(col + step < n_ctx)(copy.wait_send)
        pl.when(col >= step)(copy.wait_recv)


def exchanged(parts, pair, reach):
    n_dp, n_ctx = lax.axis_size("dp"), lax.axis_size("ctx")
    anywhere = pl.BlockSpec(memory_space=pl.ANY)
    dma = pltpu.SemaphoreType.DMA
    return pl.pallas_call(
        lambda *refs: exchange_kernel(n_dp, n_ctx, reach, *refs),
        out_shape=(
            jax.ShapeDtypeStruct(parts.shape, parts.dtype),
            jax.ShapeDtypeStruct((reach,) + pair.shape, pair.dtype),
        ),
        in_specs=[anywhere, anywhere],
        out_specs=(anywhere, anywhere),
        scratch_shapes=[dma, dma((n_dp,)), dma((n_dp,)), dma((reach + 1,)), dma((reach + 1,))],
        compiler_params=pltpu.CompilerParams(collective_id=1, has_side_effects=True),
        name="exchange",
    )(parts, pair)


def project_kernel(
    n_dp, n_ctx, d_ref, w_ref, cols_ref, gain_ref, back_ref, sum_ref, gain_out,
    blocks, acc, outbox, terms, got, gain_rows, gain_sent, gain_got,
    own_sem, send_g, recv_g, send_o, recv_o, send_w, recv_w, send_r, recv_r, send_c, recv_c,
):
    row = lax.axis_index("dp")
    col = lax.axis_index("ctx")
    line = n_dp // 2
    place = row // 2
    lane = lax.rem(row, 2)
    twin = 1 - 2 * lane
    width = w_ref.shape[1]
    bits = [1 << k for k in range(n_ctx.bit_length() - 1)]
    barrier = pltpu.get_barrier_semaphore()
    for step in range(1, n_dp):
        pl.semaphore_signal(barrier, 1, device_id={"dp": lax.rem(row + step, n_dp)}, device_id_type=MESH)
    for bit in bits:
        pl.semaphore_signal(barrier, 1, device_id={"ctx": flipped(col, bit)}, device_id_type=MESH)
    pl.semaphore_wait(barrier, n_dp - 1 + len(bits))

    def relay(block, way, target):
        return remote(blocks.at[block], blocks.at[block], send_g.at[way, block], recv_g.at[block], "dp", target)

    def arrived(block):
        relay(block, 0, lax.rem(row + 1, n_dp)).wait_recv()

    def back(block, target):
        return remote(outbox.at[block], back_ref.at[row], send_o.at[block], recv_o.at[row], "dp", target)

    def product(block):
        acc[...] = jnp.zeros_like(acc)
        depth = 2048

        @pl.loop(0, width // depth)
        def _(k):
            span = pl.ds(pl.multiple_of(k * depth, depth), depth)
            acc[...] += lax.dot_general(
                blocks[block, :, span], w_ref[:, span], (((1,), (1,)), ((), ())),
                preferred_element_type=jnp.float32,
            )

        outbox[block] = acc[...].astype(outbox.dtype)

    def answer(block):
        product(block)
        back(block, block).start()

    blocks[row] = d_ref[...]
    pl.when(place < line - 1)(lambda: relay(row, 0, row + 2).start())
    pl.when(place > 0)(lambda: relay(row, 1, row - 2).start())
    relay(row, 2, row + twin).start()

    def gain_to(peer):
        return remote(gain_ref, gain_rows.at[row], send_r.at[peer], recv_r.at[row], "dp", peer)

    gain_rows[row] = gain_ref[...]
    for step in range(1, n_dp):
        gain_to(lax.rem(row + step, n_dp)).start()
    product(row)
    own = pltpu.make_async_copy(outbox.at[row], back_ref.at[row], own_sem)
    own.start()

    @pl.loop(1, line + 1)
    def _(step):
        @pl.when(place >= step)
        def _():
            block = row - 2 * step
            arrived(block)
            pl.when(place < line - 1)(lambda: relay(block, 0, row + 2).start())
            relay(block, 2, row + twin).start()

        @pl.when(place + step < line)
        def _():
            block = row + 2 * step
            arrived(block)
            pl.when(place > 0)(lambda: relay(block, 1, row - 2).start())
            relay(block, 2, row + twin).start()

        pl.when(place >= step)(lambda: answer(row - 2 * step))
        pl.when(place + step < line)(lambda: answer(row + 2 * step))

        @pl.when(place >= step - 1)
        def _():
            block = row + twin - 2 * (step - 1)
            arrived(block)
            answer(block)

        @pl.when((step > 1) & (place + step - 1 < line))
        def _():
            block = row + twin + 2 * (step - 1)
            arrived(block)
            answer(block)

    tokens = n_dp * blocks.shape[1]
    rows = width // n_ctx
    tile = min(512, rows)

    def fill(slot):
        start = flipped(col, slot) * rows

        @pl.loop(0, rows // tile)
        def _(k):
            span = pl.ds(pl.multiple_of(start + k * tile, tile), tile)
            left = blocks[:, :, span].reshape(tokens, tile)
            right = cols_ref[...].reshape(tokens, cols_ref.shape[2])
            term = lax.dot_general(
                left, right, (((0,), (0,)), ((), ())), preferred_element_type=jnp.float32
            )
            terms[slot, pl.ds(pl.multiple_of(k * tile, tile), tile), :] = term.astype(terms.dtype)

    def share(slot):
        bit = slot & -slot
        return remote(terms.at[slot], got.at[slot], send_w.at[slot], recv_w.at[slot], "ctx", flipped(col, bit))

    def merge(slot, bit):
        share(slot + bit).wait_recv()
        if slot:
            total = terms[slot].astype(jnp.float32) + got[slot + bit].astype(jnp.float32)
            terms[slot] = total.astype(terms.dtype)
            if slot & (2 * bit):
                share(slot).start()
        else:
            held = sum_ref[...] if bit > 1 else terms[0].astype(jnp.float32)
            sum_ref[...] = held + got[bit].astype(jnp.float32)

    for slot in reversed(range(0, n_ctx, 2)):
        fill(slot + 1)
        share(slot + 1).start()
        fill(slot)
        merge(slot, 1)

    for step in range(1, n_dp):
        peer = lax.rem(row + step, n_dp)
        remote(gain_ref, gain_rows.at[peer], send_r.at[peer], recv_r.at[peer], "dp", peer).wait_recv()
    gain_total = gain_rows[0]
    for peer in range(1, n_dp):
        gain_total = gain_total + gain_rows[peer]
    for level, bit in enumerate(bits):
        gain_sent[level] = gain_total
        copy = remote(
            gain_sent.at[level], gain_got.at[level], send_c.at[level], recv_c.at[level],
            "ctx", flipped(col, bit),
        )
        copy.start()
        copy.wait()
        gain_total = gain_total + gain_got[level]
    gain_out[...] = gain_total

    for bit in bits[1:]:
        for slot in reversed(range(0, n_ctx, 2 * bit)):
            merge(slot, bit)
    for step in range(1, n_dp):
        gain_to(lax.rem(row + step, n_dp)).wait_send()
    for slot in range(1, n_ctx):
        share(slot).wait_send()
    own.wait()

    @pl.loop(1, n_dp)
    def _(step):
        source = lax.rem(row + step, n_dp)
        remote(outbox.at[source], back_ref.at[source], send_o.at[source], recv_o.at[source], "dp", source).wait_recv()
        back(source, source).wait_send()

    relay(row, 2, row + twin).wait_send()
    pl.when(place < line - 1)(lambda: relay(row, 0, row + 2).wait_send())
    pl.when(place > 0)(lambda: relay(row, 1, row - 2).wait_send())

    @pl.loop(1, line)
    def _(step):
        @pl.when(place >= step)
        def _():
            block = row - 2 * step
            pl.when(place < line - 1)(lambda: relay(block, 0, row + 2).wait_send())
            relay(block, 2, row + twin).wait_send()

        @pl.when(place + step < line)
        def _():
            block = row + 2 * step
            pl.when(place > 0)(lambda: relay(block, 1, row - 2).wait_send())
            relay(block, 2, row + twin).wait_send()


def projected(d_own, weight, cols, gains):
    n_dp, n_ctx = lax.axis_size("dp"), lax.axis_size("ctx")
    toks, width = d_own.shape
    part = weight.shape[0]
    dma = pltpu.SemaphoreType.DMA
    levels = n_ctx.bit_length() - 1
    vmem = pl.BlockSpec(memory_space=pltpu.VMEM)
    return pl.pallas_call(
        lambda *refs: project_kernel(n_dp, n_ctx, *refs),
        out_shape=(
            jax.ShapeDtypeStruct((n_dp, toks, part), jnp.bfloat16),
            jax.ShapeDtypeStruct((width // n_ctx, part), jnp.float32),
            jax.ShapeDtypeStruct(gains.shape, jnp.float32),
        ),
        in_specs=[vmem, vmem, vmem, vmem],
        out_specs=(pl.BlockSpec(memory_space=pl.ANY), vmem, vmem),
        scratch_shapes=[
            pltpu.VMEM((n_dp, toks, width), jnp.bfloat16),
            pltpu.VMEM((toks, part), jnp.float32),
            pltpu.VMEM((n_dp, toks, part), jnp.bfloat16),
            pltpu.VMEM((n_ctx, width // n_ctx, part), jnp.bfloat16),
            pltpu.VMEM((n_ctx, width // n_ctx, part), jnp.bfloat16),
            pltpu.VMEM((n_dp,) + gains.shape, jnp.float32),
            pltpu.VMEM((levels,) + gains.shape, jnp.float32),
            pltpu.VMEM((levels,) + gains.shape, jnp.float32),
            dma,
            dma((3, n_dp)),
            dma((n_dp,)),
            dma((n_dp,)),
            dma((n_dp,)),
            dma((n_ctx,)),
            dma((n_ctx,)),
            dma((n_dp,)),
            dma((n_dp,)),
            dma((levels,)),
            dma((levels,)),
        ],
        compiler_params=pltpu.CompilerParams(
            collective_id=2, has_side_effects=True, vmem_limit_bytes=56 * 1024 * 1024
        ),
        name="project",
    )(d_own, weight, cols, gains)


def rotated_unit(projected_rows, gain_vector, token_pos, head_count):
    head_width = gain_vector.shape[0]
    rows_heads = projected_rows.reshape(projected_rows.shape[0], head_count, head_width)
    inverse = lax.rsqrt(jnp.mean(rows_heads * rows_heads, axis=-1, keepdims=True) + norm_eps)
    normed = rows_heads * inverse * gain_vector
    half_width = head_width // 2
    frequency = jnp.exp(
        jnp.arange(half_width, dtype=jnp.float32) * (-2.0 * math.log(rope_base) / head_width)
    )
    angles = token_pos.astype(jnp.float32)[:, None] * frequency[None, :]
    cosine_table = jnp.cos(angles)[:, None, :]
    sine_table = jnp.sin(angles)[:, None, :]
    first_half = normed[..., :half_width]
    second_half = normed[..., half_width:]
    return jnp.concatenate(
        [
            first_half * cosine_table - second_half * sine_table,
            second_half * cosine_table + first_half * sine_table,
        ],
        axis=-1,
    )


def shards(inputs, q_proj, k_proj, v_proj, d_attn, positions, windows, q_gain, k_gain, weight):
    tok_rows = inputs.shape[1]
    head_width = q_gain.shape[0]
    query_heads = q_proj.shape[2] // head_width
    key_heads = k_proj.shape[2] // head_width
    group_size = query_heads // key_heads
    token_pos = positions[0]
    window = windows[0]
    dp_count = lax.axis_size("dp")
    model_width = inputs.shape[2]
    input_parts = inputs[0].reshape(tok_rows, dp_count, model_width // dp_count).transpose(1, 0, 2)
    def query_side(projected_rows, gain_vector):
        return rotated_unit(projected_rows, gain_vector, token_pos, query_heads)

    def key_side(projected_rows, gain_vector):
        return rotated_unit(projected_rows, gain_vector, token_pos, key_heads)

    q_full, query_back = jax.vjp(query_side, q_proj[0].astype(jnp.float32), q_gain)
    k_full, key_back = jax.vjp(key_side, k_proj[0].astype(jnp.float32), k_gain)
    query_rotated = q_full.astype(jnp.bfloat16).reshape(tok_rows, key_heads, group_size, head_width)
    key_rotated = k_full.astype(jnp.bfloat16)
    v_own = v_proj[0].reshape(tok_rows, key_heads, head_width)
    reach_count = min(REACH, lax.axis_size("ctx") - 1)
    own_pair = jnp.stack([key_rotated, v_own])
    input_cols, far_pairs = exchanged(input_parts, own_pair, reach_count)
    known = jnp.arange(1, reach_count + 1) <= lax.axis_index("ctx")
    far_pairs = jnp.where(known[:, None, None, None, None], far_pairs, 0)
    all_keys = jnp.concatenate([key_rotated[None], far_pairs[:, 0]])
    all_values = jnp.concatenate([v_own[None], far_pairs[:, 1]])
    block_ids = jnp.arange(reach_count + 1, dtype=jnp.int32)
    offsets = jnp.arange(tok_rows, dtype=jnp.int32)
    distance = block_ids[None, :, None] * tok_rows + offsets[:, None, None] - offsets[None, None, :]
    allowed = (distance >= 0) & (distance < window) & (distance <= token_pos[:, None, None])
    scores = (
        jnp.einsum("ahgd,bchd->hgabc", query_rotated, all_keys, preferred_element_type=jnp.float32)
        * score_scale
    )
    scores = jnp.where(allowed, scores, -jnp.inf)
    row_max = jnp.max(scores, axis=(3, 4), keepdims=True)
    exponent = jnp.exp(scores - row_max)
    probs = exponent / jnp.sum(exponent, axis=(3, 4), keepdims=True)
    head_gradient = d_attn[0].reshape(tok_rows, key_heads, group_size, head_width)
    dprobs = jnp.einsum(
        "ahgd,bchd->hgabc", head_gradient, all_values, preferred_element_type=jnp.float32
    )
    delta = jnp.sum(probs * dprobs, axis=(3, 4), keepdims=True)
    dscores = (probs * (dprobs - delta)).astype(jnp.bfloat16)
    probs_low = probs.astype(jnp.bfloat16)
    dq_rot = (
        jnp.einsum("hgabc,bchd->ahgd", dscores, all_keys, preferred_element_type=jnp.float32)
        * score_scale
    )
    dk_blocks = (
        jnp.einsum("hgabc,ahgd->bchd", dscores, query_rotated, preferred_element_type=jnp.float32)
        * score_scale
    )
    dv_blocks = jnp.einsum(
        "hgabc,ahgd->bchd", probs_low, head_gradient, preferred_element_type=jnp.float32
    )
    dq_proj, dq_gain = query_back(dq_rot.reshape(tok_rows, query_heads, head_width))
    pair_total = jnp.stack([dk_blocks[0], dv_blocks[0]])
    for distance_steps in range(1, reach_count + 1):
        far_pair = jnp.stack([dk_blocks[distance_steps], dv_blocks[distance_steps]])
        back_pair = from_behind(far_pair.astype(jnp.bfloat16), "ctx", -distance_steps)
        pair_total = pair_total + back_pair.astype(jnp.float32)
    dk_proj, dk_gain = key_back(pair_total[0])
    dv_proj = pair_total[1].reshape(tok_rows, key_heads * head_width)
    d_own = jnp.concatenate([dq_proj, dk_proj, dv_proj], axis=-1).astype(jnp.bfloat16)
    gains = jnp.pad(jnp.stack([dq_gain, dk_gain]), ((0, 6), (0, 0)))
    d_parts, d_weight_t, gain_sums = projected(d_own, weight, input_cols, gains)
    dq_gain_all, dk_gain_all = gain_sums[0], gain_sums[1]
    d_inputs = d_parts.transpose(1, 0, 2).reshape(1, tok_rows, model_width)
    return (d_inputs, d_weight_t, dq_gain_all, dk_gain_all)


def walk_code(line, place):
    far = 2 * (place + 1 - 2 * (place % 2)) + 1
    digits = []
    for step in range(line + 1):
        if step == 0:
            digits.append(2 * place)
            continue
        for other in (place - step, place + step):
            if 0 <= other < line:
                digits.append(2 * other)
        for other in (place - step + 1, place + step - 1):
            if 0 <= other < line and 2 * other + 1 not in digits + [far]:
                digits.append(2 * other + 1)
    digits.append(far)
    code = 0
    for digit in reversed(digits):
        code = code * 2 * line + digit
    return code


def unit_rows(values):
    inverse = lax.rsqrt(jnp.sum(values * values, axis=-1, keepdims=True) * (1.0 / values.shape[-1]) + norm_eps)
    return values * inverse, inverse


def turned(values, cosine, sine):
    return values * cosine + pltpu.roll(values, values.shape[-1] // 2, 1) * sine


def turned_back(values, cosine, sine):
    return values * cosine + pltpu.roll(values * sine, values.shape[-1] // 2, 1)


def norm_back(unit, inverse, gain, grad):
    scaled = grad * gain
    inner = jnp.sum(unit * scaled, axis=-1, keepdims=True) * (1.0 / unit.shape[-1])
    return inverse * (scaled - unit * inner)


def folded(values):
    return jnp.sum(values.reshape(values.shape[0] // 8, 8, values.shape[1]), axis=0)


def layer_kernel(
    n_dp, n_ctx, part,
    in_ref, q_ref, k_ref, v_ref, da_ref, pos_ref, win_ref, qgain_ref, kgain_ref, freq_ref, w_ref,
    ret_in, dw_in, gain_out,
    qs, ks, vs, ds, pos_own, pos_all, cos_t, sin_t, low_t, qrot, dstack, krot, dk_acc, dv_acc,
    blocks, wext, cols, acc, prod, mine, keep, core_out, core_in, y_out, y_in, ret_out,
    gain_acc, gain_own, gain_rows, gain_col, gain_cols, dw_out,
    loc_a, loc_w, loc_x, send_p, recv_p, send_a, recv_a, send_x, recv_x, send_xy, recv_xy,
    send_xc, recv_xc, send_xf, recv_xf, send_g, recv_g, send_c, recv_c, send_y, recv_y, send_r, recv_r,
    send_n, recv_n, send_m, recv_m, send_d, recv_d, own_d, recv_z, own_r,
):
    row = lax.axis_index("dp")
    col = lax.axis_index("ctx")
    line = n_dp // 2
    place = row // 2
    lane = lax.rem(row, 2)
    twin = row + 1 - 2 * lane
    near = place + 1 - 2 * lax.rem(place, 2)
    head = qgain_ref.shape[1]
    toks = in_ref.shape[0]
    wide = cols.shape[2]
    peers = range(1, n_ctx)
    key_base = q_ref.shape[1]
    value_base = key_base + k_ref.shape[1]
    groups = qs.shape[0]
    pair = qs.shape[2]
    unit = blocks.shape[3]

    barrier = pltpu.get_barrier_semaphore()
    for step in range(1, n_dp):
        pl.semaphore_signal(barrier, 1, device_id={"dp": lax.rem(row + step, n_dp)}, device_id_type=MESH)
    for step in peers:
        pl.semaphore_signal(barrier, 1, device_id={"ctx": flipped(col, step)}, device_id_type=MESH)

    first_tile = row * part // head
    shift = row * part - first_tile * head
    wext[...] = jnp.zeros_like(wext)
    shifted = pl.ds(pl.multiple_of(shift, 32), part)

    def weight_copies(g):
        sources = (
            ((2 * groups * col + 2 * g) * head, 0, 2 * head),
            (key_base + (groups * col + g) * head, 2 * head, head),
            (value_base + (groups * col + g) * head, 3 * head, head),
        )
        return [
            pltpu.make_async_copy(
                w_ref.at[:, pl.ds(pl.multiple_of(start, head), size)],
                wext.at[g, shifted, pl.ds(at, size)],
                loc_w.at[g, n],
            )
            for n, (start, at, size) in enumerate(sources)
        ]

    pos_own[...] = jnp.broadcast_to(pos_ref[...].astype(jnp.float32), pos_own.shape)
    pos_all[col] = pos_own[...]
    own_rows = pl.ds(pl.multiple_of(col * toks, toks), toks)

    def piece(target, g, source_col):
        at = pl.ds(pl.multiple_of(source_col * toks, toks), toks)
        wide_at = pl.ds(pl.multiple_of((groups * target + g) * pair, pair), pair)
        thin_at = pl.ds(pl.multiple_of((groups * target + g) * head, head), head)
        return (
            (q_ref.at[:, wide_at], qs.at[g, at, :]),
            (k_ref.at[:, thin_at], ks.at[g, at, :]),
            (v_ref.at[:, thin_at], vs.at[g, at, :]),
            (da_ref.at[:, wide_at], ds.at[g, at, :]),
        )

    def head_copies(step, g, receiving=False):
        peer = flipped(col, step)
        return [
            remote(source, target, send_a.at[step, g, n], recv_a.at[step, g, n], "ctx", peer)
            for n, (source, target) in enumerate(piece(peer, g, peer if receiving else col))
        ]

    def own_copies(g):
        return [
            pltpu.make_async_copy(source, target, loc_a.at[g, n])
            for n, (source, target) in enumerate(piece(col, g, col))
        ]

    def pos_copy(step, source_col):
        return remote(pos_own, pos_all.at[source_col], send_p.at[step], recv_p.at[step], "ctx", flipped(col, step))

    for copy in own_copies(0):
        copy.start()
    pl.semaphore_wait(barrier, n_dp + n_ctx - 2)
    for step in peers:
        pos_copy(step, col).start()
    for g in range(groups):
        for step in reversed(peers):
            for copy in head_copies(step, g):
                copy.start()
    for g in range(1, groups):
        for copy in own_copies(g):
            copy.start()

    def slab(index):
        start = index * part // head
        return pl.ds(pl.multiple_of(start * head, head), wide)

    def col_send(peer):
        return remote(in_ref.at[:, slab(peer)], cols.at[row, own_rows, :], send_x.at[peer], recv_x.at[row], "dp", peer)

    def col_recv(source):
        return remote(in_ref.at[:, slab(row)], cols.at[source, own_rows, :], send_x.at[source], recv_x.at[source], "dp", source)

    code = walk_code(line, 0)
    for other in range(1, line):
        code = jnp.where(place == other, walk_code(line, other), code)

    def member(digit):
        flag = lax.rem(digit, 2)
        return digit - flag + lane + flag * (1 - 2 * lane)

    def rows_of(step):
        return pl.ds(pl.multiple_of(flipped(col, step) * toks, toks), toks)

    def cols_out(block, step, sends, recvs, receiving=False, rows=0):
        at = rows_of((rows ^ step) if receiving else rows)
        return remote(
            cols.at[block, at, :], cols.at[block, at, :], sends.at[block], recvs.at[block], "ctx", flipped(col, step)
        )

    def spread(block):
        pl.when(block != row)(lambda: col_recv(block).wait_recv())
        pl.when(block == row)(own_cols.wait)
        cols_out(block, 2, send_xy, recv_xy).start()
        cols_out(block, 1, send_xc, recv_xc).start()

    own_cols = pltpu.make_async_copy(in_ref.at[:, slab(row)], cols.at[row, own_rows, :], loc_x)
    own_cols.start()

    def send_cols(step, rest):
        col_send(member(lax.rem(rest, n_dp))).start()
        return rest // n_dp

    lax.fori_loop(1, n_dp, send_cols, code // n_dp)
    for g in range(groups):
        for copy in weight_copies(g):
            copy.start()
    gain_acc[...] = jnp.zeros_like(gain_acc)
    acc[...] = jnp.zeros_like(acc)
    spread(row)

    for step in peers:
        pos_copy(step, flipped(col, step)).wait_recv()

    @pl.loop(0, n_ctx)
    def _(block):
        rows = pl.ds(pl.multiple_of(block * toks, toks), toks)
        place_rows = jnp.broadcast_to(pos_all[block][0:1, :], (toks, toks)).T
        angle = place_rows * freq_ref[...]
        side = lax.broadcasted_iota(jnp.int32, (toks, head), 1)
        cos_t[rows, :] = jnp.cos(angle)
        sine = jnp.sin(angle)
        sin_t[rows, :] = jnp.where(side < head // 2, -sine, sine)
        index = lax.broadcasted_iota(jnp.int32, (toks, head), 0) + block * toks
        low_t[rows, :] = index - jnp.minimum(win_ref[0] - 1, place_rows.astype(jnp.int32))

    def relay(block, g, way, target):
        return remote(blocks.at[block, g], blocks.at[block, g], send_g.at[way, block, g], recv_g.at[block, g], "dp", target)

    @pl.loop(0, groups)
    def _(g):
        for step in reversed(peers):
            for copy in head_copies(step, g, True):
                copy.wait_recv()
        for copy in own_copies(g):
            copy.wait()

        @pl.loop(0, n_ctx)
        def _(block):
            rows = pl.ds(pl.multiple_of(block * toks, toks), toks)
            cosine, sine = cos_t[rows, :], sin_t[rows, :]
            key_unit, _ = unit_rows(ks[g, rows, :].astype(jnp.float32))
            krot[rows, :] = turned(key_unit * kgain_ref[...], cosine, sine).astype(krot.dtype)
            for h in range(2):
                span = slice(h * head, (h + 1) * head)
                at = slice(h * toks, (h + 1) * toks)
                query_unit, _ = unit_rows(qs[g, rows, span].astype(jnp.float32))
                qrot[block, at, :] = turned(query_unit * qgain_ref[...], cosine, sine).astype(qrot.dtype)
                dstack[block, at, :] = ds[g, rows, span]

        dk_acc[...] = jnp.zeros_like(dk_acc)
        dv_acc[...] = jnp.zeros_like(dv_acc)
        for block in range(n_ctx):
            count = (block + 1) * toks
            rows = slice(block * toks, (block + 1) * toks)
            query, grad = qrot[block], dstack[block]
            keys, values = krot[:count, :], vs[g, :count, :]
            contract_last = (((1,), (1,)), ((), ()))
            contract_first = (((0,), (0,)), ((), ()))
            scores = lax.dot_general(query, keys, contract_last, preferred_element_type=jnp.float32) * score_scale
            key_at = lax.broadcasted_iota(jnp.int32, scores.shape, 1)
            query_at = lax.rem(lax.broadcasted_iota(jnp.int32, scores.shape, 0), toks) + block * toks
            low = jnp.concatenate([low_t[rows, :]] * 2, axis=0)
            low = jnp.concatenate([low] * (block + 1), axis=1)
            scores = jnp.where((key_at >= low) & (key_at <= query_at), scores, -jnp.inf)
            exponent = jnp.exp(scores - jnp.max(scores, axis=-1, keepdims=True))
            probs = exponent * (1.0 / jnp.sum(exponent, axis=-1, keepdims=True))
            dprobs = lax.dot_general(grad, values, contract_last, preferred_element_type=jnp.float32)
            delta = jnp.sum(probs * dprobs, axis=-1, keepdims=True)
            dscores = (probs * (dprobs - delta)).astype(jnp.bfloat16)
            dquery = (
                lax.dot_general(dscores, keys, (((1,), (0,)), ((), ())), preferred_element_type=jnp.float32)
                * score_scale
            )
            dk_acc[:count, :] += lax.dot_general(dscores, query, contract_first, preferred_element_type=jnp.float32)
            dv_acc[:count, :] += lax.dot_general(
                probs.astype(jnp.bfloat16), grad, contract_first, preferred_element_type=jnp.float32
            )
            cosine, sine = cos_t[rows, :], sin_t[rows, :]
            for h in range(2):
                span = slice(h * head, (h + 1) * head)
                query_unit, inverse = unit_rows(qs[g, rows, span].astype(jnp.float32))
                back = turned_back(dquery[h * toks:(h + 1) * toks, :], cosine, sine)
                gain_acc[0] += folded(back * query_unit)
                blocks[row, g, rows, span] = norm_back(query_unit, inverse, qgain_ref[...], back).astype(blocks.dtype)

        @pl.loop(0, n_ctx)
        def _(block):
            rows = pl.ds(pl.multiple_of(block * toks, toks), toks)
            key_unit, inverse = unit_rows(ks[g, rows, :].astype(jnp.float32))
            back = turned_back(dk_acc[rows, :] * score_scale, cos_t[rows, :], sin_t[rows, :])
            gain_acc[1] += folded(back * key_unit)
            blocks[row, g, rows, 2 * head:3 * head] = norm_back(
                key_unit, inverse, kgain_ref[...], back
            ).astype(blocks.dtype)
            blocks[row, g, rows, 3 * head:4 * head] = dv_acc[rows, :].astype(blocks.dtype)

        relay(row, g, 2, twin).start()
        pl.when(place < line - 1)(lambda: relay(row, g, 0, row + 2).start())
        pl.when(place > 0)(lambda: relay(row, g, 1, row - 2).start())

    gain_own[...] = jnp.zeros_like(gain_own)
    gain_own[0:1, :] = jnp.sum(gain_acc[0], axis=0, keepdims=True)
    gain_own[1:2, :] = jnp.sum(gain_acc[1], axis=0, keepdims=True)
    gain_rows[row] = gain_own[...]

    def gain_to(peer, source):
        return remote(gain_own, gain_rows.at[source], send_n.at[peer], recv_n.at[source], "dp", peer)

    def gain_across(step, source_col):
        return remote(gain_col, gain_cols.at[source_col], send_m.at[step], recv_m.at[step], "ctx", flipped(col, step))

    for step in range(1, n_dp):
        gain_to(lax.rem(row + step, n_dp), row).start()

    for g in range(groups):
        for copy in weight_copies(g):
            copy.wait()

    def core_copy(block):
        return remote(core_out.at[block], core_in.at[block], send_c.at[block], recv_c.at[block], "ctx", flipped(col, 1))

    def y_copy(block):
        return remote(y_out.at[block], y_in.at[block], send_y.at[block], recv_y.at[block], "ctx", flipped(col, 2))

    def back_send(block):
        return remote(ret_out.at[block], ret_in.at[row], send_r.at[block], recv_r.at[row], "dp", block)

    def own_back():
        return pltpu.make_async_copy(ret_out.at[row], ret_in.at[row], own_r)

    def back_recv(source):
        return remote(ret_out.at[source], ret_in.at[source], send_r.at[source], recv_r.at[source], "dp", source)

    tile = 256

    cut = blocks.shape[2] // 8 * 6
    last_group = groups - 1

    def most(block, target):
        ref = blocks.at[block, last_group, pl.ds(0, cut), :]
        return remote(ref, ref, send_g.at[2, block, last_group], recv_g.at[block, last_group], "dp", target)

    def remainder(block, target):
        ref = blocks.at[block, last_group, pl.ds(cut, blocks.shape[2] - cut), :]
        return remote(ref, ref, send_g.at[3, block, last_group], recv_z, "dp", target)

    def take(k, block, digit):
        zone = digit // 2
        flag = lax.rem(digit, 2)
        for g in range(groups):
            if g < groups - 1:
                pl.when(block != row)(lambda: relay(block, g, 2, twin).wait_recv())
            else:
                pl.when((block != row) & ((flag == 0) | (zone != near)))(lambda: relay(block, g, 2, twin).wait_recv())

                @pl.when((flag == 1) & (zone == near))
                def _():
                    most(block, twin).wait_recv()
                    remainder(block, twin).wait_recv()

            @pl.when((flag == 0) & (zone < place) & (place < line - 1))
            def _():
                relay(block, g, 0, row + 2).start()

            @pl.when((flag == 0) & (zone > place) & (place > 0))
            def _():
                relay(block, g, 1, row - 2).start()

            if g < groups - 1:
                pl.when((flag == 0) & (zone != place))(lambda: relay(block, g, 2, twin).start())
            else:
                pl.when((flag == 0) & (zone != place) & (zone != near))(lambda: relay(block, g, 2, twin).start())
                pl.when((flag == 0) & (zone == near))(lambda: most(block, twin).start())

        @pl.when(k == line + 1)
        def _():
            remainder(twin, 2 * near + lane).start()

        @pl.loop(0, wide // tile)
        def _(n):
            span = pl.ds(pl.multiple_of(n * tile, tile), tile)
            total = None
            for g in range(groups):
                term = lax.dot_general(
                    blocks[block, g], wext[g, span, :], (((1,), (1,)), ((), ())), preferred_element_type=jnp.float32
                )
                total = term if total is None else total + term
            prod[:, span] = total

        core_out[block, 0] = prod[rows_of(1), :].astype(core_out.dtype)
        core_out[block, 1] = prod[rows_of(3), :].astype(core_out.dtype)
        core_copy(block).start()
        keep[block] = prod[rows_of(0), :]
        mine[block] = prod[rows_of(2), :]

    def cross_core(block):
        core_copy(block).wait_recv()
        y_out[block] = (mine[block] + core_in[block, 1].astype(jnp.float32)).astype(y_out.dtype)
        y_copy(block).start()
        keep[block] += core_in[block, 0].astype(jnp.float32)

    def cross_y(block):
        y_copy(block).wait_recv()
        ret_out[block] = (keep[block] + y_in[block].astype(jnp.float32)).astype(ret_out.dtype)
        pl.when(block != row)(lambda: back_send(block).start())
        pl.when(block == row)(lambda: own_back().start())

    def weigh(block):
        cols_out(block, 1, send_xc, recv_xc, True).wait_recv()
        cols_out(block, 1, send_xf, recv_xf, True, 2).wait_recv()

        @pl.loop(0, groups * (wide // tile))
        def _(n):
            g = n // (wide // tile)
            span = pl.ds(pl.multiple_of(lax.rem(n, wide // tile) * tile, tile), tile)
            at = pl.ds(pl.multiple_of(g * unit, unit), unit)
            acc[span, at] += lax.dot_general(
                cols[block, :, span], blocks[block, g], (((0,), (0,)), ((), ())),
                preferred_element_type=jnp.float32,
            )

    def pass_on(block):
        cols_out(block, 2, send_xy, recv_xy, True).wait_recv()
        cols_out(block, 1, send_xf, recv_xf, False, 2).start()

    def repeat(counts, k, rest, action):
        count = 0
        for at, value in enumerate(counts):
            count = count + jnp.where(k == at, value, 0)

        def once(_, left):
            action(member(lax.rem(left, n_dp)))
            return left // n_dp

        return lax.fori_loop(0, count, once, rest)

    def walk(k, carry):
        rest, spreads, passes, weighs, cores, crosses = carry
        digit = lax.rem(rest, n_dp)
        take(k, member(digit), digit)
        spreads = repeat([0, 4, 3], k, spreads, spread)
        crosses = repeat([0, 0, 0, 0, 3, 1, 1, 1], k, crosses, cross_y)
        passes = repeat([0, 0, 0, 2, 4, 2], k, passes, pass_on)
        weighs = repeat([0, 0, 0, 0, 2, 2, 2, 2], k, weighs, weigh)
        cores = repeat([0, 1, 1, 1, 2, 1, 1, 1], k, cores, cross_core)

        @pl.when(k == line + 1)
        def _():
            for step in range(1, n_dp):
                source = lax.rem(row + step, n_dp)
                gain_to(source, source).wait_recv()
            total = gain_rows[0]
            for other in range(1, n_dp):
                total = total + gain_rows[other]
            gain_col[...] = total
            gain_cols[col] = total
            for step in peers:
                gain_across(step, col).start()

        return rest // n_dp, spreads, passes, weighs, cores, crosses

    crosses = lax.fori_loop(0, n_dp, walk, (code, code // n_dp, code, code, code, code))[-1]

    def plans(source):
        k_target, v_target = n_ctx // 2, n_ctx // 2 + 1
        return (
            (0, 2 * head, source // 2, lax.rem(source, 2) * groups * 2 * head),
            (2 * head, head, k_target, groups * source * head),
            (3 * head, head, v_target, groups * source * head),
        )

    def share(g, source, plan, peer, receiving=False):
        start, size, target, at = plan
        here = dw_out.at[shifted, pl.ds(pl.multiple_of(g * unit + start, head), size)]
        there = dw_in.at[:, pl.ds(pl.multiple_of(at + g * size, head), size)]
        if peer is None:
            return pltpu.make_async_copy(here, there, own_d.at[g])
        return remote(here, there, send_d.at[g, start // head], recv_d.at[source, g], "ctx", peer)

    @pl.loop(0, groups)
    def _(g):
        at = pl.ds(pl.multiple_of(g * unit, unit), unit)
        dw_out[:, at] = acc[:, at].astype(dw_out.dtype)
        for plan in plans(col):
            pl.when(plan[2] != col)(lambda: share(g, col, plan, plan[2]).start())
            pl.when(plan[2] == col)(lambda: share(g, col, plan, None).start())

    @pl.loop(0, 2, init_carry=crosses)
    def _(_, left):
        cross_y(member(lax.rem(left, n_dp)))
        return left // n_dp

    for step in peers:
        gain_across(step, flipped(col, step)).wait_recv()
    gain_total = gain_cols[0]
    for other in range(1, n_ctx):
        gain_total = gain_total + gain_cols[other]
    gain_out[...] = gain_total

    for step in range(1, n_dp):
        back_recv(lax.rem(row + step, n_dp)).wait_recv()
    own_back().wait()

    for step in range(n_ctx):
        source = flipped(col, step)
        for plan in plans(source):
            for g in range(groups):
                if step:
                    pl.when(plan[2] == col)(lambda: share(g, source, plan, source).wait_recv())
                else:
                    pl.when(plan[2] == col)(lambda: share(g, source, plan, None).wait())

    for step in peers:
        pos_copy(step, col).wait_send()
        gain_across(step, col).wait_send()
        for g in range(groups):
            for copy in head_copies(step, g):
                copy.wait_send()
    for plan in plans(col):
        for g in range(groups):
            pl.when(plan[2] != col)(lambda: share(g, col, plan, plan[2]).wait_send())

    @pl.loop(1, n_dp)
    def _(step):
        peer = lax.rem(row + step, n_dp)
        col_send(peer).wait_send()
        gain_to(peer, row).wait_send()
        back_send(peer).wait_send()

    @pl.loop(0, n_dp)
    def _(block):
        cols_out(block, 2, send_xy, recv_xy).wait_send()
        cols_out(block, 1, send_xc, recv_xc).wait_send()
        cols_out(block, 1, send_xf, recv_xf, False, 2).wait_send()
        core_copy(block).wait_send()
        y_copy(block).wait_send()
        zone = block // 2

        @pl.when(lax.rem(block, 2) == lane)
        def _():
            for g in range(groups):
                if g < groups - 1:
                    relay(block, g, 2, twin).wait_send()
                else:
                    pl.when(zone != near)(lambda: relay(block, g, 2, twin).wait_send())
                    pl.when(zone == near)(lambda: most(block, twin).wait_send())
                pl.when((zone <= place) & (place < line - 1))(lambda: relay(block, g, 0, row + 2).wait_send())
                pl.when((zone >= place) & (place > 0))(lambda: relay(block, g, 1, row - 2).wait_send())

    remainder(twin, 2 * near + lane).wait_send()


def layer(inputs, q_proj, k_proj, v_proj, d_attn, positions, windows, q_gain, k_gain, weight):
    n_dp, n_ctx = lax.axis_size("dp"), lax.axis_size("ctx")
    toks, model = inputs.shape
    part = weight.shape[0]
    head = q_gain.shape[0]
    groups = k_proj.shape[1] // head // n_ctx
    pair = q_proj.shape[1] // n_ctx // groups
    unit = pair + 2 * head
    length = n_ctx * toks
    wide = max(-(-(index * part % head + part) // head) for index in range(n_dp)) * head
    frequency = np.exp(np.arange(head // 2) * (-2.0 * math.log(rope_base) / head))
    frequency = jnp.asarray(np.tile(frequency, 2)[None, :], jnp.float32)
    dma = pltpu.SemaphoreType.DMA
    vmem = pl.BlockSpec(memory_space=pltpu.VMEM)
    smem = pl.BlockSpec(memory_space=pltpu.SMEM)
    anywhere = pl.BlockSpec(memory_space=pl.ANY)
    low, full = jnp.bfloat16, jnp.float32
    return pl.pallas_call(
        lambda *refs: layer_kernel(n_dp, n_ctx, part, *refs),
        out_shape=(
            jax.ShapeDtypeStruct((n_dp, toks, wide), low),
            jax.ShapeDtypeStruct((part, groups * unit), low),
            jax.ShapeDtypeStruct((8, head), full),
        ),
        in_specs=[anywhere] * 5 + [vmem, smem, vmem, vmem, vmem, anywhere],
        out_specs=(anywhere, anywhere, vmem),
        scratch_shapes=[
            pltpu.VMEM((groups, length, pair), low),
            pltpu.VMEM((groups, length, head), low),
            pltpu.VMEM((groups, length, head), low),
            pltpu.VMEM((groups, length, pair), low),
            pltpu.VMEM((8, head), full),
            pltpu.VMEM((n_ctx, 8, head), full),
            pltpu.VMEM((length, head), full),
            pltpu.VMEM((length, head), full),
            pltpu.VMEM((length, head), jnp.int32),
            pltpu.VMEM((n_ctx, 2 * toks, head), low),
            pltpu.VMEM((n_ctx, 2 * toks, head), low),
            pltpu.VMEM((length, head), low),
            pltpu.VMEM((length, head), full),
            pltpu.VMEM((length, head), full),
            pltpu.VMEM((n_dp, groups, length, unit), low),
            pltpu.VMEM((groups, wide, unit), low),
            pltpu.VMEM((n_dp, length, wide), low),
            pltpu.VMEM((wide, groups * unit), full),
            pltpu.VMEM((length, wide), full),
            pltpu.VMEM((n_dp, toks, wide), full),
            pltpu.VMEM((n_dp, toks, wide), full),
            pltpu.VMEM((n_dp, 2, toks, wide), low),
            pltpu.VMEM((n_dp, 2, toks, wide), low),
            pltpu.VMEM((n_dp, toks, wide), low),
            pltpu.VMEM((n_dp, toks, wide), low),
            pltpu.VMEM((n_dp, toks, wide), low),
            pltpu.VMEM((2, 8, head), full),
            pltpu.VMEM((8, head), full),
            pltpu.VMEM((n_dp, 8, head), full),
            pltpu.VMEM((8, head), full),
            pltpu.VMEM((n_ctx, 8, head), full),
            pltpu.VMEM((wide, groups * unit), low),
            dma((groups, 4)),
            dma((groups, 3)),
            dma,
            dma((n_ctx,)),
            dma((n_ctx,)),
            dma((n_ctx, groups, 4)),
            dma((n_ctx, groups, 4)),
            dma((n_dp,)),
            dma((n_dp,)),
            dma((n_dp,)),
            dma((n_dp,)),
            dma((n_dp,)),
            dma((n_dp,)),
            dma((n_dp,)),
            dma((n_dp,)),
            dma((4, n_dp, groups)),
            dma((n_dp, groups)),
            dma((n_dp,)),
            dma((n_dp,)),
            dma((n_dp,)),
            dma((n_dp,)),
            dma((n_dp,)),
            dma((n_dp,)),
            dma((n_dp,)),
            dma((n_dp,)),
            dma((n_ctx,)),
            dma((n_ctx,)),
            dma((groups, unit // head)),
            dma((n_ctx, groups)),
            dma((groups,)),
            dma,
            dma,
        ],
        compiler_params=pltpu.CompilerParams(
            collective_id=3, has_side_effects=True, vmem_limit_bytes=58 * 1024 * 1024
        ),
        name="layer",
    )(
        inputs, q_proj, k_proj, v_proj, d_attn, positions, windows,
        q_gain[None, :], k_gain[None, :], frequency, weight,
    )


def finish_kernel(part, ret_ref, dw_ref, gain_ref, din_ref, out_ref, q_out, k_out):
    count, _, wide = ret_ref.shape
    head = gain_ref.shape[1]
    starts = [index * part // head for index in range(count)]
    pieces = wide // head
    for index in range(count):
        first = 1 if index > 0 and starts[index] < starts[index - 1] + pieces else 0
        last = pieces - 1 if index + 1 < count and starts[index + 1] < starts[index] + pieces else pieces
        base = starts[index] * head
        din_ref[:, base + first * head:base + last * head] = ret_ref[index, :, first * head:last * head]
        if last < pieces:
            both = ret_ref[index, :, last * head:].astype(jnp.float32) + ret_ref[index + 1, :, :head].astype(jnp.float32)
            din_ref[:, base + last * head:base + pieces * head] = both.astype(din_ref.dtype)
    out_ref[...] = dw_ref[...].astype(out_ref.dtype)
    q_out[...] = gain_ref[0:1, :]
    k_out[...] = gain_ref[1:2, :]


def finished(returned, weight_rows, gains, model):
    n_dp, toks, wide = returned.shape
    part, rows = weight_rows.shape
    head = gains.shape[1]
    steps = 2
    return pl.pallas_call(
        lambda *refs: finish_kernel(part, *refs),
        grid=(steps,),
        out_shape=(
            jax.ShapeDtypeStruct((toks, model), jnp.bfloat16),
            jax.ShapeDtypeStruct((part, rows), jnp.float32),
            jax.ShapeDtypeStruct((1, head), jnp.float32),
            jax.ShapeDtypeStruct((1, head), jnp.float32),
        ),
        in_specs=[
            pl.BlockSpec((n_dp, toks // steps, wide), lambda i: (0, i, 0)),
            pl.BlockSpec((part // steps, rows), lambda i: (i, 0)),
            pl.BlockSpec((8, head), lambda i: (0, 0)),
        ],
        out_specs=(
            pl.BlockSpec((toks // steps, model), lambda i: (i, 0)),
            pl.BlockSpec((part // steps, rows), lambda i: (i, 0)),
            pl.BlockSpec((1, head), lambda i: (0, 0)),
            pl.BlockSpec((1, head), lambda i: (0, 0)),
        ),
        compiler_params=pltpu.CompilerParams(vmem_limit_bytes=58 * 1024 * 1024),
        name="finish",
    )(returned, weight_rows, gains)


def head_shards(inputs, q_proj, k_proj, v_proj, d_attn, positions, windows, q_gain, k_gain, weight):
    returned, weight_rows, gains = layer(
        inputs[0], q_proj[0], k_proj[0], v_proj[0], d_attn[0], positions, windows, q_gain, k_gain, weight
    )
    d_inputs, d_weight, dq_gain, dk_gain = finished(returned, weight_rows, gains, inputs.shape[2])
    return (d_inputs[None], d_weight.T, dq_gain[0], dk_gain[0])


def by_heads(mesh):
    return mesh.shape["dp"] == 8 and mesh.shape["ctx"] == 4


def solution(mesh):
    placed = (
        P("dp", "ctx", None),
        P("dp", "ctx", None),
        P("dp", "ctx", None),
        P("dp", "ctx", None),
        P("dp", "ctx", None),
        P("dp", "ctx"),
        P("dp"),
        P(),
        P(),
        P("dp", None),
    )
    return jax.shard_map(
        head_shards if by_heads(mesh) else shards,
        mesh=mesh,
        in_specs=placed,
        out_specs=(P("dp", "ctx", None), P("ctx", "dp"), P(), P()),
        check_vma=False,
    )
```
